32 devices in a mesh: seq: 16 (over z, y, core), blk: 2 (over x).
Axes of the slice: x: 2, y: 2, z: 4, core: 2. Of those that a mesh axis runs over, the one named last changes fastest.
Arguments:
- tokens: bfloat16 [32, 1024, 512], P('seq', 'blk'), may hold values from -6 to 6
- memory: bfloat16 [32, 512, 512], P('seq', 'blk'), may hold values from -6 to 6
- segment_ends: int32 [32, 1024], P('seq', 'blk'), may hold values from 1 to 8192, as said below
- memory_ends: int32 [32, 512], P('seq', 'blk'), may hold values from -4088 to 0, as said below
- segment_counts: int32 [32], P('seq'), may hold values from 512 to 1024, as said below
- memory_lengths: int32 [32], P('seq'), may hold values from 128 to 512, as said below
- first_gain: float32 [512], replicated, may hold values from 0.5 to 1.5
- first_shift: float32 [512], replicated, may hold values from -1.2 to 1.2
- query_weight: bfloat16 [512, 512], replicated, may hold values from -0.25 to 0.25
- key_weight: bfloat16 [512, 512], replicated, may hold values from -0.25 to 0.25
- value_weight: bfloat16 [512, 512], replicated, may hold values from -0.25 to 0.25
- out_weight: bfloat16 [512, 512], replicated, may hold values from -2 to 2
- head_slopes: float32 [8], replicated, may hold values from 1e-05 to 0.03
- second_gain: float32 [512], replicated, may hold values from 0.5 to 1.5
- second_shift: float32 [512], replicated, may hold values from -1.2 to 1.2
- hidden_weight: bfloat16 [512, 2048], replicated, may hold values from -0.25 to 0.25
- output_weight: bfloat16 [2048, 512], replicated, may hold values from -0.125 to 0.125
- output_grad: bfloat16 [32, 1024, 512], P('seq', 'blk'), may hold values from -6 to 6
Outputs:
- layer_out: bfloat16 [32, 1024, 512], P('seq', 'blk')
- input_grad: bfloat16 [32, 1024, 512], P('seq', 'blk')
- grad_first_gain: float32 [512], replicated
- grad_first_shift: float32 [512], replicated
- grad_query_weight: float32 [512, 512], replicated
- grad_key_weight: float32 [512, 512], replicated
- grad_value_weight: float32 [512, 512], replicated
- grad_out_weight: float32 [512, 512], replicated
- grad_head_slopes: float32 [8], replicated
- grad_second_gain: float32 [512], replicated
- grad_second_shift: float32 [512], replicated
- grad_hidden_weight: float32 [512, 2048], replicated
- grad_output_weight: float32 [2048, 512], replicated
The draws below stay inside these ranges and needn't reach their ends.
Inputs may be any that keep to these rules, and one draw needn't show every extreme that they name: `segment_ends`: each row rises strictly by 1 to 8 bytes from slot to slot; the first slot ends 1 to 8 bytes after the row's last memory end. In some sequence every step is 8 bytes; in another the first slot ends 1 byte after its memory. `memory_ends`: each row rises strictly by 1 to 8 bytes from entry to entry and its last entry is 0; in some sequence every step is 8 bytes. `segment_counts`: slots 0 to count - 1 of a sequence hold segments, the others are empty; some sequence uses all 1024 slots and some exactly half of them. `memory_lengths`: the last length memory rows of a sequence are valid; some sequence has all 512 and some a quarter.
All inputs are finite; a program needn't handle non-finite values.
Results may differ from the reference program's by a relative error of at most 0.022.
Values may be sent and summed in bfloat16 or wider, within the bound.
A program may use at most 256 MiB of HBM per device.

```python
import math
import jax
import jax.numpy as jnp
from jax import lax

D = 512
H = 8
FF = 2048
SLOT_DEV = 512
MEM = 512
SLOTS = 1024
SEQS = 32


def ends_pair(key):
    inner = jax.random.fold_in(key, 7)
    widths = jax.random.randint(inner, (SEQS, MEM + SLOTS), 1, 9).astype(jnp.int32)
    full_row = jax.random.randint(jax.random.fold_in(key, 21), (), 0, SEQS)
    short_row = (full_row + 1 + jax.random.randint(jax.random.fold_in(key, 22), (), 0, SEQS - 1)) % SEQS
    rows = jnp.arange(SEQS, dtype=jnp.int32)[:, None]
    columns = jnp.arange(MEM + SLOTS, dtype=jnp.int32)[None, :]
    widths = jnp.where(rows == full_row, 8, widths)
    widths = jnp.where((rows == short_row) & (columns == MEM), 1, widths).astype(jnp.int32)
    running = jnp.cumsum(widths, axis=1)
    running = running - running[:, MEM - 1:MEM]
    return (running[:, MEM:].astype(jnp.int32), running[:, :MEM].astype(jnp.int32))


def reach_both(key, lowest, highest_value):
    values = jax.random.randint(jax.random.fold_in(key, 1), (SEQS,), lowest, highest_value + 1).astype(jnp.int32)
    top_at = jax.random.randint(jax.random.fold_in(key, 2), (), 0, SEQS)
    bottom_at = (top_at + 1 + jax.random.randint(jax.random.fold_in(key, 3), (), 0, SEQS - 1)) % SEQS
    places = jnp.arange(SEQS, dtype=jnp.int32)
    values = jnp.where(places == top_at, highest_value, values)
    values = jnp.where(places == bottom_at, lowest, values)
    return values.astype(jnp.int32)


def draw_segment_ends(key, part):
    return ends_pair(key)[0]


def draw_memory_ends(key, part):
    return ends_pair(key)[1]


def draw_segment_counts(key, part):
    return reach_both(jax.random.fold_in(key, 11), SLOTS // 2, SLOTS)


def draw_memory_lengths(key, part):
    return reach_both(jax.random.fold_in(key, 13), MEM // 4, MEM)


def steps_of(rng, shape, cuts, least, largest):
    def one(dim, blocks):
        draws = jax.random.uniform(jax.random.fold_in(jax.random.fold_in(rng, 6), dim), (blocks,), jnp.float32, least / len(cuts), largest / len(cuts))
        return jnp.repeat(jnp.exp(draws), shape[dim] // blocks).reshape((-1,) + (1,) * (len(shape) - dim - 1))

    level = one(*cuts[0])
    for cut in cuts[1:]:
        level = level * one(*cut)
    return level


def noise(own_key, extent, deviation, limit, shards=(), kind=jnp.bfloat16):
    drawn = jax.random.normal(own_key, extent, jnp.float32) * deviation
    if len(shards) > 0:
        drawn = steps_of(own_key, extent, shards, -0.22, 0.18) * drawn
    return jnp.clip(drawn, min=-limit, max=limit).astype(kind)


def setup_inputs(seed: int = 0) -> dict:
    key_of = jax.random.split(jax.random.key(seed), 19)
    return {
        "tokens": noise(key_of[0], (SEQS, SLOTS, D), 1.0, 6.0, ((0, 16), (1, 2))),
        "memory": noise(key_of[1], (SEQS, MEM, D), 1.0, 6.0, ((0, 16), (1, 2))),
        "segment_ends": draw_segment_ends(jax.random.fold_in(key_of[18], 71), 0),
        "memory_ends": draw_memory_ends(jax.random.fold_in(key_of[18], 71), 0),
        "segment_counts": draw_segment_counts(jax.random.fold_in(key_of[18], 71), 0),
        "memory_lengths": draw_memory_lengths(jax.random.fold_in(key_of[18], 71), 0),
        "first_gain": jnp.clip(1.0 + 0.1 * jax.random.normal(key_of[6], (D,), jnp.float32), 0.5, 1.5),
        "first_shift": noise(key_of[7], (D,), 0.2, 1.2, (), jnp.float32),
        "query_weight": noise(key_of[8], (D, D), D ** -0.5, 0.25),
        "key_weight": noise(key_of[9], (D, D), D ** -0.5, 0.25),
        "value_weight": noise(key_of[10], (D, D), D ** -0.5, 0.25),
        "out_weight": noise(key_of[11], (D, D), (D // 64) ** -0.5, 2.0),
        "head_slopes": jnp.clip(jnp.exp(jax.random.uniform(key_of[12], (H,), jnp.float32, math.log(9.999999747378752e-06), math.log(0.03))), 9.999999747378752e-06, 0.03),
        "second_gain": jnp.clip(1.0 + 0.1 * jax.random.normal(key_of[13], (D,), jnp.float32), 0.5, 1.5),
        "second_shift": noise(key_of[14], (D,), 0.2, 1.2, (), jnp.float32),
        "hidden_weight": noise(key_of[15], (D, FF), D ** -0.5, 0.25),
        "output_weight": noise(key_of[16], (FF, D), FF ** -0.5, 0.125),
        "output_grad": noise(key_of[17], (SEQS, SLOTS, D), 1.0, 6.0, ((0, 16), (1, 2))),
    }


epsilon = 1e-05
far_order = 1073741824
highest = lax.Precision.HIGHEST

@jax.custom_vjp
def low(v):
    return lax.optimization_barrier(v.astype(jnp.bfloat16)).astype(jnp.float32)

@jax.custom_vjp
def low_back(v):
    return v

def low_keep(v):
    return (low(v), None)

def low_pass(kept, grad):
    return (grad,)

def back_keep(v):
    return (v, None)

def back_low(kept, grad):
    return (low(grad),)
low.defvjp(low_keep, low_pass)
low_back.defvjp(back_keep, back_low)

def layer_norm(values, gain, shift):
    centred = values - lax.optimization_barrier(jnp.mean(values, axis=-1, keepdims=True))
    spread = lax.optimization_barrier(jnp.mean(centred * centred, axis=-1, keepdims=True))
    return centred * lax.rsqrt(spread + epsilon) * gain + shift

def matmul(left, right):
    return jnp.dot(left, right, precision=highest, preferred_element_type=jnp.float32)

def one_sequence(params, pieces):
    x_rows, mem_rows, slot_ends, mem_ends, used_slots, mem_valid = pieces
    first_gain, first_shift, query_weight, key_weight, value_weight, out_weight, head_slopes, second_gain, second_shift, hidden_weight, output_weight = params
    slot_total = x_rows.shape[0]
    mem_total = mem_rows.shape[0]
    model_width = x_rows.shape[1]
    head_count = head_slopes.shape[0]
    head_dim = model_width // head_count
    score_scale = 1.0 / math.sqrt(head_dim)
    normed = low(layer_norm(x_rows, first_gain, first_shift))
    mem_normed = low(layer_norm(mem_rows, first_gain, first_shift))
    key_input = jnp.concatenate([mem_normed, normed], axis=0)
    query = low(low_back(matmul(normed, query_weight))).reshape(slot_total, head_count, head_dim)
    key_heads = low(low_back(matmul(key_input, key_weight))).reshape(mem_total + slot_total, head_count, head_dim)
    value_heads = low(low_back(matmul(key_input, value_weight))).reshape(mem_total + slot_total, head_count, head_dim)
    mem_index = jnp.arange(mem_total, dtype=jnp.int32)
    slot_index = jnp.arange(slot_total, dtype=jnp.int32)
    mem_order = jnp.where(mem_index >= mem_total - mem_valid, -1, far_order).astype(jnp.int32)
    slot_order = jnp.where(slot_index < used_slots, slot_index, far_order).astype(jnp.int32)
    key_order = jnp.concatenate([mem_order, slot_order])
    key_ends = jnp.concatenate([mem_ends.astype(jnp.int32), slot_ends.astype(jnp.int32)])
    block_count = slot_total // SLOT_DEV

    def attend(block):
        q_block, q_index, q_ends = block
        scores = jnp.einsum('qhd,khd->hqk', q_block, key_heads, precision=highest) * score_scale
        distance = (q_ends[:, None] - key_ends[None, :]).astype(jnp.float32)
        scores = low_back(scores - head_slopes[:, None, None] * distance[None])
        allowed = key_order[None, :] <= q_index[:, None]
        scores = jnp.where(allowed[None], scores, -1e+30)
        attn_probs = low(jax.nn.softmax(scores, axis=-1))
        return jnp.einsum('hqk,khd->qhd', attn_probs, value_heads, precision=highest)
    blocks = (query.reshape(block_count, SLOT_DEV, head_count, head_dim), slot_index.reshape(block_count, SLOT_DEV), slot_ends.astype(jnp.int32).reshape(block_count, SLOT_DEV))
    mixed = lax.map(jax.checkpoint(attend), blocks).reshape(slot_total, model_width)
    mixed = low(low_back(mixed))
    residual = x_rows + low_back(matmul(mixed, out_weight))
    second = low(layer_norm(residual, second_gain, second_shift))
    hidden_pre = low_back(matmul(second, hidden_weight))
    activation = low(jax.nn.gelu(hidden_pre, approximate=False))
    return residual + matmul(activation, output_weight)

def reference(tokens, memory, segment_ends, memory_ends, segment_counts, memory_lengths, first_gain, first_shift, query_weight, key_weight, value_weight, out_weight, head_slopes, second_gain, second_shift, hidden_weight, output_weight, output_grad):
    params = (first_gain.astype(jnp.float32), first_shift.astype(jnp.float32), query_weight.astype(jnp.float32), key_weight.astype(jnp.float32), value_weight.astype(jnp.float32), out_weight.astype(jnp.float32), head_slopes.astype(jnp.float32), second_gain.astype(jnp.float32), second_shift.astype(jnp.float32), hidden_weight.astype(jnp.float32), output_weight.astype(jnp.float32))
    mem_float = memory.astype(jnp.float32)

    def forward(inputs, weights):
        return lax.map(lambda pieces: one_sequence(weights, pieces), (inputs, mem_float, segment_ends, memory_ends, segment_counts, memory_lengths))
    layer, pullback = jax.vjp(forward, tokens.astype(jnp.float32), params)
    in_grad, weight_grads = pullback(output_grad.astype(jnp.float32))
    return (layer.astype(jnp.bfloat16), in_grad.astype(jnp.bfloat16), weight_grads[0], weight_grads[1], weight_grads[2], weight_grads[3], weight_grads[4], weight_grads[5], weight_grads[6], weight_grads[7], weight_grads[8], weight_grads[9], weight_grads[10])
```

```python
import functools
import math

import jax
import jax.numpy as jnp
from jax import lax
from jax.experimental import pallas as pl
from jax.experimental.pallas import tpu as pltpu
from jax.sharding import PartitionSpec as P

epsilon = 1e-05
far_order = 1073741824
f32 = jnp.float32
bf16 = jnp.bfloat16
BLOCK = 256
LOG2E = 1.4426950408889634
LN2 = 0.6931471805599453


def dot_nn(left, right):
    return lax.dot_general(left, right, (((1,), (0,)), ((), ())), preferred_element_type=f32)


def dot_nt(left, right):
    return lax.dot_general(left, right, (((1,), (1,)), ((), ())), preferred_element_type=f32)


def norm_stats(values):
    centred = values - jnp.mean(values, axis=-1, keepdims=True)
    spread = jnp.mean(centred * centred, axis=-1, keepdims=True)
    scale = lax.rsqrt(spread + epsilon)
    return centred * scale, scale


def norm_back(unit, scale, grad_unit):
    mean_grad = jnp.mean(grad_unit, axis=-1, keepdims=True)
    mean_prod = jnp.mean(grad_unit * unit, axis=-1, keepdims=True)
    return (grad_unit - mean_grad - unit * mean_prod) * scale


def pieces_of(value, count):
    out = []
    for _ in range(count):
        part = value.astype(bf16).astype(f32)
        out.append(part)
        value = value - part
    return out


ERFC_P = 0.4
ERFC_C = (0.22567586600780487, 0.2256695181131363, 0.2078438550233841, 0.16853390634059906, 0.1414608359336853, -0.005667657125741243, 0.16915477812290192, -0.18294358253479004, 0.050272583961486816)


def gelu_both(x):
    a = jnp.abs(x) * math.sqrt(0.5)
    t = 1.0 / (1.0 + ERFC_P * a)
    poly = jnp.full_like(t, ERFC_C[-1])
    for c in ERFC_C[-2::-1]:
        poly = poly * t + c
    ex = jnp.exp(-0.5 * (x * x))
    half = 0.5 * (poly * t * ex)
    cdf = jnp.where(x >= 0, 1.0 - half, half)
    return x * cdf, cdf + x * ex * (1.0 / math.sqrt(2.0 * math.pi))


def col_sum8(value):
    return jnp.sum(value.reshape(-1, 8, value.shape[-1]), axis=0)


def layer_kernel(
    counts_ref,
    lengths_ref,
    which_ref,
    x_ref,
    mem_ref,
    ends_ref,
    og_ref,
    gain1_ref,
    shift1_ref,
    wq_ref,
    wk_ref,
    wv_ref,
    wo_ref,
    slopes_ref,
    gain2_ref,
    shift2_ref,
    w1_ref,
    w2_ref,
    layer_ref,
    ingrad_ref,
    gq_ref,
    gk_ref,
    gv_ref,
    go_ref,
    gw1_ref,
    gw2t_ref,
    small_ref,
    keyint,
    k_s,
    v_s,
    kx,
    q_s,
    qt,
    rl_s,
    o_s,
    mixed,
    gw1_s,
    gw2t_s,
    go_s,
    dres,
    dolt,
    delta_s,
    *probs,
):
    S, D = x_ref.shape
    M = mem_ref.shape[0]
    R = M + S
    FF = w1_ref.shape[1]
    H = slopes_ref.shape[0]
    DH = D // H
    HP = H // 2
    NB = S // BLOCK
    MB = M // BLOCK
    which = which_ref[0]
    count = counts_ref[which]
    length = lengths_ref[which]
    gain1 = gain1_ref[...]
    shift1 = shift1_ref[...]
    gain2 = gain2_ref[...]
    shift2 = shift2_ref[...]

    lane = lax.broadcasted_iota(jnp.int32, (128, 128), 1)
    row = lax.broadcasted_iota(jnp.int32, (128, 128), 0)
    for r in range(R // 128):
        ends = ends_ref[:, r * 128 : (r + 1) * 128].astype(f32)
        end_col = jnp.broadcast_to(ends, (128, 128)).T
        high = jnp.floor(end_col * (1.0 / 256.0)) * 256.0
        index = row + r * 128
        if r * 128 < M:
            valid = index >= M - length
        else:
            valid = index - M < count
        bias = jnp.where(valid, 0.0, -1e30)
        extra = jnp.where(lane < 3, high, jnp.where(lane < 6, end_col - high, bias))
        extra = jnp.where(lane == 7, 1.0, jnp.where(lane > 7, 0.0, extra))
        kx[r * 128 : (r + 1) * 128, :] = extra.astype(bf16)

    def project(normed, key_rows):
        keyint[:, key_rows] = normed.T
        k_s[key_rows, :] = dot_nn(normed, wk_ref[...]).astype(bf16)
        v_s[key_rows, :] = dot_nn(normed, wv_ref[...]).astype(bf16)

    def norm_mem(b, _):
        rows = pl.ds(pl.multiple_of(b * BLOCK, BLOCK), BLOCK)
        unit, _ = norm_stats(mem_ref[rows, :].astype(f32))
        project((unit * gain1 + shift1).astype(bf16), rows)
        return 0

    def norm_slot(b, _):
        rows = pl.ds(pl.multiple_of(b * BLOCK, BLOCK), BLOCK)
        key_rows = pl.ds(pl.multiple_of(b * BLOCK + M, BLOCK), BLOCK)
        unit, _ = norm_stats(x_ref[rows, :].astype(f32))
        normed = (unit * gain1 + shift1).astype(bf16)
        project(normed, key_rows)
        query = (dot_nn(normed, wq_ref[...]) * (LOG2E / math.sqrt(DH))).astype(bf16)
        q_s[rows, :] = query
        qt[:, rows] = query.T
        return 0

    lax.fori_loop(0, MB, norm_mem, 0)
    lax.fori_loop(0, NB, norm_slot, 0)

    lane_q = lax.broadcasted_iota(jnp.int32, (BLOCK, 128), 1)
    first_half = lane_q < DH
    lane_row = lax.broadcasted_iota(jnp.int32, (1, 128), 1)

    def key_full(lanes, keys):
        return jnp.concatenate([k_s[0:keys, lanes], kx[0:keys, :]], axis=1)

    def value_full(lanes, keys):
        return jnp.concatenate([v_s[0:keys, lanes], jnp.ones((keys, 128), bf16)], axis=1)

    def query_extra(head):
        slope = jnp.full((1, 128), slopes_ref[head] * LOG2E, f32)
        s1, s2, s3 = pieces_of(slope, 3)
        at = jnp.where(lane_row >= 3, lane_row - 3, lane_row)
        out = jnp.where(at == 0, s1, jnp.where(at == 1, s2, s3))
        out = jnp.where(lane_row < 6, out, jnp.where(lane_row == 6, 1.0, 0.0))
        return out

    rl_s[...] = jnp.zeros_like(rl_s)
    for b in range(NB):
        keys = M + (b + 1) * BLOCK
        rows = slice(b * BLOCK, (b + 1) * BLOCK)
        e_ref = probs[b]

        def fwd_pair(p, _):
            lanes = pl.ds(pl.multiple_of(p * 128, 128), 128)
            q_pair = q_s[rows, lanes]
            outs = []
            for half in range(2):
                keep = first_half if half == 0 else jnp.logical_not(first_half)
                q_half = jnp.where(keep, q_pair, jnp.zeros_like(q_pair))
                extra = jnp.broadcast_to(query_extra(2 * p + half), (BLOCK, 128)).astype(bf16)
                q_full = jnp.concatenate([q_half, extra], axis=1)
                scores = dot_nt(q_full, key_full(lanes, keys))
                diag = scores[:, keys - BLOCK :]
                below = lax.broadcasted_iota(
                    jnp.int32, (BLOCK, BLOCK), 1
                ) <= lax.broadcasted_iota(jnp.int32, (BLOCK, BLOCK), 0)
                diag = jnp.where(below, diag, -1e30)
                scores = jnp.concatenate([scores[:, : keys - BLOCK], diag], axis=1)
                top = jnp.max(scores, axis=1, keepdims=True)
                e = jnp.exp2(scores - top).astype(bf16)
                e_ref[2 * p + half, :, :] = e
                both = dot_nn(e, value_full(lanes, keys))
                outs.append((both[:, 0:128], 1.0 / both[:, 128:256]))
            rl = jnp.where(first_half, outs[0][1], outs[1][1])
            o = jnp.where(first_half, outs[0][0], outs[1][0]) * rl
            packed = jnp.where(lane_q == 2 * p, outs[0][1], rl_s[rows, :])
            rl_s[rows, :] = jnp.where(lane_q == 2 * p + 1, outs[1][1], packed)
            o_s[rows, lanes] = o
            mixed[rows, lanes] = o.astype(bf16)
            return 0

        lax.fori_loop(0, HP, fwd_pair, 0)

    gw1_s[...] = jnp.zeros_like(gw1_s)
    gw2t_s[...] = jnp.zeros_like(gw2t_s)
    go_s[...] = jnp.zeros_like(go_s)
    CH = 512

    def feed(b, sums):
        rows = pl.ds(pl.multiple_of(b * BLOCK, BLOCK), BLOCK)
        mix = mixed[rows, :]
        residual = x_ref[rows, :].astype(f32) + dot_nn(mix, wo_ref[...])
        unit, scale = norm_stats(residual)
        second = (unit * gain2 + shift2).astype(bf16)
        second_t = second.T
        og = og_ref[rows, :]
        og_t = og.T
        out = residual
        d_second = jnp.zeros((BLOCK, D), f32)
        for c in range(FF // CH):
            cols = slice(c * CH, (c + 1) * CH)
            hidden = dot_nn(second, w1_ref[:, cols])
            d_act = dot_nt(og, w2_ref[cols, :])
            act, slope = gelu_both(hidden)
            act = act.astype(bf16)
            d_pre = (d_act * slope).astype(bf16)
            out = out + dot_nn(act, w2_ref[cols, :])
            d_second = d_second + dot_nt(d_pre, w1_ref[:, cols])
            gw2t_s[:, cols] += dot_nn(og_t, act)
            gw1_s[:, cols] += dot_nn(second_t, d_pre)
        layer_ref[rows, :] = out.astype(bf16)
        d_residual = og.astype(f32) + norm_back(unit, scale, d_second * gain2)
        dres[rows, :] = d_residual
        d_branch = d_residual.astype(bf16)
        go_s[...] += dot_nn(mix.T, d_branch)
        d_mixed = dot_nt(d_branch, wo_ref[...]).astype(bf16).astype(f32)
        rl_b = rl_s[rows, :]
        rl_wide = []
        for p in range(HP):
            first = jnp.broadcast_to(rl_b[:, 2 * p : 2 * p + 1], (BLOCK, 128))
            other = jnp.broadcast_to(rl_b[:, 2 * p + 1 : 2 * p + 2], (BLOCK, 128))
            rl_wide.append(jnp.where(first_half, first, other))
        dol_b = (d_mixed * jnp.concatenate(rl_wide, axis=1)).astype(bf16)
        mixed[rows, :] = dol_b
        dolt[:, rows] = dol_b.T
        prod = dol_b.astype(f32) * o_s[rows, :]
        packed = jnp.zeros((BLOCK, 128), f32)
        for head in range(H):
            part = prod[:, (head // 2) * 128 : (head // 2 + 1) * 128]
            keep = first_half if head % 2 == 0 else jnp.logical_not(first_half)
            delta = jnp.sum(jnp.where(keep, part, 0.0), axis=1, keepdims=True)
            for at, piece in enumerate(pieces_of(jnp.broadcast_to(-delta, (BLOCK, 128)), 3)):
                packed = jnp.where(lane_q == 4 * head + at, piece, packed)
        delta_s[rows, :] = packed.astype(bf16)
        return sums[0] + col_sum8(d_second * unit), sums[1] + col_sum8(d_second)

    zero8 = jnp.zeros((8, D), f32)
    gain2_sum, shift2_sum = lax.fori_loop(0, NB, feed, (zero8, zero8))
    gw1_ref[...] = gw1_s[...].astype(bf16)
    gw2t_ref[...] = gw2t_s[...].astype(bf16)
    go_ref[...] = go_s[...].astype(bf16)

    dkt, dvt = gw1_s.at[:, 0:R], gw2t_s.at[:, 0:R]
    dkt[...] = jnp.zeros((D, R), f32)
    dvt[...] = jnp.zeros((D, R), f32)
    small_ref[...] = jnp.zeros_like(small_ref)
    for b in range(NB):
        keys = M + (b + 1) * BLOCK
        rows = slice(b * BLOCK, (b + 1) * BLOCK)
        e_ref = probs[b]
        end_row = ends_ref[:, M + b * BLOCK : M + (b + 1) * BLOCK].astype(f32)
        end_b = jnp.broadcast_to(end_row, (128, BLOCK)).T
        weight = jnp.where(
            (lane_q == 0) | (lane_q == 3), 1.0, jnp.where(lane_q == 7, -end_b, 0.0)
        )

        def bwd_pair(p, _):
            lanes = pl.ds(pl.multiple_of(p * 128, 128), 128)
            dol_pair = mixed[rows, lanes]
            outs = []
            for half in range(2):
                head = 2 * p + half
                keep = first_half if half == 0 else jnp.logical_not(first_half)
                d_half = jnp.where(keep, dol_pair, jnp.zeros_like(dol_pair))
                delta = delta_s[rows, :]
                delta = jnp.where(lane_q // 4 == head, delta, jnp.zeros_like(delta))
                d_full = jnp.concatenate([d_half, delta], axis=1)
                e = e_ref[head, :, :]
                ds = (dot_nt(d_full, value_full(lanes, keys)) * e.astype(f32)).astype(bf16)
                dqx = dot_nn(ds, key_full(lanes, keys))
                outs.append(dqx[:, 0:128])
                hrows = pl.ds(pl.multiple_of(head * DH, DH), DH)
                dkt[hrows, 0:keys] += dot_nn(qt[hrows, rows], ds)
                dvt[hrows, 0:keys] += dot_nn(dolt[hrows, rows], e)
                tail = jnp.sum(dqx[:, 128:256] * weight, axis=0, keepdims=True)
                at = lax.broadcasted_iota(jnp.int32, (8, 128), 0) == head
                small_ref[8:16, 0:128] += jnp.where(at, tail, 0.0)
            dq = jnp.where(first_half, outs[0], outs[1]) * (1.0 / math.sqrt(DH))
            q_s[rows, lanes] = dq.astype(bf16)
            return 0

        lax.fori_loop(0, HP, bwd_pair, 0)

    gq_ref[...] = dot_nn(keyint[:, M:], q_s[...]).astype(bf16)

    def rows_back(b, grads):
        rows = pl.ds(pl.multiple_of(b * BLOCK, BLOCK), BLOCK)
        dk = (dkt[:, rows] * LN2).astype(bf16).T
        dv = dvt[:, rows].astype(bf16).T
        k_s[rows, :] = dk
        v_s[rows, :] = dv
        return grads

    lax.fori_loop(0, MB + NB, rows_back, 0)
    gk_ref[...] = dot_nn(keyint[...], k_s[...]).astype(bf16)
    gv_ref[...] = dot_nn(keyint[...], v_s[...]).astype(bf16)

    def mem_back(b, sums):
        rows = pl.ds(pl.multiple_of(b * BLOCK, BLOCK), BLOCK)
        unit, _ = norm_stats(mem_ref[rows, :].astype(f32))
        d_rows = dot_nt(k_s[rows, :], wk_ref[...]) + dot_nt(v_s[rows, :], wv_ref[...])
        return sums[0] + col_sum8(d_rows * unit), sums[1] + col_sum8(d_rows)

    def slot_back(b, sums):
        rows = pl.ds(pl.multiple_of(b * BLOCK, BLOCK), BLOCK)
        key_rows = pl.ds(pl.multiple_of(b * BLOCK + M, BLOCK), BLOCK)
        unit, scale = norm_stats(x_ref[rows, :].astype(f32))
        d_rows = dot_nt(k_s[key_rows, :], wk_ref[...]) + dot_nt(v_s[key_rows, :], wv_ref[...])
        d_rows = d_rows + dot_nt(q_s[rows, :], wq_ref[...])
        grad = norm_back(unit, scale, d_rows * gain1) + dres[rows, :]
        ingrad_ref[rows, :] = grad.astype(bf16)
        return sums[0] + col_sum8(d_rows * unit), sums[1] + col_sum8(d_rows)

    sums = lax.fori_loop(0, MB, mem_back, (zero8, zero8))
    gain1_sum, shift1_sum = lax.fori_loop(0, NB, slot_back, sums)
    small_ref[0:1, :] = jnp.sum(gain1_sum, axis=0, keepdims=True)
    small_ref[1:2, :] = jnp.sum(shift1_sum, axis=0, keepdims=True)
    small_ref[2:3, :] = jnp.sum(gain2_sum, axis=0, keepdims=True)
    small_ref[3:4, :] = jnp.sum(shift2_sum, axis=0, keepdims=True)


def layer_call(counts, lengths, which, x, mem, ends, og, params):
    S, D = x.shape
    M = mem.shape[0]
    R = M + S
    gain1, shift1, wq, wk, wv, wo, slopes, gain2, shift2, w1, w2 = params
    FF = w1.shape[1]
    H = slopes.shape[0]
    vmem = pl.BlockSpec(memory_space=pltpu.VMEM)
    smem = pl.BlockSpec(memory_space=pltpu.SMEM)
    V = pltpu.VMEM
    scratch = [
        V((D, R), bf16),
        V((R, D), bf16),
        V((R, D), bf16),
        V((R, 128), bf16),
        V((S, D), bf16),
        V((D, S), bf16),
        V((S, 128), f32),
        V((S, D), f32),
        V((S, D), bf16),
        V((D, FF), f32),
        V((D, FF), f32),
        V((D, D), f32),
        V((S, D), f32),
        V((D, S), bf16),
        V((S, 128), bf16),
    ]
    for b in range(S // BLOCK):
        scratch.append(V((H, BLOCK, M + (b + 1) * BLOCK), bf16))
    shapes = (
        jax.ShapeDtypeStruct((S, D), bf16),
        jax.ShapeDtypeStruct((S, D), bf16),
        jax.ShapeDtypeStruct((D, D), bf16),
        jax.ShapeDtypeStruct((D, D), bf16),
        jax.ShapeDtypeStruct((D, D), bf16),
        jax.ShapeDtypeStruct((D, D), bf16),
        jax.ShapeDtypeStruct((D, FF), bf16),
        jax.ShapeDtypeStruct((D, FF), bf16),
        jax.ShapeDtypeStruct((16, D), f32),
    )
    return pl.pallas_call(
        layer_kernel,
        out_shape=shapes,
        in_specs=[smem, smem, smem] + [vmem] * 10 + [smem] + [vmem] * 4,
        out_specs=[vmem] * len(shapes),
        scratch_shapes=scratch,
        compiler_params=pltpu.CompilerParams(vmem_limit_bytes=64 * 1024 * 1024 - 65536),
        name="layer",
    )(
        counts, lengths, which, x, mem, ends, og,
        gain1.reshape(1, D), shift1.reshape(1, D), wq, wk, wv, wo, slopes,
        gain2.reshape(1, D), shift2.reshape(1, D), w1, w2,
    )


def layer_norm(values, gain, shift):
    centred = values - jnp.mean(values, axis=-1, keepdims=True)
    spread = jnp.mean(centred * centred, axis=-1, keepdims=True)
    return centred * lax.rsqrt(spread + epsilon) * gain + shift


def block_scores(
    q_heads, key_block, q_ends, key_order, key_ends, q_index, head_slopes, score_scale
):
    scores = (
        jnp.einsum("qhd,khd->hqk", q_heads, key_block, preferred_element_type=jnp.float32)
        * score_scale
    )
    distance = (q_ends[:, None] - key_ends[None, :]).astype(jnp.float32)
    scores = scores - head_slopes[:, None, None] * distance[None]
    allowed = key_order[None, :] <= q_index[:, None]
    return (jnp.where(allowed[None], scores, -1e30), distance)


def spread_device(
    tokens,
    memory,
    segment_ends,
    memory_ends,
    segment_counts,
    memory_lengths,
    first_gain,
    first_shift,
    query_weight,
    key_weight,
    value_weight,
    out_weight,
    head_slopes,
    second_gain,
    second_shift,
    hidden_weight,
    output_weight,
    output_grad,
):
    seq_count, slot_count, model_width = tokens.shape
    mem_count = memory.shape[1]
    head_count = head_slopes.shape[0]
    head_dim = model_width // head_count
    score_scale = 1.0 / math.sqrt(head_dim)
    key_rows = mem_count + slot_count
    blocks = lax.axis_size("blk")
    my_block = lax.axis_index("blk")
    x_float = tokens.astype(jnp.float32)
    mem_float = memory.astype(jnp.float32)
    normed = layer_norm(x_float, first_gain, first_shift).astype(jnp.bfloat16)
    mem_normed = layer_norm(mem_float, first_gain, first_shift).astype(jnp.bfloat16)
    key_input = jnp.concatenate([mem_normed, normed], axis=1)
    query = jnp.einsum(
        "std,de->ste", normed, query_weight, preferred_element_type=jnp.float32
    ).astype(jnp.bfloat16)
    pair_weight = jnp.concatenate([key_weight, value_weight], axis=1)
    key_value = jnp.einsum(
        "srd,de->rse", key_input, pair_weight, preferred_element_type=jnp.float32
    ).astype(jnp.bfloat16)
    mem_index = my_block * mem_count + jnp.arange(mem_count, dtype=jnp.int32)
    slot_index = my_block * slot_count + jnp.arange(slot_count, dtype=jnp.int32)
    mem_order = jnp.where(
        mem_index[None, :] >= mem_count * blocks - memory_lengths[:, None], -1, far_order
    )
    slot_order = jnp.where(
        slot_index[None, :] < segment_counts[:, None], slot_index[None, :], far_order
    )
    key_meta = jnp.stack(
        [
            jnp.concatenate([mem_order, slot_order], axis=1),
            jnp.concatenate([memory_ends, segment_ends], axis=1),
        ]
    )
    all_pairs, all_meta = (
        lax.all_gather(key_value, "blk", axis=0, tiled=True),
        lax.all_gather(key_meta, "blk", axis=2, tiled=True),
    )
    query_heads = query.reshape(seq_count, slot_count, head_count, head_dim)

    def pick(seq_index):
        pair_rows = lax.dynamic_index_in_dim(all_pairs, seq_index, 1, keepdims=False)
        meta_rows = lax.dynamic_index_in_dim(all_meta, seq_index, 1, keepdims=False)
        key_heads = pair_rows[:, :model_width].reshape(-1, key_rows, head_count, head_dim)
        value_heads = pair_rows[:, model_width:].reshape(-1, key_rows, head_count, head_dim)
        return (
            key_heads,
            value_heads,
            meta_rows[0].reshape(-1, key_rows),
            meta_rows[1].reshape(-1, key_rows),
        )

    def attend(seq_index):
        key_heads, value_heads, key_order, key_ends = pick(seq_index)
        q_heads = lax.dynamic_index_in_dim(query_heads, seq_index, 0, keepdims=False)
        q_ends = lax.dynamic_index_in_dim(segment_ends, seq_index, 0, keepdims=False)

        def stats_step(running, pieces):
            scores = block_scores(
                q_heads,
                pieces[0],
                q_ends,
                pieces[1],
                pieces[2],
                slot_index,
                head_slopes,
                score_scale,
            )[0]
            running_max = jnp.maximum(running[0], jnp.max(scores, axis=-1))
            running_sum = running[1] * jnp.exp(running[0] - running_max) + jnp.sum(
                jnp.exp(scores - running_max[..., None]), axis=-1
            )
            return ((running_max, running_sum), None)

        start_max = jnp.full((head_count, slot_count), -jnp.inf, jnp.float32)
        (top_max, top_sum), _ = lax.scan(
            stats_step, (start_max, jnp.zeros_like(start_max)), (key_heads, key_order, key_ends)
        )
        log_total = top_max + jnp.log(top_sum)

        def out_step(summed, pieces):
            scores = block_scores(
                q_heads,
                pieces[0],
                q_ends,
                pieces[1],
                pieces[2],
                slot_index,
                head_slopes,
                score_scale,
            )[0]
            attn_probs = jnp.exp(scores - log_total[..., None]).astype(jnp.bfloat16)
            return (
                summed
                + jnp.einsum(
                    "hqk,khd->qhd", attn_probs, pieces[3], preferred_element_type=jnp.float32
                ),
                None,
            )

        start_out = jnp.zeros((slot_count, head_count, head_dim), jnp.float32)
        mixed_heads, _ = lax.scan(
            out_step, start_out, (key_heads, key_order, key_ends, value_heads)
        )
        return (mixed_heads, log_total)

    mixed_all, log_totals = lax.map(attend, jnp.arange(seq_count))
    mixed_low = mixed_all.reshape(seq_count, slot_count, model_width).astype(jnp.bfloat16)
    residual = x_float + jnp.einsum(
        "std,de->ste", mixed_low, out_weight, preferred_element_type=jnp.float32
    )
    second_low = layer_norm(residual, second_gain, second_shift).astype(jnp.bfloat16)
    hidden_pre = jnp.einsum(
        "std,df->stf", second_low, hidden_weight, preferred_element_type=jnp.float32
    )
    act_low = jax.nn.gelu(hidden_pre, approximate=False).astype(jnp.bfloat16)
    layer_out = (
        residual
        + jnp.einsum("stf,fd->std", act_low, output_weight, preferred_element_type=jnp.float32)
    ).astype(jnp.bfloat16)
    grad_output_w = jnp.einsum(
        "stf,std->fd", act_low, output_grad, preferred_element_type=jnp.float32
    )
    d_act = jnp.einsum(
        "std,fd->stf", output_grad, output_weight, preferred_element_type=jnp.float32
    )
    _, gelu_pull = jax.vjp(lambda inner: jax.nn.gelu(inner, approximate=False), hidden_pre)
    d_pre_low = gelu_pull(d_act)[0].astype(jnp.bfloat16)
    grad_hidden_w = jnp.einsum(
        "std,stf->df", second_low, d_pre_low, preferred_element_type=jnp.float32
    )
    d_second = jnp.einsum(
        "stf,df->std", d_pre_low, hidden_weight, preferred_element_type=jnp.float32
    )
    _, second_pull = jax.vjp(layer_norm, residual, second_gain, second_shift)
    d_resid_norm, grad_second_g, grad_second_b = second_pull(d_second)
    d_residual = d_resid_norm + output_grad.astype(jnp.float32)
    d_branch = d_residual.astype(jnp.bfloat16)
    grad_out_w = jnp.einsum("std,ste->de", mixed_low, d_branch, preferred_element_type=jnp.float32)
    d_mixed = jnp.einsum(
        "ste,de->std", d_branch, out_weight, preferred_element_type=jnp.float32
    ).astype(jnp.bfloat16)
    d_mixed_heads = d_mixed.reshape(seq_count, slot_count, head_count, head_dim)

    def query_side(seq_index):
        key_heads, value_heads, key_order, key_ends = pick(seq_index)
        q_heads = lax.dynamic_index_in_dim(query_heads, seq_index, 0, keepdims=False)
        q_ends = lax.dynamic_index_in_dim(segment_ends, seq_index, 0, keepdims=False)
        d_heads = lax.dynamic_index_in_dim(d_mixed_heads, seq_index, 0, keepdims=False)
        log_total = lax.dynamic_index_in_dim(log_totals, seq_index, 0, keepdims=False)

        def probs_of(key_block, order_block, ends_block, value_block):
            scores, distance = block_scores(
                q_heads,
                key_block,
                q_ends,
                order_block,
                ends_block,
                slot_index,
                head_slopes,
                score_scale,
            )
            attn_probs = jnp.exp(scores - log_total[..., None])
            d_probs = jnp.einsum(
                "qhd,khd->hqk", d_heads, value_block, preferred_element_type=jnp.float32
            )
            return (attn_probs, d_probs, distance)

        def delta_step(summed, pieces):
            attn_probs, d_probs, _ = probs_of(pieces[0], pieces[1], pieces[2], pieces[3])
            return (summed + jnp.sum(attn_probs * d_probs, axis=-1), None)

        delta_rows, _ = lax.scan(
            delta_step,
            jnp.zeros((head_count, slot_count), jnp.float32),
            (key_heads, key_order, key_ends, value_heads),
        )

        def grad_step(running, pieces):
            attn_probs, d_probs, distance = probs_of(pieces[0], pieces[1], pieces[2], pieces[3])
            d_scores = (attn_probs * (d_probs - delta_rows[..., None])).astype(jnp.bfloat16)
            d_query = running[0] + jnp.einsum(
                "hqk,khd->qhd", d_scores, pieces[0], preferred_element_type=jnp.float32
            )
            d_slopes = running[1] - jnp.sum(
                d_scores.astype(jnp.float32) * distance[None], axis=(1, 2)
            )
            return ((d_query, d_slopes), None)

        start_grads = (
            jnp.zeros((slot_count, head_count, head_dim), jnp.float32),
            jnp.zeros((head_count,), jnp.float32),
        )
        (d_query, d_slopes), _ = lax.scan(
            grad_step, start_grads, (key_heads, key_order, key_ends, value_heads)
        )
        return (d_query * score_scale, delta_rows, d_slopes)

    d_query_all, delta_all, slope_parts = lax.map(query_side, jnp.arange(seq_count))
    grad_slopes = jnp.sum(slope_parts, axis=0)
    d_query_low = d_query_all.reshape(seq_count, slot_count, model_width).astype(jnp.bfloat16)

    def pair_terms(
        pair_rows, order_block, ends_block, q_heads, q_ends, q_index, d_heads, log_total, delta_rows
    ):
        key_block = pair_rows[:, :model_width].reshape(key_rows, head_count, head_dim)
        value_block = pair_rows[:, model_width:].reshape(key_rows, head_count, head_dim)
        scores, _ = block_scores(
            q_heads, key_block, q_ends, order_block, ends_block, q_index, head_slopes, score_scale
        )
        attn_probs = jnp.exp(scores - log_total[..., None])
        d_probs = jnp.einsum(
            "qhd,khd->hqk", d_heads, value_block, preferred_element_type=jnp.float32
        )
        d_scores = (attn_probs * (d_probs - delta_rows[..., None])).astype(jnp.bfloat16)
        d_value = jnp.einsum(
            "hqk,qhd->khd",
            attn_probs.astype(jnp.bfloat16),
            d_heads,
            preferred_element_type=jnp.float32,
        )
        d_key = (
            jnp.einsum("hqk,qhd->khd", d_scores, q_heads, preferred_element_type=jnp.float32)
            * score_scale
        )
        return jnp.concatenate(
            [d_key.reshape(key_rows, model_width), d_value.reshape(key_rows, model_width)], axis=1
        )

    def one_block(block_index):
        offset = block_index * key_rows
        pair_block = lax.dynamic_slice_in_dim(all_pairs, offset, key_rows, 0)
        meta_block = lax.dynamic_slice_in_dim(all_meta, offset, key_rows, 2)
        return jax.vmap(pair_terms, in_axes=(1, 0, 0, 0, 0, None, 0, 0, 0), out_axes=1)(
            pair_block,
            meta_block[0],
            meta_block[1],
            query_heads,
            segment_ends,
            slot_index,
            d_mixed_heads,
            log_totals,
            delta_all,
        )

    pieces = lax.map(one_block, jnp.arange(lax.axis_size("blk") * key_rows // key_rows))
    pair_grads = lax.psum_scatter(
        pieces.reshape(lax.axis_size("blk") * key_rows, seq_count, 2 * model_width).astype(
            jnp.bfloat16
        ),
        "blk",
        scatter_dimension=0,
        tiled=True,
    )
    grad_pair_w = jnp.einsum(
        "srd,rse->de", key_input, pair_grads, preferred_element_type=jnp.float32
    )
    grad_key_w = grad_pair_w[:, :model_width]
    grad_value_w = grad_pair_w[:, model_width:]
    d_key_input = jnp.einsum(
        "rse,de->srd", pair_grads, pair_weight, preferred_element_type=jnp.float32
    )
    grad_query_w = jnp.einsum(
        "std,ste->de", normed, d_query_low, preferred_element_type=jnp.float32
    )
    d_normed = (
        jnp.einsum("ste,de->std", d_query_low, query_weight, preferred_element_type=jnp.float32)
        + d_key_input[:, mem_count:]
    )
    _, first_pull = jax.vjp(layer_norm, x_float, first_gain, first_shift)
    d_tokens, gain_slots, shift_slots = first_pull(d_normed)
    _, mem_pull = jax.vjp(
        lambda gain, shift: layer_norm(mem_float, gain, shift), first_gain, first_shift
    )
    gain_mem, shift_mem = mem_pull(d_key_input[:, :mem_count])
    input_grad = (d_tokens + d_residual).astype(jnp.bfloat16)
    grad_first_g = gain_slots + gain_mem
    grad_first_b = shift_slots + shift_mem
    summed = lax.psum(
        (
            grad_first_g,
            grad_first_b,
            grad_query_w,
            grad_key_w,
            grad_value_w,
            grad_out_w,
            grad_slopes,
            grad_second_g,
            grad_second_b,
            grad_hidden_w,
            grad_output_w,
        ),
        ("seq", "blk"),
    )
    return (
        layer_out,
        input_grad,
        summed[0],
        summed[1],
        summed[2],
        summed[3],
        summed[4],
        summed[5],
        summed[6],
        summed[7],
        summed[8],
        summed[9],
        summed[10],
    )


def whole_device(*args):
    tokens, memory, segment_ends, memory_ends, counts, lengths = args[:6]
    params = args[6:17]
    output_grad = args[17]
    D = tokens.shape[2]

    def gather(array):
        return lax.all_to_all(array, "blk", 0, 1, tiled=True)[0]

    x = gather(tokens)
    mem = gather(memory)
    og = gather(output_grad)
    ends = jnp.concatenate([gather(memory_ends), gather(segment_ends)])[None]
    which = lax.axis_index("blk").astype(jnp.int32).reshape(1)
    layer, in_grad, gq, gk, gv, go, gw1, gw2t, small = layer_call(
        counts, lengths, which, x, mem, ends, og, params
    )

    def scatter(array):
        return lax.all_to_all(array[None], "blk", 1, 0, tiled=True)

    gq, gk, gv, go, gw1, gw2t, small = lax.psum(
        (gq, gk, gv, go, gw1, gw2t, small), ("seq", "blk")
    )
    H = params[6].shape[0]
    return (
        scatter(layer),
        scatter(in_grad),
        small[0],
        small[1],
        gq.astype(f32),
        gk.astype(f32),
        gv.astype(f32),
        go.astype(f32),
        jnp.sum(small[8 : 8 + H], axis=1),
        small[2],
        small[3],
        gw1.astype(f32),
        gw2t.astype(f32).T,
    )


def per_device(*args):
    if args[0].shape[0] == lax.axis_size("blk"):
        return whole_device(*args)
    return spread_device(*args)


def solution(mesh):
    placed = (
        P("seq", "blk", None),
        P("seq", "blk", None),
        P("seq", "blk"),
        P("seq", "blk"),
        P("seq"),
        P("seq"),
        P(),
        P(),
        P(),
        P(),
        P(),
        P(),
        P(),
        P(),
        P(),
        P(),
        P(),
        P("seq", "blk", None),
    )
    return jax.shard_map(
        per_device,
        mesh=mesh,
        in_specs=placed,
        out_specs=(
            P("seq", "blk", None),
            P("seq", "blk", None),
            P(),
            P(),
            P(),
            P(),
            P(),
            P(),
            P(),
            P(),
            P(),
            P(),
            P(),
        ),
        check_vma=False,
    )
```

```python
import functools
import math

import jax
import jax.numpy as jnp
from jax import lax
from jax.experimental import pallas as pl
from jax.experimental.pallas import tpu as pltpu
from jax.sharding import PartitionSpec as P

epsilon = 1e-05
far_order = 1073741824
f32 = jnp.float32
bf16 = jnp.bfloat16
BLOCK = 256
LOG2E = 1.4426950408889634
LN2 = 0.6931471805599453


def dot_nn(left, right):
    return lax.dot_general(left, right, (((1,), (0,)), ((), ())), preferred_element_type=f32)


def dot_nt(left, right):
    return lax.dot_general(left, right, (((1,), (1,)), ((), ())), preferred_element_type=f32)


def norm_stats(values):
    centred = values - jnp.mean(values, axis=-1, keepdims=True)
    spread = jnp.mean(centred * centred, axis=-1, keepdims=True)
    scale = lax.rsqrt(spread + epsilon)
    return centred * scale, scale


def norm_back(unit, scale, grad_unit):
    mean_grad = jnp.mean(grad_unit, axis=-1, keepdims=True)
    mean_prod = jnp.mean(grad_unit * unit, axis=-1, keepdims=True)
    return (grad_unit - mean_grad - unit * mean_prod) * scale


def pieces_of(value, count):
    out = []
    for _ in range(count):
        part = value.astype(bf16).astype(f32)
        out.append(part)
        value = value - part
    return out


ERFC_P = 0.4
ERFC_C = (0.22567586600780487, 0.2256695181131363, 0.2078438550233841, 0.16853390634059906, 0.1414608359336853, -0.005667657125741243, 0.16915477812290192, -0.18294358253479004, 0.050272583961486816)


def gelu_both(x):
    a = jnp.abs(x) * math.sqrt(0.5)
    t = 1.0 / (1.0 + ERFC_P * a)
    poly = jnp.full_like(t, ERFC_C[-1])
    for c in ERFC_C[-2::-1]:
        poly = poly * t + c
    ex = jnp.exp(-0.5 * (x * x))
    half = 0.5 * (poly * t * ex)
    cdf = jnp.where(x >= 0, 1.0 - half, half)
    return x * cdf, cdf + x * ex * (1.0 / math.sqrt(2.0 * math.pi))


def col_sum8(value):
    return jnp.sum(value.reshape(-1, 8, value.shape[-1]), axis=0)


def flip(bit):
    return 1 - bit


def layer_kernel(
    talk,
    counts_ref,
    lengths_ref,
    slopes_ref,
    tokens_ref,
    memory_ref,
    ends_ref,
    grad_ref,
    gain1_ref,
    shift1_ref,
    gain2_ref,
    shift2_ref,
    wq_hbm,
    wk_hbm,
    wv_hbm,
    wo_hbm,
    w1_hbm,
    w2_hbm,
    layer_hbm,
    ingrad_hbm,
    grads_hbm,
    small_ref,
    x_ref,
    mem_ref,
    og_ref,
    ends_s,
    wq_ref,
    wk_ref,
    wv_ref,
    wo_ref,
    w1_ref,
    w2_ref,
    keyint,
    k_s,
    v_s,
    kx,
    q_s,
    qt,
    rl_s,
    o_s,
    mixed,
    second_s,
    secondt,
    ogt,
    act_s,
    dpre_s,
    acc_s,
    dres,
    dolt,
    delta_s,
    stage,
    g_s,
    rc_s,
    r1_s,
    r2_s,
    sm_own,
    sm_in,
    load_sem,
    ex_send,
    ex_recv,
    ar_send,
    ar_recv,
    sm_send,
    sm_recv,
    out_sem,
    *probs,
):
    S, D = x_ref.shape
    M = mem_ref.shape[0]
    R = M + S
    FF = w1_ref.shape[1]
    H = slopes_ref.shape[0]
    DH = D // H
    HP = H // 2
    NB = S // BLOCK
    MB = M // BLOCK
    SH = S // 2
    MH = M // 2
    KC = 512
    CH = 512
    NC = FF // CH

    if talk:
        seq = lax.axis_index("seq")
        blk = lax.axis_index("blk")
    else:
        seq = 0
        blk = 0
    core = seq % 2
    why = (seq // 2) % 2
    zed = seq // 4

    def at(z=None, y=None, c=None, x=None):
        z = zed if z is None else z
        y = why if y is None else y
        c = core if c is None else c
        return {"seq": z * 4 + y * 2 + c, "blk": blk if x is None else x}

    sibling = at(c=flip(core))
    partner = at(x=flip(blk))
    z_to = [zed + 1 - 2 * (zed % 2), (zed + 2) % 4, 3 - zed]
    z_peers = [(at(z=z), z) for z in z_to]
    plane = blk * 2 + why
    xy_peers = [
        (at(y=flip(why)), blk * 2 + flip(why)),
        (at(x=flip(blk)), flip(blk) * 2 + why),
        (at(x=flip(blk), y=flip(why)), flip(blk) * 2 + flip(why)),
    ]
    z_group = (zed, z_peers)
    xy_group = (plane, xy_peers)

    def remote(src, dst, send, recv, device):
        return pltpu.make_async_remote_copy(
            src_ref=src,
            dst_ref=dst,
            send_sem=send,
            recv_sem=recv,
            device_id=device,
            device_id_type=pl.DeviceIdType.MESH,
        )

    other = 1 - blk

    def half_rows(half, size):
        return pl.ds(pl.multiple_of(half * size, BLOCK), size)

    def slot_piece(part, index, half, i):
        src = tokens_ref if part == 0 else grad_ref
        dst = x_ref if part == 0 else og_ref
        rows = pl.ds(pl.multiple_of(half * SH + i * BLOCK, BLOCK), BLOCK)
        return src.at[index, i * BLOCK : (i + 1) * BLOCK, :], dst.at[rows, :]

    nslot = SH // BLOCK
    loads = [
        (memory_ref.at[blk], mem_ref.at[half_rows(blk, MH), :]),
        (ends_ref.at[blk], ends_s.at[blk]),
        (wk_hbm, wk_ref),
        (wv_hbm, wv_ref),
        (wq_hbm, wq_ref),
    ]
    loads += [slot_piece(0, blk, blk, i) for i in range(nslot)]
    n_first = len(loads)
    loads += [(wo_hbm, wo_ref), (w1_hbm, w1_ref), (w2_hbm, w2_ref)]
    loads += [slot_piece(1, blk, blk, i) for i in range(nslot)]
    copies = [
        pltpu.make_async_copy(src, dst, load_sem.at[i]) for i, (src, dst) in enumerate(loads)
    ]
    sends = [
        (memory_ref.at[other], mem_ref.at[half_rows(blk, MH), :]),
        (ends_ref.at[other], ends_s.at[blk]),
    ]
    sends += [slot_piece(0, other, blk, i) for i in range(nslot)]
    sends += [slot_piece(1, other, blk, i) for i in range(nslot)]
    if talk:
        exchange = [
            remote(src, dst, ex_send.at[i], ex_recv.at[i], partner)
            for i, (src, dst) in enumerate(sends)
        ]
    else:
        local = [
            (memory_ref.at[other], mem_ref.at[half_rows(other, MH), :]),
            (ends_ref.at[other], ends_s.at[other]),
        ]
        local += [slot_piece(0, other, other, i) for i in range(nslot)]
        local += [slot_piece(1, other, other, i) for i in range(nslot)]
        exchange = [
            pltpu.make_async_copy(src, dst, ex_send.at[i]) for i, (src, dst) in enumerate(local)
        ]
    for copy in copies[:n_first]:
        copy.start()
    if talk:
        barrier = pltpu.get_barrier_semaphore()
        greet = [sibling] + [d for d, _ in z_peers] + [d for d, _ in xy_peers]
        for device in greet:
            pl.semaphore_signal(
                barrier, inc=1, device_id=device, device_id_type=pl.DeviceIdType.MESH
            )
        pl.semaphore_wait(barrier, len(greet))
    for copy in exchange:
        copy.start()
    for copy in copies[n_first:]:
        copy.start()

    def arrive(i):
        if talk:
            exchange[i].wait_recv()
        else:
            exchange[i].wait()

    units = []
    for c in range(NC):
        units.append((c * 2 * CH, 2 * CH, c % 3 == 2))
    units.append((2 * FF, D, False))
    for p in range(HP):
        units.append((2 * FF + D + p * 384, 384, False))
    half0 = core * (D // 2)
    N1, N2 = D // 8, D // 32

    def rows_at(start, size):
        return pl.ds(pl.multiple_of(start, 16), size)

    def unit_copies(u, phase):
        col, width, z_first = units[u]
        (g, peers1), (h, peers2) = (z_group, xy_group) if z_first else (xy_group, z_group)
        cols = slice(col, col + width)
        out = []
        if phase == 0:
            rows = rows_at((1 - core) * (D // 2), D // 2)
            out.append((g_s.at[rows, cols], rc_s.at[:, cols], 0, sibling))
        elif phase == 1:
            for d, (device, index) in enumerate(peers1):
                rows = rows_at(half0 + index * N1, N1)
                out.append((g_s.at[rows, cols], r1_s.at[d, :, cols], 1 + d, device))
        elif phase == 2:
            for d, (device, index) in enumerate(peers2):
                rows = rows_at(half0 + g * N1 + index * N2, N2)
                out.append((g_s.at[rows, cols], r2_s.at[d, :, cols], 4 + d, device))
        elif phase == 3:
            rows = rows_at(half0 + g * N1 + h * N2, N2)
            for d, (device, _) in enumerate(peers2):
                out.append((g_s.at[rows, cols], grads_hbm.at[rows, cols], 7 + d, device))
        elif phase == 4:
            rows = rows_at(half0 + g * N1, N1)
            for d, (device, _) in enumerate(peers1):
                out.append((grads_hbm.at[rows, cols], grads_hbm.at[rows, cols], 10 + d, device))
        else:
            rows = rows_at(half0, D // 2)
            out.append((grads_hbm.at[rows, cols], grads_hbm.at[rows, cols], 13, sibling))
        return [
            remote(src, dst, ar_send.at[u, k], ar_recv.at[u, k], device)
            for src, dst, k, device in out
        ]

    def unit_add(u, phase):
        col, width, z_first = units[u]
        (g, _), (h, _) = (z_group, xy_group) if z_first else (xy_group, z_group)
        cols = slice(col, col + width)
        if phase == 0:
            step = 64

            def add(i, _):
                rows = rows_at(half0 + i * step, step)
                mine = g_s[rows, cols].astype(f32)
                theirs = rc_s[rows_at(i * step, step), cols].astype(f32)
                g_s[rows, cols] = (mine + theirs).astype(bf16)
                return 0

            lax.fori_loop(0, D // 2 // step, add, 0)
        elif phase == 1:
            rows = rows_at(half0 + g * N1, N1)
            total = g_s[rows, cols].astype(f32)
            for d in range(3):
                total = total + r1_s[d, :, cols].astype(f32)
            g_s[rows, cols] = total.astype(bf16)
        elif phase == 2:
            rows = rows_at(half0 + g * N1 + h * N2, N2)
            total = g_s[rows, cols].astype(f32)
            for d in range(3):
                total = total + r2_s[d, :, cols].astype(f32)
            g_s[rows, cols] = total.astype(bf16)

    def unit_out(u):
        col, width, z_first = units[u]
        (g, _), (h, _) = (z_group, xy_group) if z_first else (xy_group, z_group)
        cols = slice(col, col + width)
        rows = rows_at(half0 + g * N1 + h * N2, N2) if talk else slice(0, D)
        return pltpu.make_async_copy(g_s.at[rows, cols], grads_hbm.at[rows, cols], out_sem.at[u])

    def advance(u, step):
        if not talk:
            return
        if step > 0:
            for copy in unit_copies(u, step - 1):
                copy.wait()
            unit_add(u, step - 1)
        if step == 3:
            unit_out(u).start()
        if step == 4:
            unit_out(u).wait()
        if step < 6:
            for copy in unit_copies(u, step):
                copy.start()

    gain1 = gain1_ref[...]
    shift1 = shift1_ref[...]
    gain2 = gain2_ref[...]
    shift2 = shift2_ref[...]
    count = counts_ref[blk]
    length = lengths_ref[blk]

    def project(normed, key_rows):
        keyint[:, key_rows] = normed.T
        k_s[key_rows, :] = dot_nn(normed, wk_ref[...]).astype(bf16)
        v_s[key_rows, :] = dot_nn(normed, wv_ref[...]).astype(bf16)

    def norm_mem(b):
        rows = pl.ds(pl.multiple_of(b * BLOCK, BLOCK), BLOCK)
        unit, _ = norm_stats(mem_ref[rows, :].astype(f32))
        project((unit * gain1 + shift1).astype(bf16), rows)

    def norm_slot(b):
        rows = pl.ds(pl.multiple_of(b * BLOCK, BLOCK), BLOCK)
        key_rows = pl.ds(pl.multiple_of(b * BLOCK + M, BLOCK), BLOCK)
        unit, _ = norm_stats(x_ref[rows, :].astype(f32))
        normed = (unit * gain1 + shift1).astype(bf16)
        project(normed, key_rows)
        query = (dot_nn(normed, wq_ref[...]) * (LOG2E / math.sqrt(DH))).astype(bf16)
        q_s[rows, :] = query
        qt[:, rows] = query.T

    for copy in copies[:n_first]:
        copy.wait()
    mh = MH // BLOCK
    lax.fori_loop(0, mh, lambda i, _: (norm_mem(blk * mh + i), 0)[1], 0)
    lax.fori_loop(0, nslot, lambda i, _: (norm_slot(blk * nslot + i), 0)[1], 0)
    arrive(0)
    lax.fori_loop(0, mh, lambda i, _: (norm_mem(other * mh + i), 0)[1], 0)
    arrive(1)

    lane = lax.broadcasted_iota(jnp.int32, (128, 128), 1)
    row = lax.broadcasted_iota(jnp.int32, (128, 128), 0)

    def end_row(start, size):
        if start < M:
            half, off = start // MH, start % MH
        else:
            half, off = (start - M) // SH, MH + (start - M) % SH
        return ends_s[half, :, off : off + size].astype(f32)

    for r in range(R // 128):
        end_col = jnp.broadcast_to(end_row(r * 128, 128), (128, 128)).T
        high = jnp.floor(end_col * (1.0 / 256.0)) * 256.0
        index = row + r * 128
        if r * 128 < M:
            valid = index >= M - length
        else:
            valid = index - M < count
        bias = jnp.where(valid, 0.0, -1e30)
        extra = jnp.where(lane < 3, high, jnp.where(lane < 6, end_col - high, bias))
        extra = jnp.where(lane == 7, 1.0, jnp.where(lane > 7, 0.0, extra))
        kx[r * 128 : (r + 1) * 128, :] = extra.astype(bf16)

    for i in range(nslot):
        arrive(2 + i)
        norm_slot(other * nslot + i)

    lane_q = lax.broadcasted_iota(jnp.int32, (BLOCK, 128), 1)
    first_half = lane_q < DH
    lane_row = lax.broadcasted_iota(jnp.int32, (1, 128), 1)

    def key_chunks(b):
        end = M + (b + 1) * BLOCK
        return [(start, min(KC, end - start)) for start in range(0, end, KC)]

    def key_full(lanes, start, size):
        return jnp.concatenate(
            [k_s[start : start + size, lanes], kx[start : start + size, :]], axis=1
        )

    def value_full(lanes, start, size):
        return jnp.concatenate(
            [v_s[start : start + size, lanes], jnp.ones((size, 128), bf16)], axis=1
        )

    def query_extra(head):
        slope = jnp.full((1, 128), slopes_ref[head] * LOG2E, f32)
        s1, s2, s3 = pieces_of(slope, 3)
        where = jnp.where(lane_row >= 3, lane_row - 3, lane_row)
        out = jnp.where(where == 0, s1, jnp.where(where == 1, s2, s3))
        return jnp.where(lane_row < 6, out, jnp.where(lane_row == 6, 1.0, 0.0))

    rl_s[...] = jnp.zeros_like(rl_s)
    for b in range(NB):
        rows = slice(b * BLOCK, (b + 1) * BLOCK)
        e_ref = probs[b]

        def fwd_pair(p, _):
            lanes = pl.ds(pl.multiple_of(p * 128, 128), 128)
            q_pair = q_s[rows, lanes]
            outs = []
            for half in range(2):
                keep = first_half if half == 0 else jnp.logical_not(first_half)
                q_half = jnp.where(keep, q_pair, jnp.zeros_like(q_pair))
                extra = jnp.broadcast_to(query_extra(2 * p + half), (BLOCK, 128)).astype(bf16)
                q_full = jnp.concatenate([q_half, extra], axis=1)
                chunks = key_chunks(b)
                scores = [dot_nt(q_full, key_full(lanes, k0, kn)) for k0, kn in chunks]
                below = lax.broadcasted_iota(
                    jnp.int32, (BLOCK, BLOCK), 1
                ) <= lax.broadcasted_iota(jnp.int32, (BLOCK, BLOCK), 0)
                last = scores[-1]
                cut = last.shape[1] - BLOCK
                diag = jnp.where(below, last[:, cut:], -1e30)
                scores[-1] = jnp.concatenate([last[:, :cut], diag], axis=1) if cut else diag
                top = jnp.max(scores[0], axis=1, keepdims=True)
                for part in scores[1:]:
                    top = jnp.maximum(top, jnp.max(part, axis=1, keepdims=True))
                both = jnp.zeros((BLOCK, 256), f32)
                for part, (k0, kn) in zip(scores, chunks):
                    e = jnp.exp2(part - top).astype(bf16)
                    e_ref[2 * p + half, :, k0 : k0 + kn] = e
                    both = both + dot_nn(e, value_full(lanes, k0, kn))
                outs.append((both[:, 0:128], 1.0 / both[:, 128:256]))
            rl = jnp.where(first_half, outs[0][1], outs[1][1])
            o = jnp.where(first_half, outs[0][0], outs[1][0]) * rl
            packed = jnp.where(lane_q == 2 * p, outs[0][1], rl_s[rows, :])
            rl_s[rows, :] = jnp.where(lane_q == 2 * p + 1, outs[1][1], packed)
            o_s[rows, lanes] = o
            mixed[rows, lanes] = o.astype(bf16)
            return 0

        lax.fori_loop(0, HP, fwd_pair, 0)

    for copy in copies[n_first:]:
        copy.wait()
    for i in range(nslot):
        arrive(2 + nslot + i)

    def residual_of(rows):
        return x_ref[rows, :].astype(f32) + dot_nn(mixed[rows, :], wo_ref[...])

    def feed_prep(b, _):
        rows = pl.ds(pl.multiple_of(b * BLOCK, BLOCK), BLOCK)
        residual = residual_of(rows)
        unit, _ = norm_stats(residual)
        second = (unit * gain2 + shift2).astype(bf16)
        second_s[rows, :] = second
        secondt[:, rows] = second.T
        ogt[:, rows] = og_ref[rows, :].T
        acc_s[rows, :] = residual
        return 0

    lax.fori_loop(0, NB, feed_prep, 0)
    for c in range(NC):
        cols = slice(c * CH, (c + 1) * CH)

        def feed(b, _):
            rows = pl.ds(pl.multiple_of(b * BLOCK, BLOCK), BLOCK)
            hidden = dot_nn(second_s[rows, :], w1_ref[:, cols])
            d_act = dot_nt(og_ref[rows, :], w2_ref[cols, :])
            act, slope = gelu_both(hidden)
            act = act.astype(bf16)
            d_pre = (d_act * slope).astype(bf16)
            act_s[rows, :] = act
            dpre_s[rows, :] = d_pre
            acc_s[rows, :] += dot_nn(act, w2_ref[cols, :])
            d_second = dot_nt(d_pre, w1_ref[:, cols])
            dres[rows, :] = d_second if c == 0 else dres[rows, :] + d_second
            return 0

        lax.fori_loop(0, NB, feed, 0)
        base = c * 2 * CH
        for r in range(D // BLOCK):
            rows = slice(r * BLOCK, (r + 1) * BLOCK)
            g_s[rows, base : base + CH] = dot_nn(secondt[rows, :], dpre_s[...]).astype(bf16)
            g_s[rows, base + CH : base + 2 * CH] = dot_nn(ogt[rows, :], act_s[...]).astype(bf16)
        ticks(advance, "feed", c)

    def feed_post(b, sums):
        rows = pl.ds(pl.multiple_of(b * BLOCK, BLOCK), BLOCK)
        unit, scale = norm_stats(residual_of(rows))
        stage[rows, :] = acc_s[rows, :].astype(bf16)
        d_second = dres[rows, :]
        d_residual = og_ref[rows, :].astype(f32) + norm_back(unit, scale, d_second * gain2)
        dres[rows, :] = d_residual
        d_branch = d_residual.astype(bf16)
        act_s[rows, :] = d_branch
        secondt[:, rows] = mixed[rows, :].T
        d_mixed = dot_nt(d_branch, wo_ref[...]).astype(bf16).astype(f32)
        rl_b = rl_s[rows, :]
        rl_wide = []
        for p in range(HP):
            first = jnp.broadcast_to(rl_b[:, 2 * p : 2 * p + 1], (BLOCK, 128))
            second = jnp.broadcast_to(rl_b[:, 2 * p + 1 : 2 * p + 2], (BLOCK, 128))
            rl_wide.append(jnp.where(first_half, first, second))
        dol_b = (d_mixed * jnp.concatenate(rl_wide, axis=1)).astype(bf16)
        mixed[rows, :] = dol_b
        dolt[:, rows] = dol_b.T
        prod = dol_b.astype(f32) * o_s[rows, :]
        packed = jnp.zeros((BLOCK, 128), f32)
        for head in range(H):
            part = prod[:, (head // 2) * 128 : (head // 2 + 1) * 128]
            keep = first_half if head % 2 == 0 else jnp.logical_not(first_half)
            delta = jnp.sum(jnp.where(keep, part, 0.0), axis=1, keepdims=True)
            for k, piece in enumerate(pieces_of(jnp.broadcast_to(-delta, (BLOCK, 128)), 3)):
                packed = jnp.where(lane_q == 4 * head + k, piece, packed)
        delta_s[rows, :] = packed.astype(bf16)
        return sums[0] + col_sum8(d_second * unit), sums[1] + col_sum8(d_second)

    zero8 = jnp.zeros((8, D), f32)
    gain2_sum, shift2_sum = lax.fori_loop(0, NB, feed_post, (zero8, zero8))
    for r in range(D // BLOCK):
        rows = slice(r * BLOCK, (r + 1) * BLOCK)
        g_s[rows, 2 * FF : 2 * FF + D] = dot_nn(secondt[rows, :], act_s[...]).astype(bf16)

    def give(result, hbm, k):
        own = pltpu.make_async_copy(
            result.at[half_rows(blk, SH), :], hbm.at[blk], load_sem.at[k]
        )
        theirs = result.at[half_rows(other, SH), :]
        if talk:
            away = remote(theirs, hbm.at[blk], ex_send.at[n_ex + k], ex_recv.at[n_ex + k], partner)
        else:
            away = pltpu.make_async_copy(theirs, hbm.at[other], ex_send.at[n_ex + k])
        return own, away

    n_ex = len(sends)
    layer_copies = give(stage, layer_hbm, 0)
    for copy in layer_copies:
        copy.start()
    ticks(advance, "post", 0)

    small_ref[...] = jnp.zeros_like(small_ref)
    NK = R // KC
    lane_w = (lane_q == 0) | (lane_q == 3)

    def bwd_pair(p, slope_sums):
        lanes = pl.ds(pl.multiple_of(p * 128, 128), 128)
        acc_s[0 : 2 * NK * 128, :] = jnp.zeros((2 * NK * 128, KC), f32)
        for b in range(NB):
            rows = slice(b * BLOCK, (b + 1) * BLOCK)
            e_ref = probs[b]
            end_b = jnp.broadcast_to(end_row(M + b * BLOCK, BLOCK), (128, BLOCK)).T
            weight = jnp.where(lane_w, 1.0, jnp.where(lane_q == 7, -end_b, 0.0))
            dol_pair = mixed[rows, lanes]
            outs = []
            for half in range(2):
                head = 2 * p + half
                keep = first_half if half == 0 else jnp.logical_not(first_half)
                d_half = jnp.where(keep, dol_pair, jnp.zeros_like(dol_pair))
                delta = delta_s[rows, :]
                delta = jnp.where(lane_q // 4 == head, delta, jnp.zeros_like(delta))
                d_full = jnp.concatenate([d_half, delta], axis=1)
                hrows = pl.ds(pl.multiple_of(head * DH, DH), DH)
                q_t = qt[hrows, rows]
                d_t = dolt[hrows, rows]
                dqx = jnp.zeros((BLOCK, 256), f32)
                for j, (k0, kn) in enumerate(key_chunks(b)):
                    e = e_ref[head, :, k0 : k0 + kn]
                    ds = (dot_nt(d_full, value_full(lanes, k0, kn)) * e.astype(f32)).astype(bf16)
                    dqx = dqx + dot_nn(ds, key_full(lanes, k0, kn))
                    at_k = j * 128 + half * DH
                    acc_s[at_k : at_k + DH, 0:kn] += dot_nn(q_t, ds)
                    at_v = (NK + j) * 128 + half * DH
                    acc_s[at_v : at_v + DH, 0:kn] += dot_nn(d_t, e)
                outs.append(dqx[:, 0:128])
                tail = jnp.sum(dqx[:, 128:256] * weight, axis=0, keepdims=True)
                here = lax.broadcasted_iota(jnp.int32, (8, 128), 0) == head
                slope_sums = slope_sums + jnp.where(here, tail, 0.0)
            dq = jnp.where(first_half, outs[0], outs[1]) * (1.0 / math.sqrt(DH))
            q_s[rows, lanes] = dq.astype(bf16)
            for k in range(HP):
                if has_ticks("bwd", k * NB + b):

                    @pl.when(p == k)
                    def _():
                        ticks(advance, "bwd", k * NB + b)

        for j in range(NK):
            dk = (acc_s[j * 128 : (j + 1) * 128, :] * LN2).astype(bf16).T
            k_s[j * KC : (j + 1) * KC, lanes] = dk
            dv = acc_s[(NK + j) * 128 : (NK + j + 1) * 128, :].astype(bf16).T
            v_s[j * KC : (j + 1) * KC, lanes] = dv
        for r in range(D // BLOCK):
            rows = slice(r * BLOCK, (r + 1) * BLOCK)
            gq = dot_nn(keyint[rows, M:], q_s[:, lanes]).astype(bf16)
            pair = jnp.concatenate([k_s[:, lanes], v_s[:, lanes]], axis=1)
            gkv = dot_nn(keyint[rows, :], pair).astype(bf16)
            col = 2 * FF + D + p * 384
            g_s[rows, pl.ds(pl.multiple_of(col, 128), 128)] = gq
            g_s[rows, pl.ds(pl.multiple_of(col + 128, 128), 256)] = gkv
        for k in range(HP):
            if has_ticks("pair", k):

                @pl.when(p == k)
                def _():
                    ticks(advance, "pair", k)

        return slope_sums

    slope_sums = lax.fori_loop(0, HP, bwd_pair, jnp.zeros((8, 128), f32))

    def key_back(key_rows):
        return dot_nt(k_s[key_rows, :], wk_ref[...]) + dot_nt(v_s[key_rows, :], wv_ref[...])

    def mem_back(b, sums):
        rows = pl.ds(pl.multiple_of(b * BLOCK, BLOCK), BLOCK)
        unit, _ = norm_stats(mem_ref[rows, :].astype(f32))
        d_rows = key_back(rows)
        return sums[0] + col_sum8(d_rows * unit), sums[1] + col_sum8(d_rows)

    def slot_back(b, sums):
        rows = pl.ds(pl.multiple_of(b * BLOCK, BLOCK), BLOCK)
        key_rows = pl.ds(pl.multiple_of(b * BLOCK + M, BLOCK), BLOCK)
        unit, scale = norm_stats(x_ref[rows, :].astype(f32))
        d_rows = key_back(key_rows) + dot_nt(q_s[rows, :], wq_ref[...])
        grad = norm_back(unit, scale, d_rows * gain1) + dres[rows, :]
        stage[rows, :] = grad.astype(bf16)
        return sums[0] + col_sum8(d_rows * unit), sums[1] + col_sum8(d_rows)

    layer_copies[0].wait()
    if talk:
        layer_copies[1].wait_send()
    else:
        layer_copies[1].wait()
    sums = (zero8, zero8)
    ingrad_own, ingrad_away = give(stage, ingrad_hbm, 1)
    for i in range(nslot):
        sums = slot_back(other * nslot + i, sums)
        ticks(advance, "tail", i)
    ingrad_away.start()
    sums = lax.fori_loop(0, MB, mem_back, sums)
    ticks(advance, "tail", nslot)
    for i in range(nslot):
        sums = slot_back(blk * nslot + i, sums)
        ticks(advance, "tail", nslot + 1 + i)
    ingrad_own.start()
    gain1_sum, shift1_sum = sums
    sm_own[0] = jnp.zeros_like(sm_own[0])
    for k, part in enumerate((gain1_sum, shift1_sum, gain2_sum, shift2_sum)):
        sm_own[0, k : k + 1, :] = jnp.sum(part, axis=0, keepdims=True)
    total = jnp.broadcast_to(jnp.sum(slope_sums, axis=1, keepdims=True), (8, 128))
    sm_own[0, 4:5, 0:128] = jnp.sum(
        jnp.where(lax.broadcasted_iota(jnp.int32, (8, 128), 0)
                  == lax.broadcasted_iota(jnp.int32, (8, 128), 1), total, 0.0),
        axis=0, keepdims=True)

    if talk:
        k = 0
        for level, devices in enumerate(
            ([sibling], [d for d, _ in z_peers], [d for d, _ in xy_peers])
        ):
            hops = []
            for device in devices:
                hops.append(
                    remote(sm_own.at[level], sm_in.at[k], sm_send.at[k], sm_recv.at[k], device)
                )
                k += 1
            for hop in hops:
                hop.start()
            ticks(advance, "small", level)
            total = sm_own[level]
            for i, hop in enumerate(hops):
                hop.wait()
                total = total + sm_in[k - len(hops) + i]
            sm_own[level + 1] = total
        small_ref[...] = sm_own[3]
    else:
        for level in range(3):
            ticks(advance, "small", level)
        small_ref[...] = sm_own[0]
    ticks(advance, "last", 0)
    ingrad_own.wait()
    if not talk:
        for u in range(len(units)):
            unit_out(u).start()
            unit_out(u).wait()
    if talk:
        for copy in exchange:
            copy.wait_send()
        layer_copies[1].wait_recv()
    ingrad_away.wait()


SCHEDULE = {}


def plan(points):
    for key, moves in points.items():
        SCHEDULE[key] = moves


def has_ticks(kind, index):
    return (kind, index) in SCHEDULE


def ticks(advance, kind, index):
    for u, step in SCHEDULE.get((kind, index), ()):
        advance(u, step)


def make_plan():
    points = [("feed", c) for c in range(4)] + [("post", 0)]
    for k in range(4):
        points += [("bwd", k * 4 + b) for b in range(4)] + [("pair", k)]
    points += [("tail", i) for i in range(5)]
    points += [("small", i) for i in range(3)] + [("last", 0)]
    where = {key: i for i, key in enumerate(points)}
    ready = [where["feed", c] for c in range(4)] + [where["post", 0]]
    ready += [where["pair", k] for k in range(4)]
    table = {}
    for u, start in enumerate(ready):
        spot = start
        for step in range(7):
            spot = min(spot, len(points) - 1)
            table.setdefault(spot, []).append((u, step))
            kind = points[spot][0]
            spot += 1 if kind in ("feed", "post", "tail", "small", "pair") else 2
    for spot, moves in table.items():
        SCHEDULE[points[spot]] = tuple(sorted(moves, key=lambda move: (move[1], move[0])))


make_plan()


def layer_call(counts, lengths, tokens, memory, ends, grad, params, talk=True):
    _, SH, D = tokens.shape
    MH = memory.shape[1]
    S, M = 2 * SH, 2 * MH
    R = M + S
    gain1, shift1, wq, wk, wv, wo, slopes, gain2, shift2, w1, w2 = params
    FF = w1.shape[1]
    H = slopes.shape[0]
    vmem = pl.BlockSpec(memory_space=pltpu.VMEM)
    smem = pl.BlockSpec(memory_space=pltpu.SMEM)
    hbm = pl.BlockSpec(memory_space=pl.ANY)
    V = pltpu.VMEM
    G = 2 * FF + 4 * D
    units = FF // 512 + 1 + H // 2
    dma = pltpu.SemaphoreType.DMA
    scratch = [
        V((S, D), bf16),
        V((M, D), bf16),
        V((S, D), bf16),
        V((2, 1, MH + SH), jnp.int32),
        V((D, D), bf16),
        V((D, D), bf16),
        V((D, D), bf16),
        V((D, D), bf16),
        V((D, FF), bf16),
        V((FF, D), bf16),
        V((D, R), bf16),
        V((R, D), bf16),
        V((R, D), bf16),
        V((R, 128), bf16),
        V((S, D), bf16),
        V((D, S), bf16),
        V((S, 128), f32),
        V((S, D), f32),
        V((S, D), bf16),
        V((S, D), bf16),
        V((D, S), bf16),
        V((D, S), bf16),
        V((S, 512), bf16),
        V((S, 512), bf16),
        V((S, D), f32),
        V((S, D), f32),
        V((D, S), bf16),
        V((S, 128), bf16),
        V((S, D), bf16),
        V((D, G), bf16),
        V((D // 2, G), bf16),
        V((3, D // 8, G), bf16),
        V((3, D // 32, G), bf16),
        V((4, 8, D), f32),
        V((7, 8, D), f32),
        dma((16,)),
        dma((10,)),
        dma((10,)),
        dma((units, 14)),
        dma((units, 14)),
        dma((7,)),
        dma((7,)),
        dma((units,)),
    ]
    for b in range(S // BLOCK):
        scratch.append(V((H, BLOCK, M + (b + 1) * BLOCK), bf16))
    shapes = (
        jax.ShapeDtypeStruct((2, SH, D), bf16),
        jax.ShapeDtypeStruct((2, SH, D), bf16),
        jax.ShapeDtypeStruct((D, G), bf16),
        jax.ShapeDtypeStruct((8, D), f32),
    )
    extra = {"collective_id": 1, "has_side_effects": True} if talk else {}
    return pl.pallas_call(
        functools.partial(layer_kernel, talk),
        out_shape=shapes,
        in_specs=[smem] * 3 + [hbm] * 4 + [vmem] * 4 + [hbm] * 6,
        out_specs=[hbm, hbm, hbm, vmem],
        scratch_shapes=scratch,
        compiler_params=pltpu.CompilerParams(
            vmem_limit_bytes=64 * 1024 * 1024 - 65536, **extra
        ),
        name="layer",
    )(
        counts, lengths, slopes, tokens, memory, ends, grad,
        gain1.reshape(1, D), shift1.reshape(1, D), gain2.reshape(1, D), shift2.reshape(1, D),
        wq, wk, wv, wo, w1, w2,
    )


def layer_norm(values, gain, shift):
    centred = values - jnp.mean(values, axis=-1, keepdims=True)
    spread = jnp.mean(centred * centred, axis=-1, keepdims=True)
    return centred * lax.rsqrt(spread + epsilon) * gain + shift


def block_scores(
    q_heads, key_block, q_ends, key_order, key_ends, q_index, head_slopes, score_scale
):
    scores = (
        jnp.einsum("qhd,khd->hqk", q_heads, key_block, preferred_element_type=jnp.float32)
        * score_scale
    )
    distance = (q_ends[:, None] - key_ends[None, :]).astype(jnp.float32)
    scores = scores - head_slopes[:, None, None] * distance[None]
    allowed = key_order[None, :] <= q_index[:, None]
    return (jnp.where(allowed[None], scores, -1e30), distance)


def spread_device(
    tokens,
    memory,
    segment_ends,
    memory_ends,
    segment_counts,
    memory_lengths,
    first_gain,
    first_shift,
    query_weight,
    key_weight,
    value_weight,
    out_weight,
    head_slopes,
    second_gain,
    second_shift,
    hidden_weight,
    output_weight,
    output_grad,
):
    seq_count, slot_count, model_width = tokens.shape
    mem_count = memory.shape[1]
    head_count = head_slopes.shape[0]
    head_dim = model_width // head_count
    score_scale = 1.0 / math.sqrt(head_dim)
    key_rows = mem_count + slot_count
    blocks = lax.axis_size("blk")
    my_block = lax.axis_index("blk")
    x_float = tokens.astype(jnp.float32)
    mem_float = memory.astype(jnp.float32)
    normed = layer_norm(x_float, first_gain, first_shift).astype(jnp.bfloat16)
    mem_normed = layer_norm(mem_float, first_gain, first_shift).astype(jnp.bfloat16)
    key_input = jnp.concatenate([mem_normed, normed], axis=1)
    query = jnp.einsum(
        "std,de->ste", normed, query_weight, preferred_element_type=jnp.float32
    ).astype(jnp.bfloat16)
    pair_weight = jnp.concatenate([key_weight, value_weight], axis=1)
    key_value = jnp.einsum(
        "srd,de->rse", key_input, pair_weight, preferred_element_type=jnp.float32
    ).astype(jnp.bfloat16)
    mem_index = my_block * mem_count + jnp.arange(mem_count, dtype=jnp.int32)
    slot_index = my_block * slot_count + jnp.arange(slot_count, dtype=jnp.int32)
    mem_order = jnp.where(
        mem_index[None, :] >= mem_count * blocks - memory_lengths[:, None], -1, far_order
    )
    slot_order = jnp.where(
        slot_index[None, :] < segment_counts[:, None], slot_index[None, :], far_order
    )
    key_meta = jnp.stack(
        [
            jnp.concatenate([mem_order, slot_order], axis=1),
            jnp.concatenate([memory_ends, segment_ends], axis=1),
        ]
    )
    all_pairs, all_meta = (
        lax.all_gather(key_value, "blk", axis=0, tiled=True),
        lax.all_gather(key_meta, "blk", axis=2, tiled=True),
    )
    query_heads = query.reshape(seq_count, slot_count, head_count, head_dim)

    def pick(seq_index):
        pair_rows = lax.dynamic_index_in_dim(all_pairs, seq_index, 1, keepdims=False)
        meta_rows = lax.dynamic_index_in_dim(all_meta, seq_index, 1, keepdims=False)
        key_heads = pair_rows[:, :model_width].reshape(-1, key_rows, head_count, head_dim)
        value_heads = pair_rows[:, model_width:].reshape(-1, key_rows, head_count, head_dim)
        return (
            key_heads,
            value_heads,
            meta_rows[0].reshape(-1, key_rows),
            meta_rows[1].reshape(-1, key_rows),
        )

    def attend(seq_index):
        key_heads, value_heads, key_order, key_ends = pick(seq_index)
        q_heads = lax.dynamic_index_in_dim(query_heads, seq_index, 0, keepdims=False)
        q_ends = lax.dynamic_index_in_dim(segment_ends, seq_index, 0, keepdims=False)

        def stats_step(running, pieces):
            scores = block_scores(
                q_heads,
                pieces[0],
                q_ends,
                pieces[1],
                pieces[2],
                slot_index,
                head_slopes,
                score_scale,
            )[0]
            running_max = jnp.maximum(running[0], jnp.max(scores, axis=-1))
            running_sum = running[1] * jnp.exp(running[0] - running_max) + jnp.sum(
                jnp.exp(scores - running_max[..., None]), axis=-1
            )
            return ((running_max, running_sum), None)

        start_max = jnp.full((head_count, slot_count), -jnp.inf, jnp.float32)
        (top_max, top_sum), _ = lax.scan(
            stats_step, (start_max, jnp.zeros_like(start_max)), (key_heads, key_order, key_ends)
        )
        log_total = top_max + jnp.log(top_sum)

        def out_step(summed, pieces):
            scores = block_scores(
                q_heads,
                pieces[0],
                q_ends,
                pieces[1],
                pieces[2],
                slot_index,
                head_slopes,
                score_scale,
            )[0]
            attn_probs = jnp.exp(scores - log_total[..., None]).astype(jnp.bfloat16)
            return (
                summed
                + jnp.einsum(
                    "hqk,khd->qhd", attn_probs, pieces[3], preferred_element_type=jnp.float32
                ),
                None,
            )

        start_out = jnp.zeros((slot_count, head_count, head_dim), jnp.float32)
        mixed_heads, _ = lax.scan(
            out_step, start_out, (key_heads, key_order, key_ends, value_heads)
        )
        return (mixed_heads, log_total)

    mixed_all, log_totals = lax.map(attend, jnp.arange(seq_count))
    mixed_low = mixed_all.reshape(seq_count, slot_count, model_width).astype(jnp.bfloat16)
    residual = x_float + jnp.einsum(
        "std,de->ste", mixed_low, out_weight, preferred_element_type=jnp.float32
    )
    second_low = layer_norm(residual, second_gain, second_shift).astype(jnp.bfloat16)
    hidden_pre = jnp.einsum(
        "std,df->stf", second_low, hidden_weight, preferred_element_type=jnp.float32
    )
    act_low = jax.nn.gelu(hidden_pre, approximate=False).astype(jnp.bfloat16)
    layer_out = (
        residual
        + jnp.einsum("stf,fd->std", act_low, output_weight, preferred_element_type=jnp.float32)
    ).astype(jnp.bfloat16)
    grad_output_w = jnp.einsum(
        "stf,std->fd", act_low, output_grad, preferred_element_type=jnp.float32
    )
    d_act = jnp.einsum(
        "std,fd->stf", output_grad, output_weight, preferred_element_type=jnp.float32
    )
    _, gelu_pull = jax.vjp(lambda inner: jax.nn.gelu(inner, approximate=False), hidden_pre)
    d_pre_low = gelu_pull(d_act)[0].astype(jnp.bfloat16)
    grad_hidden_w = jnp.einsum(
        "std,stf->df", second_low, d_pre_low, preferred_element_type=jnp.float32
    )
    d_second = jnp.einsum(
        "stf,df->std", d_pre_low, hidden_weight, preferred_element_type=jnp.float32
    )
    _, second_pull = jax.vjp(layer_norm, residual, second_gain, second_shift)
    d_resid_norm, grad_second_g, grad_second_b = second_pull(d_second)
    d_residual = d_resid_norm + output_grad.astype(jnp.float32)
    d_branch = d_residual.astype(jnp.bfloat16)
    grad_out_w = jnp.einsum("std,ste->de", mixed_low, d_branch, preferred_element_type=jnp.float32)
    d_mixed = jnp.einsum(
        "ste,de->std", d_branch, out_weight, preferred_element_type=jnp.float32
    ).astype(jnp.bfloat16)
    d_mixed_heads = d_mixed.reshape(seq_count, slot_count, head_count, head_dim)

    def query_side(seq_index):
        key_heads, value_heads, key_order, key_ends = pick(seq_index)
        q_heads = lax.dynamic_index_in_dim(query_heads, seq_index, 0, keepdims=False)
        q_ends = lax.dynamic_index_in_dim(segment_ends, seq_index, 0, keepdims=False)
        d_heads = lax.dynamic_index_in_dim(d_mixed_heads, seq_index, 0, keepdims=False)
        log_total = lax.dynamic_index_in_dim(log_totals, seq_index, 0, keepdims=False)

        def probs_of(key_block, order_block, ends_block, value_block):
            scores, distance = block_scores(
                q_heads,
                key_block,
                q_ends,
                order_block,
                ends_block,
                slot_index,
                head_slopes,
                score_scale,
            )
            attn_probs = jnp.exp(scores - log_total[..., None])
            d_probs = jnp.einsum(
                "qhd,khd->hqk", d_heads, value_block, preferred_element_type=jnp.float32
            )
            return (attn_probs, d_probs, distance)

        def delta_step(summed, pieces):
            attn_probs, d_probs, _ = probs_of(pieces[0], pieces[1], pieces[2], pieces[3])
            return (summed + jnp.sum(attn_probs * d_probs, axis=-1), None)

        delta_rows, _ = lax.scan(
            delta_step,
            jnp.zeros((head_count, slot_count), jnp.float32),
            (key_heads, key_order, key_ends, value_heads),
        )

        def grad_step(running, pieces):
            attn_probs, d_probs, distance = probs_of(pieces[0], pieces[1], pieces[2], pieces[3])
            d_scores = (attn_probs * (d_probs - delta_rows[..., None])).astype(jnp.bfloat16)
            d_query = running[0] + jnp.einsum(
                "hqk,khd->qhd", d_scores, pieces[0], preferred_element_type=jnp.float32
            )
            d_slopes = running[1] - jnp.sum(
                d_scores.astype(jnp.float32) * distance[None], axis=(1, 2)
            )
            return ((d_query, d_slopes), None)

        start_grads = (
            jnp.zeros((slot_count, head_count, head_dim), jnp.float32),
            jnp.zeros((head_count,), jnp.float32),
        )
        (d_query, d_slopes), _ = lax.scan(
            grad_step, start_grads, (key_heads, key_order, key_ends, value_heads)
        )
        return (d_query * score_scale, delta_rows, d_slopes)

    d_query_all, delta_all, slope_parts = lax.map(query_side, jnp.arange(seq_count))
    grad_slopes = jnp.sum(slope_parts, axis=0)
    d_query_low = d_query_all.reshape(seq_count, slot_count, model_width).astype(jnp.bfloat16)

    def pair_terms(
        pair_rows, order_block, ends_block, q_heads, q_ends, q_index, d_heads, log_total, delta_rows
    ):
        key_block = pair_rows[:, :model_width].reshape(key_rows, head_count, head_dim)
        value_block = pair_rows[:, model_width:].reshape(key_rows, head_count, head_dim)
        scores, _ = block_scores(
            q_heads, key_block, q_ends, order_block, ends_block, q_index, head_slopes, score_scale
        )
        attn_probs = jnp.exp(scores - log_total[..., None])
        d_probs = jnp.einsum(
            "qhd,khd->hqk", d_heads, value_block, preferred_element_type=jnp.float32
        )
        d_scores = (attn_probs * (d_probs - delta_rows[..., None])).astype(jnp.bfloat16)
        d_value = jnp.einsum(
            "hqk,qhd->khd",
            attn_probs.astype(jnp.bfloat16),
            d_heads,
            preferred_element_type=jnp.float32,
        )
        d_key = (
            jnp.einsum("hqk,qhd->khd", d_scores, q_heads, preferred_element_type=jnp.float32)
            * score_scale
        )
        return jnp.concatenate(
            [d_key.reshape(key_rows, model_width), d_value.reshape(key_rows, model_width)], axis=1
        )

    def one_block(block_index):
        offset = block_index * key_rows
        pair_block = lax.dynamic_slice_in_dim(all_pairs, offset, key_rows, 0)
        meta_block = lax.dynamic_slice_in_dim(all_meta, offset, key_rows, 2)
        return jax.vmap(pair_terms, in_axes=(1, 0, 0, 0, 0, None, 0, 0, 0), out_axes=1)(
            pair_block,
            meta_block[0],
            meta_block[1],
            query_heads,
            segment_ends,
            slot_index,
            d_mixed_heads,
            log_totals,
            delta_all,
        )

    pieces = lax.map(one_block, jnp.arange(lax.axis_size("blk") * key_rows // key_rows))
    pair_grads = lax.psum_scatter(
        pieces.reshape(lax.axis_size("blk") * key_rows, seq_count, 2 * model_width).astype(
            jnp.bfloat16
        ),
        "blk",
        scatter_dimension=0,
        tiled=True,
    )
    grad_pair_w = jnp.einsum(
        "srd,rse->de", key_input, pair_grads, preferred_element_type=jnp.float32
    )
    grad_key_w = grad_pair_w[:, :model_width]
    grad_value_w = grad_pair_w[:, model_width:]
    d_key_input = jnp.einsum(
        "rse,de->srd", pair_grads, pair_weight, preferred_element_type=jnp.float32
    )
    grad_query_w = jnp.einsum(
        "std,ste->de", normed, d_query_low, preferred_element_type=jnp.float32
    )
    d_normed = (
        jnp.einsum("ste,de->std", d_query_low, query_weight, preferred_element_type=jnp.float32)
        + d_key_input[:, mem_count:]
    )
    _, first_pull = jax.vjp(layer_norm, x_float, first_gain, first_shift)
    d_tokens, gain_slots, shift_slots = first_pull(d_normed)
    _, mem_pull = jax.vjp(
        lambda gain, shift: layer_norm(mem_float, gain, shift), first_gain, first_shift
    )
    gain_mem, shift_mem = mem_pull(d_key_input[:, :mem_count])
    input_grad = (d_tokens + d_residual).astype(jnp.bfloat16)
    grad_first_g = gain_slots + gain_mem
    grad_first_b = shift_slots + shift_mem
    summed = lax.psum(
        (
            grad_first_g,
            grad_first_b,
            grad_query_w,
            grad_key_w,
            grad_value_w,
            grad_out_w,
            grad_slopes,
            grad_second_g,
            grad_second_b,
            grad_hidden_w,
            grad_output_w,
        ),
        ("seq", "blk"),
    )
    return (
        layer_out,
        input_grad,
        summed[0],
        summed[1],
        summed[2],
        summed[3],
        summed[4],
        summed[5],
        summed[6],
        summed[7],
        summed[8],
        summed[9],
        summed[10],
    )


def widen_kernel(ga, gb, gc, layer_in, grad_in, small, *outs):
    gw1, gw2, go, gq, gk, gv, layer, grad, gain1, shift1, slopes, gain2, shift2 = outs
    half = ga.shape[1] // 2
    gw1[...] = ga[:, :half].astype(f32)
    gw2[...] = ga[:, half:].astype(f32).T
    go[...] = gb[...].astype(f32)
    for i, out in enumerate((gq, gk, gv)):
        out[...] = gc[:, i * 128 : (i + 1) * 128].astype(f32)
    layer[...] = layer_in[...]
    grad[...] = grad_in[...]

    @pl.when((pl.program_id(0) == 0) & (pl.program_id(1) == 0))
    def _():
        for i, out in enumerate((gain1, shift1, gain2, shift2)):
            out[...] = small[i : i + 1, :]
        slopes[...] = small[4:5, 0:128]


def widen(grads, layer, in_grad, small, D, FF):
    RB = D // 2
    LB = layer.shape[0] // 8
    out = [
        ((D, FF), (RB, 512), lambda c, r: (r, c)),
        ((FF, D), (512, RB), lambda c, r: (c, r)),
        ((D, D), (RB, 128), lambda c, r: (r, c)),
        ((D, D), (RB, 128), lambda c, r: (r, c)),
        ((D, D), (RB, 128), lambda c, r: (r, c)),
        ((D, D), (RB, 128), lambda c, r: (r, c)),
        ((8 * LB, D), (LB, D), lambda c, r: (2 * c + r, 0)),
        ((8 * LB, D), (LB, D), lambda c, r: (2 * c + r, 0)),
    ]
    kinds = [f32] * 6 + [bf16] * 2
    shapes = [jax.ShapeDtypeStruct(shape, kind) for (shape, _, _), kind in zip(out, kinds)]
    specs = [pl.BlockSpec(block, index) for _, block, index in out]
    for width in (D, D, 128, D, D):
        shapes.append(jax.ShapeDtypeStruct((1, width), f32))
        specs.append(pl.BlockSpec((1, width), lambda c, r: (0, 0)))
    go_at = 2 * FF // 128
    head_at = (2 * FF + D) // 384
    return pl.pallas_call(
        widen_kernel,
        grid=(4, 2),
        out_shape=shapes,
        in_specs=[
            pl.BlockSpec((RB, 1024), lambda c, r: (r, c)),
            pl.BlockSpec((RB, 128), lambda c, r: (r, go_at + c)),
            pl.BlockSpec((RB, 384), lambda c, r: (r, head_at + c)),
            pl.BlockSpec((LB, D), lambda c, r: (2 * c + r, 0)),
            pl.BlockSpec((LB, D), lambda c, r: (2 * c + r, 0)),
            pl.BlockSpec((8, D), lambda c, r: (0, 0)),
        ],
        out_specs=specs,
        compiler_params=pltpu.CompilerParams(vmem_limit_bytes=32 * 1024 * 1024),
        name="widen",
    )(grads, grads, grads, layer, in_grad, small)


def whole_device(*args):
    tokens, memory, segment_ends, memory_ends, counts, lengths = args[:6]
    params = args[6:17]
    output_grad = args[17]
    D = tokens.shape[2]
    FF = params[9].shape[1]
    H = params[6].shape[0]
    ends = jnp.concatenate([memory_ends, segment_ends], axis=1)[:, None]
    layer, in_grad, grads, small = layer_call(
        counts, lengths, tokens, memory, ends, output_grad, params
    )
    gw1, gw2, go, gq, gk, gv, layer, in_grad, *rows = widen(
        grads, layer.reshape(-1, D), in_grad.reshape(-1, D), small, D, FF
    )
    gain1, shift1, slopes, gain2, shift2 = (row[0] for row in rows)
    return (
        layer.reshape(tokens.shape),
        in_grad.reshape(tokens.shape),
        gain1,
        shift1,
        gq,
        gk,
        gv,
        go,
        slopes[:H],
        gain2,
        shift2,
        gw1,
        gw2,
    )


def per_device(*args):
    whole = args[0].shape[0] == lax.axis_size("blk") == 2 and lax.axis_size("seq") == 16
    if whole:
        return whole_device(*args)
    return spread_device(*args)


def solution(mesh):
    placed = (
        P("seq", "blk", None),
        P("seq", "blk", None),
        P("seq", "blk"),
        P("seq", "blk"),
        P("seq"),
        P("seq"),
        P(),
        P(),
        P(),
        P(),
        P(),
        P(),
        P(),
        P(),
        P(),
        P(),
        P(),
        P("seq", "blk", None),
    )
    return jax.shard_map(
        per_device,
        mesh=mesh,
        in_specs=placed,
        out_specs=(
            P("seq", "blk", None),
            P("seq", "blk", None),
            P(),
            P(),
            P(),
            P(),
            P(),
            P(),
            P(),
            P(),
            P(),
            P(),
            P(),
        ),
        check_vma=False,
    )
```

```python
import functools
import math

import jax
import jax.numpy as jnp
from jax import lax
from jax.experimental import pallas as pl
from jax.experimental.pallas import tpu as pltpu
from jax.sharding import PartitionSpec as P

epsilon = 1e-05
far_order = 1073741824
f32 = jnp.float32
bf16 = jnp.bfloat16
BLOCK = 256
LOG2E = 1.4426950408889634
LN2 = 0.6931471805599453


def dot_nn(left, right):
    return lax.dot_general(left, right, (((1,), (0,)), ((), ())), preferred_element_type=f32)


def dot_nt(left, right):
    return lax.dot_general(left, right, (((1,), (1,)), ((), ())), preferred_element_type=f32)


def norm_stats(values):
    centred = values - jnp.mean(values, axis=-1, keepdims=True)
    spread = jnp.mean(centred * centred, axis=-1, keepdims=True)
    scale = lax.rsqrt(spread + epsilon)
    return centred * scale, scale


def norm_back(unit, scale, grad_unit):
    mean_grad = jnp.mean(grad_unit, axis=-1, keepdims=True)
    mean_prod = jnp.mean(grad_unit * unit, axis=-1, keepdims=True)
    return (grad_unit - mean_grad - unit * mean_prod) * scale


def pieces_of(value, count):
    out = []
    for _ in range(count):
        part = value.astype(bf16).astype(f32)
        out.append(part)
        value = value - part
    return out


ERFC_P = 0.4
ERFC_C = (0.22567586600780487, 0.2256695181131363, 0.2078438550233841, 0.16853390634059906, 0.1414608359336853, -0.005667657125741243, 0.16915477812290192, -0.18294358253479004, 0.050272583961486816)


def gelu_both(x):
    cdf = 0.5 * lax.erf(x * math.sqrt(0.5)) + 0.5
    ex = jnp.exp2((x * x) * (-0.5 * LOG2E))
    return x * cdf, cdf + x * (ex * (1.0 / math.sqrt(2.0 * math.pi)))


def col_sum8(value):
    return jnp.sum(value.reshape(-1, 8, value.shape[-1]), axis=0)


def flip(bit):
    return 1 - bit


def layer_kernel(
    talk,
    counts_ref,
    lengths_ref,
    slopes_ref,
    tokens_ref,
    memory_ref,
    ends_ref,
    grad_ref,
    gain1_ref,
    shift1_ref,
    gain2_ref,
    shift2_ref,
    wq_hbm,
    wk_hbm,
    wv_hbm,
    wo_hbm,
    w1_hbm,
    w2_hbm,
    layer_hbm,
    ingrad_hbm,
    grads_hbm,
    small_ref,
    x_ref,
    mem_ref,
    og_ref,
    ends_s,
    wq_ref,
    wk_ref,
    wv_ref,
    wo_ref,
    w1_ref,
    w2_ref,
    keyint,
    k_s,
    v_s,
    kx,
    q_s,
    qt,
    rl_s,
    o_s,
    mixed,
    second_s,
    secondt,
    ogt,
    act_s,
    dpre_s,
    acc_s,
    dres,
    dolt,
    delta_s,
    g_s,
    rc_s,
    r1_s,
    sm_own,
    sm_in,
    load_sem,
    ex_send,
    ex_recv,
    ar_send,
    ar_recv,
    sm_send,
    sm_recv,
    out_sem,
    *probs,
):
    S, D = x_ref.shape
    M = mem_ref.shape[0]
    R = M + S
    FF = w1_ref.shape[1]
    H = slopes_ref.shape[0]
    DH = D // H
    HP = H // 2
    NB = S // BLOCK
    MB = M // BLOCK
    SH = S // 2
    MH = M // 2
    KC = 512
    CH = 512
    NC = FF // CH

    if talk:
        seq = lax.axis_index("seq")
        blk = lax.axis_index("blk")
    else:
        seq = 0
        blk = 0
    core = seq % 2
    why = (seq // 2) % 2
    zed = seq // 4

    def at(z=None, y=None, c=None, x=None):
        z = zed if z is None else z
        y = why if y is None else y
        c = core if c is None else c
        return {"seq": z * 4 + y * 2 + c, "blk": blk if x is None else x}

    sibling = at(c=flip(core))
    partner = at(x=flip(blk))
    z_to = [zed + 1 - 2 * (zed % 2), (zed + 2) % 4, 3 - zed]
    z_peers = [(at(z=z), z) for z in z_to]
    plane = blk * 2 + why
    xy_peers = [
        (at(y=flip(why)), blk * 2 + flip(why)),
        (at(x=flip(blk)), flip(blk) * 2 + why),
        (at(x=flip(blk), y=flip(why)), flip(blk) * 2 + flip(why)),
    ]

    def remote(src, dst, send, recv, device):
        return pltpu.make_async_remote_copy(
            src_ref=src,
            dst_ref=dst,
            send_sem=send,
            recv_sem=recv,
            device_id=device,
            device_id_type=pl.DeviceIdType.MESH,
        )

    other = 1 - blk

    def half_rows(half, size):
        return pl.ds(pl.multiple_of(half * size, BLOCK), size)

    def slot_piece(part, index, half, i):
        src = tokens_ref if part == 0 else grad_ref
        dst = x_ref if part == 0 else og_ref
        rows = pl.ds(pl.multiple_of(half * SH + i * BLOCK, BLOCK), BLOCK)
        return src.at[index, i * BLOCK : (i + 1) * BLOCK, :], dst.at[rows, :]

    nslot = SH // BLOCK
    loads = [
        (memory_ref.at[blk], mem_ref.at[half_rows(blk, MH), :]),
        (ends_ref.at[blk], ends_s.at[blk]),
        (wk_hbm, wk_ref),
        (wv_hbm, wv_ref),
        (wq_hbm, wq_ref),
    ]
    loads += [slot_piece(0, blk, blk, i) for i in range(nslot)]
    n_first = len(loads)
    loads += [(wo_hbm, wo_ref), (w1_hbm, w1_ref), (w2_hbm, w2_ref)]
    loads += [slot_piece(1, blk, blk, i) for i in range(nslot)]
    copies = [
        pltpu.make_async_copy(src, dst, load_sem.at[i]) for i, (src, dst) in enumerate(loads)
    ]
    sends = [
        (memory_ref.at[other], mem_ref.at[half_rows(blk, MH), :]),
        (ends_ref.at[other], ends_s.at[blk]),
    ]
    sends += [slot_piece(0, other, blk, i) for i in range(nslot)]
    sends += [slot_piece(1, other, blk, i) for i in range(nslot)]
    if talk:
        exchange = [
            remote(src, dst, ex_send.at[i], ex_recv.at[i], partner)
            for i, (src, dst) in enumerate(sends)
        ]
    else:
        local = [
            (memory_ref.at[other], mem_ref.at[half_rows(other, MH), :]),
            (ends_ref.at[other], ends_s.at[other]),
        ]
        local += [slot_piece(0, other, other, i) for i in range(nslot)]
        local += [slot_piece(1, other, other, i) for i in range(nslot)]
        exchange = [
            pltpu.make_async_copy(src, dst, ex_send.at[i]) for i, (src, dst) in enumerate(local)
        ]
    for copy in copies[:n_first]:
        copy.start()
    if talk:
        barrier = pltpu.get_barrier_semaphore()
        greet = [sibling] + [d for d, _ in z_peers] + [d for d, _ in xy_peers]
        for device in greet:
            pl.semaphore_signal(
                barrier, inc=1, device_id=device, device_id_type=pl.DeviceIdType.MESH
            )
        pl.semaphore_wait(barrier, len(greet))
    for copy in exchange:
        copy.start()
    for copy in copies[n_first:]:
        copy.start()

    def arrive(i):
        if talk:
            exchange[i].wait_recv()
        else:
            exchange[i].wait()

    directions = {
        "x": (blk, [(partner, other)]),
        "y": (why, [(at(y=flip(why)), flip(why))]),
        "a": (zed % 2, [(z_peers[0][0], 1 - zed % 2)]),
        "b": (zed // 2, [(z_peers[1][0], 1 - zed // 2)]),
        "z": (zed, z_peers),
        "p": (plane, xy_peers),
    }
    units = []
    for c in range(2 * NC):
        units.append((c * CH, CH))
    units.append((2 * FF, D))
    for p in range(HP):
        units.append((2 * FF + D + p * 384, 384))
    HALF = D // 2

    def rows_at(start, size):
        return pl.ds(pl.multiple_of(start, 16), size)

    def unit_rounds(u):
        start, size, place = core * HALF, HALF, 0
        rounds = []
        for name in ORDERS[u]:
            mine, peers = directions[name]
            piece = size // (len(peers) + 1)
            rounds.append((start, piece, mine, peers, place))
            place += piece * len(peers)
            start, size = start + mine * piece, piece
        return rounds, start, size

    def unit_copies(u, step):
        col, width = units[u]
        cols = slice(col, col + width)
        rounds, start, size = unit_rounds(u)
        n = len(rounds)
        out = []
        if step == 0:
            rows = rows_at((1 - core) * HALF, HALF)
            out.append((g_s.at[rows, cols], rc_s.at[:, cols], sibling))
        elif step <= n:
            begin, piece, _, peers, place = rounds[step - 1]
            for d, (device, index) in enumerate(peers):
                rows = rows_at(begin + index * piece, piece)
                here = slice(place + d * piece, place + (d + 1) * piece)
                out.append((g_s.at[rows, cols], r1_s.at[here, cols], device))
        elif step <= 2 * n:
            level = 2 * n - step
            begin, piece, mine, peers, _ = rounds[level]
            rows = rows_at(begin + mine * piece, piece)
            src = g_s if level == n - 1 else grads_hbm
            for device, _ in peers:
                out.append((src.at[rows, cols], grads_hbm.at[rows, cols], device))
        else:
            rows = rows_at(core * HALF, HALF)
            out.append((grads_hbm.at[rows, cols], grads_hbm.at[rows, cols], sibling))
        first = 0
        for earlier in range(step):
            if 1 <= earlier <= n:
                first += len(rounds[earlier - 1][3])
            elif n < earlier <= 2 * n:
                first += len(rounds[2 * n - earlier][3])
            else:
                first += 1
        return [
            remote(src, dst, ar_send.at[u, first + k], ar_recv.at[u, first + k], device)
            for k, (src, dst, device) in enumerate(out)
        ]

    def unit_add(u, step):
        col, width = units[u]
        cols = slice(col, col + width)
        rounds, _, _ = unit_rounds(u)
        if step == 0:
            begin, piece, places, buffer = core * HALF, HALF, [0], rc_s
        else:
            begin, piece, mine, peers, place = rounds[step - 1]
            begin = begin + mine * piece
            places, buffer = [place + d * piece for d in range(len(peers))], r1_s
        block = min(piece, 64)

        def add(i, _):
            rows = rows_at(begin + i * block, block)
            total = g_s[rows, cols].astype(f32)
            for place in places:
                total = total + buffer[rows_at(place + i * block, block), cols].astype(f32)
            g_s[rows, cols] = total.astype(bf16)
            return 0

        if piece == block:
            add(0, 0)
        else:
            lax.fori_loop(0, piece // block, add, 0)

    def unit_out(u):
        col, width = units[u]
        cols = slice(col, col + width)
        _, start, size = unit_rounds(u)
        rows = rows_at(start, size) if talk else slice(0, D)
        return pltpu.make_async_copy(g_s.at[rows, cols], grads_hbm.at[rows, cols], out_sem.at[u])

    def advance(u, step):
        if not talk:
            return
        n = len(ORDERS[u])
        if step > 0:
            for copy in unit_copies(u, step - 1):
                copy.wait()
            if step - 1 <= n:
                unit_add(u, step - 1)
        if step == n + 1:
            unit_out(u).start()
        if step == n + 2:
            unit_out(u).wait()
        if step < 2 * n + 2:
            for copy in unit_copies(u, step):
                copy.start()

    def ticks(kind, index):
        moves = SCHEDULE.get((kind, index), ())
        if not moves:
            return

        @pl.when(seq >= 0)
        def _():
            for u, step in moves:
                if u < 0:
                    layer_copies[1 + step].start()
                else:
                    advance(u, step)

    def ticks_in_loop(kind, index, count, base=0):
        for k in range(count):
            if (kind, base + k) in SCHEDULE:

                @pl.when(index == k)
                def _():
                    ticks(kind, base + k)

    gain1 = gain1_ref[...]
    shift1 = shift1_ref[...]
    gain2 = gain2_ref[...]
    shift2 = shift2_ref[...]
    count = counts_ref[blk]
    length = lengths_ref[blk]

    def give(result, hbm, k, pieces):
        own = pltpu.make_async_copy(result.at[half_rows(blk, SH), :], hbm.at[blk], load_sem.at[k])
        moves = [own]
        size = SH // pieces
        for i in range(pieces):
            theirs = result.at[pl.ds(pl.multiple_of(other * SH + i * size, size), size), :]
            rows = slice(i * size, (i + 1) * size)
            sem = len(sends) + 4 * k + i
            if talk:
                there = hbm.at[blk, rows, :]
                moves.append(remote(theirs, there, ex_send.at[sem], ex_recv.at[sem], partner))
            else:
                moves.append(
                    pltpu.make_async_copy(theirs, hbm.at[other, rows, :], ex_send.at[sem])
                )
        return moves

    layer_copies = give(second_s, layer_hbm, 0, 4)
    ingrad_copies = give(second_s, ingrad_hbm, 1, nslot)

    def project(normed, key_rows):
        keyint[:, key_rows] = normed.T
        k_s[key_rows, :] = dot_nn(normed, wk_ref[...]).astype(bf16)
        v_s[key_rows, :] = dot_nn(normed, wv_ref[...]).astype(bf16)

    def norm_mem(b):
        rows = pl.ds(pl.multiple_of(b * BLOCK, BLOCK), BLOCK)
        unit, _ = norm_stats(mem_ref[rows, :].astype(f32))
        project((unit * gain1 + shift1).astype(bf16), rows)

    def norm_slot(b):
        rows = pl.ds(pl.multiple_of(b * BLOCK, BLOCK), BLOCK)
        key_rows = pl.ds(pl.multiple_of(b * BLOCK + M, BLOCK), BLOCK)
        unit, _ = norm_stats(x_ref[rows, :].astype(f32))
        normed = (unit * gain1 + shift1).astype(bf16)
        project(normed, key_rows)
        query = (dot_nn(normed, wq_ref[...]) * (LOG2E / math.sqrt(DH))).astype(bf16)
        q_s[rows, :] = query
        qt[:, rows] = query.T

    for copy in copies[:n_first]:
        copy.wait()
    mh = MH // BLOCK
    lax.fori_loop(0, mh, lambda i, _: (norm_mem(blk * mh + i), 0)[1], 0)
    lax.fori_loop(0, nslot, lambda i, _: (norm_slot(blk * nslot + i), 0)[1], 0)
    arrive(0)
    lax.fori_loop(0, mh, lambda i, _: (norm_mem(other * mh + i), 0)[1], 0)
    arrive(1)

    lane = lax.broadcasted_iota(jnp.int32, (128, 128), 1)
    row = lax.broadcasted_iota(jnp.int32, (128, 128), 0)

    def end_row(start, size):
        if start < M:
            half, off = start // MH, start % MH
        else:
            half, off = (start - M) // SH, MH + (start - M) % SH
        return ends_s[half, :, off : off + size].astype(f32)

    for r in range(R // 128):
        end_col = jnp.broadcast_to(end_row(r * 128, 128), (128, 128)).T
        high = jnp.floor(end_col * (1.0 / 256.0)) * 256.0
        index = row + r * 128
        if r * 128 < M:
            valid = index >= M - length
        else:
            valid = index - M < count
        bias = jnp.where(valid, 0.0, -1e30)
        extra = jnp.where(lane < 3, high, jnp.where(lane < 6, end_col - high, bias))
        extra = jnp.where(lane == 7, 1.0, jnp.where(lane > 7, 0.0, extra))
        kx[r * 128 : (r + 1) * 128, :] = extra.astype(bf16)

    for i in range(nslot):
        arrive(2 + i)
        norm_slot(other * nslot + i)

    lane_q = lax.broadcasted_iota(jnp.int32, (BLOCK, 128), 1)
    first_half = lane_q < DH
    lane_row = lax.broadcasted_iota(jnp.int32, (1, 128), 1)

    def key_chunks(b):
        end = M + (b + 1) * BLOCK
        return [(start, min(KC, end - start)) for start in range(0, end, KC)]

    def key_full(lanes, start, size):
        return jnp.concatenate(
            [k_s[start : start + size, lanes], kx[start : start + size, :]], axis=1
        )

    def value_full(lanes, start, size):
        return jnp.concatenate(
            [v_s[start : start + size, lanes], jnp.ones((size, 128), bf16)], axis=1
        )

    def query_extra(head):
        slope = jnp.full((1, 128), slopes_ref[head] * LOG2E, f32)
        s1, s2, s3 = pieces_of(slope, 3)
        where = jnp.where(lane_row >= 3, lane_row - 3, lane_row)
        out = jnp.where(where == 0, s1, jnp.where(where == 1, s2, s3))
        return jnp.where(lane_row < 6, out, jnp.where(lane_row == 6, 1.0, 0.0))

    rl_s[...] = jnp.zeros_like(rl_s)
    for b in range(NB):
        rows = slice(b * BLOCK, (b + 1) * BLOCK)
        e_ref = probs[b]

        def fwd_pair(p, _):
            lanes = slice(p * 128, (p + 1) * 128)
            q_pair = q_s[rows, lanes]
            outs = []
            for half in range(2):
                keep = first_half if half == 0 else jnp.logical_not(first_half)
                q_half = jnp.where(keep, q_pair, jnp.zeros_like(q_pair))
                extra = jnp.broadcast_to(query_extra(2 * p + half), (BLOCK, 128)).astype(bf16)
                q_full = jnp.concatenate([q_half, extra], axis=1)
                chunks = key_chunks(b)
                scores = [dot_nt(q_full, key_full(lanes, k0, kn)) for k0, kn in chunks]
                below = lax.broadcasted_iota(
                    jnp.int32, (BLOCK, BLOCK), 1
                ) <= lax.broadcasted_iota(jnp.int32, (BLOCK, BLOCK), 0)
                last = scores[-1]
                cut = last.shape[1] - BLOCK
                diag = jnp.where(below, last[:, cut:], -1e30)
                scores[-1] = jnp.concatenate([last[:, :cut], diag], axis=1) if cut else diag
                top = scores[-1][:, 0:128]
                for part in scores:
                    for k in range(0, part.shape[1], 128):
                        top = jnp.maximum(top, part[:, k : k + 128])
                top = jnp.max(top, axis=1, keepdims=True)
                both = jnp.zeros((BLOCK, 256), f32)
                for part, (k0, kn) in zip(scores, chunks):
                    e = jnp.exp2(part - top).astype(bf16)
                    e_ref[2 * p + half, :, k0 : k0 + kn] = e
                    both = both + dot_nn(e, value_full(lanes, k0, kn))
                outs.append((both[:, 0:128], 1.0 / both[:, 128:256]))
            rl = jnp.where(first_half, outs[0][1], outs[1][1])
            o = jnp.where(first_half, outs[0][0], outs[1][0]) * rl
            packed = jnp.where(lane_q == 2 * p, outs[0][1], rl_s[rows, :])
            rl_s[rows, :] = jnp.where(lane_q == 2 * p + 1, outs[1][1], packed)
            o_s[rows, lanes] = o
            mixed[rows, lanes] = o.astype(bf16)
            return 0

        for p in range(HP):
            fwd_pair(p, 0)

    for copy in copies[n_first:]:
        copy.wait()
    for i in range(nslot):
        arrive(2 + nslot + i)

    def residual_of(rows):
        return x_ref[rows, :].astype(f32) + dot_nn(mixed[rows, :], wo_ref[...])

    def feed_prep(b, _):
        rows = slice(b * BLOCK, (b + 1) * BLOCK)
        residual = residual_of(rows)
        unit, _ = norm_stats(residual)
        second = (unit * gain2 + shift2).astype(bf16)
        second_s[rows, :] = second
        secondt[:, rows] = second.T
        ogt[:, rows] = og_ref[rows, :].T
        acc_s[rows, :] = residual
        return 0

    for b in range(NB):
        feed_prep(b, 0)
    for c in range(NC):
        cols = slice(c * CH, (c + 1) * CH)

        def feed(b, _):
            rows = slice(b * BLOCK, (b + 1) * BLOCK)
            hidden = dot_nn(second_s[rows, :], w1_ref[:, cols])
            d_act = dot_nt(og_ref[rows, :], w2_ref[cols, :])
            act, slope = gelu_both(hidden)
            act = act.astype(bf16)
            d_pre = (d_act * slope).astype(bf16)
            act_s[rows, :] = act
            dpre_s[rows, :] = d_pre
            acc_s[rows, :] += dot_nn(act, w2_ref[cols, :])
            d_second = dot_nt(d_pre, w1_ref[:, cols])
            dres[rows, :] = d_second if c == 0 else dres[rows, :] + d_second
            ticks("feed", c * NB + b)
            return 0

        for b in range(NB):
            feed(b, 0)
        base = c * 2 * CH
        for r in range(D // BLOCK):
            rows = slice(r * BLOCK, (r + 1) * BLOCK)
            g_s[rows, base : base + CH] = dot_nn(secondt[rows, :], dpre_s[...]).astype(bf16)
            g_s[rows, base + CH : base + 2 * CH] = dot_nn(ogt[rows, :], act_s[...]).astype(bf16)
        ticks("chunk", c)

    def feed_post(b, sums):
        rows = slice(b * BLOCK, (b + 1) * BLOCK)
        unit, scale = norm_stats(residual_of(rows))
        d_second = dres[rows, :]
        d_residual = og_ref[rows, :].astype(f32) + norm_back(unit, scale, d_second * gain2)
        dres[rows, :] = d_residual
        d_branch = d_residual.astype(bf16)
        act_s[rows, :] = d_branch
        secondt[:, rows] = mixed[rows, :].T
        d_mixed = dot_nt(d_branch, wo_ref[...]).astype(bf16).astype(f32)
        rl_b = rl_s[rows, :]
        rl_wide = []
        for p in range(HP):
            first = jnp.broadcast_to(rl_b[:, 2 * p : 2 * p + 1], (BLOCK, 128))
            second = jnp.broadcast_to(rl_b[:, 2 * p + 1 : 2 * p + 2], (BLOCK, 128))
            rl_wide.append(jnp.where(first_half, first, second))
        dol_b = (d_mixed * jnp.concatenate(rl_wide, axis=1)).astype(bf16)
        mixed[rows, :] = dol_b
        dolt[:, rows] = dol_b.T
        prod = dol_b.astype(f32) * o_s[rows, :]
        packed = jnp.zeros((BLOCK, 128), f32)
        for head in range(H):
            part = prod[:, (head // 2) * 128 : (head // 2 + 1) * 128]
            keep = first_half if head % 2 == 0 else jnp.logical_not(first_half)
            delta = jnp.sum(jnp.where(keep, part, 0.0), axis=1, keepdims=True)
            for k, piece in enumerate(pieces_of(jnp.broadcast_to(-delta, (BLOCK, 128)), 3)):
                packed = jnp.where(lane_q == 4 * head + k, piece, packed)
        delta_s[rows, :] = packed.astype(bf16)
        ticks("post", b)
        return sums[0] + col_sum8(d_second * unit), sums[1] + col_sum8(d_second)

    def feed_out(b, _):
        rows = pl.ds(pl.multiple_of(b * BLOCK, BLOCK), BLOCK)
        second_s[rows, :] = acc_s[rows, :].astype(bf16)
        return 0

    lax.fori_loop(0, NB, feed_out, 0)
    layer_copies[0].start()
    zero8 = jnp.zeros((8, D), f32)
    gain2_sum, shift2_sum = (zero8, zero8)
    for b in range(NB):
        gain2_sum, shift2_sum = feed_post(b, (gain2_sum, shift2_sum))
    for r in range(D // BLOCK):
        rows = slice(r * BLOCK, (r + 1) * BLOCK)
        g_s[rows, 2 * FF : 2 * FF + D] = dot_nn(secondt[rows, :], act_s[...]).astype(bf16)

    ticks("go", 0)

    small_ref[...] = jnp.zeros_like(small_ref)
    NK = R // KC
    lane_w = (lane_q == 0) | (lane_q == 3)

    def bwd_pair(p, slope_sums):
        lanes = pl.ds(pl.multiple_of(p * 128, 128), 128)
        acc_s[0 : 2 * NK * 128, :] = jnp.zeros((2 * NK * 128, KC), f32)
        for b in range(NB):
            rows = slice(b * BLOCK, (b + 1) * BLOCK)
            e_ref = probs[b]
            end_b = jnp.broadcast_to(end_row(M + b * BLOCK, BLOCK), (128, BLOCK)).T
            weight = jnp.where(lane_w, 1.0, jnp.where(lane_q == 7, -end_b, 0.0))
            dol_pair = mixed[rows, lanes]
            outs = []
            for half in range(2):
                head = 2 * p + half
                keep = first_half if half == 0 else jnp.logical_not(first_half)
                d_half = jnp.where(keep, dol_pair, jnp.zeros_like(dol_pair))
                delta = delta_s[rows, :]
                delta = jnp.where(lane_q // 4 == head, delta, jnp.zeros_like(delta))
                d_full = jnp.concatenate([d_half, delta], axis=1)
                hrows = pl.ds(pl.multiple_of(head * DH, DH), DH)
                q_t = qt[hrows, rows]
                d_t = dolt[hrows, rows]
                dqx = jnp.zeros((BLOCK, 256), f32)
                for j, (k0, kn) in enumerate(key_chunks(b)):
                    e = e_ref[head, :, k0 : k0 + kn]
                    ds = (dot_nt(d_full, value_full(lanes, k0, kn)) * e.astype(f32)).astype(bf16)
                    dqx = dqx + dot_nn(ds, key_full(lanes, k0, kn))
                    at_k = j * 128 + half * DH
                    acc_s[at_k : at_k + DH, 0:kn] += dot_nn(q_t, ds)
                    at_v = (NK + j) * 128 + half * DH
                    acc_s[at_v : at_v + DH, 0:kn] += dot_nn(d_t, e)
                outs.append(dqx[:, 0:128])
                tail = jnp.sum(dqx[:, 128:256] * weight, axis=0, keepdims=True)
                here = lax.broadcasted_iota(jnp.int32, (8, 128), 0) == head
                slope_sums = slope_sums + jnp.where(here, tail, 0.0)
            dq = jnp.where(first_half, outs[0], outs[1]) * (1.0 / math.sqrt(DH))
            q_s[rows, lanes] = dq.astype(bf16)
            for k in range(HP):
                if ("bwd", k * NB + b) in SCHEDULE:

                    @pl.when(p == k)
                    def _():
                        ticks("bwd", k * NB + b)

        for j in range(NK):
            dk = (acc_s[j * 128 : (j + 1) * 128, :] * LN2).astype(bf16).T
            k_s[j * KC : (j + 1) * KC, lanes] = dk
            dv = acc_s[(NK + j) * 128 : (NK + j + 1) * 128, :].astype(bf16).T
            v_s[j * KC : (j + 1) * KC, lanes] = dv
        for r in range(D // BLOCK):
            rows = slice(r * BLOCK, (r + 1) * BLOCK)
            gq = dot_nn(keyint[rows, M:], q_s[:, lanes]).astype(bf16)
            pair = jnp.concatenate([k_s[:, lanes], v_s[:, lanes]], axis=1)
            gkv = dot_nn(keyint[rows, :], pair).astype(bf16)
            col = 2 * FF + D + p * 384
            g_s[rows, pl.ds(pl.multiple_of(col, 128), 128)] = gq
            g_s[rows, pl.ds(pl.multiple_of(col + 128, 128), 256)] = gkv
        ticks_in_loop("pair", p, HP)
        return slope_sums

    slope_sums = lax.fori_loop(0, HP, bwd_pair, jnp.zeros((8, 128), f32))

    def key_back(key_rows):
        return dot_nt(k_s[key_rows, :], wk_ref[...]) + dot_nt(v_s[key_rows, :], wv_ref[...])

    def mem_back(b, sums):
        rows = pl.ds(pl.multiple_of(b * BLOCK, BLOCK), BLOCK)
        unit, _ = norm_stats(mem_ref[rows, :].astype(f32))
        d_rows = key_back(rows)
        return sums[0] + col_sum8(d_rows * unit), sums[1] + col_sum8(d_rows)

    def slot_back(b, sums):
        rows = pl.ds(pl.multiple_of(b * BLOCK, BLOCK), BLOCK)
        key_rows = pl.ds(pl.multiple_of(b * BLOCK + M, BLOCK), BLOCK)
        unit, scale = norm_stats(x_ref[rows, :].astype(f32))
        d_rows = key_back(key_rows) + dot_nt(q_s[rows, :], wq_ref[...])
        grad = norm_back(unit, scale, d_rows * gain1) + dres[rows, :]
        second_s[rows, :] = grad.astype(bf16)
        return sums[0] + col_sum8(d_rows * unit), sums[1] + col_sum8(d_rows)

    layer_copies[0].wait()
    for copy in layer_copies[1:]:
        if talk:
            copy.wait_send()
        else:
            copy.wait()
    sums = (zero8, zero8)
    for i in range(nslot):
        sums = slot_back(other * nslot + i, sums)
        ingrad_copies[1 + i].start()
        ticks("tail", i)
    for i in range(MB):
        sums = mem_back(i, sums)
        ticks("tail", nslot + i)
    for i in range(nslot):
        sums = slot_back(blk * nslot + i, sums)
        ticks("tail", nslot + MB + i)
    ingrad_copies[0].start()
    gain1_sum, shift1_sum = sums
    sm_own[0] = jnp.zeros_like(sm_own[0])
    for k, part in enumerate((gain1_sum, shift1_sum, gain2_sum, shift2_sum)):
        sm_own[0, k : k + 1, :] = jnp.sum(part, axis=0, keepdims=True)
    total = jnp.broadcast_to(jnp.sum(slope_sums, axis=1, keepdims=True), (8, 128))
    sm_own[0, 4:5, 0:128] = jnp.sum(
        jnp.where(lax.broadcasted_iota(jnp.int32, (8, 128), 0)
                  == lax.broadcasted_iota(jnp.int32, (8, 128), 1), total, 0.0),
        axis=0, keepdims=True)

    if talk:
        k = 0
        for level, devices in enumerate(
            ([sibling], [d for d, _ in z_peers], [d for d, _ in xy_peers])
        ):
            hops = []
            for device in devices:
                hops.append(
                    remote(sm_own.at[level], sm_in.at[k], sm_send.at[k], sm_recv.at[k], device)
                )
                k += 1
            for hop in hops:
                hop.start()
            ticks("small", level)
            total = sm_own[level]
            for i, hop in enumerate(hops):
                hop.wait()
                total = total + sm_in[k - len(hops) + i]
            sm_own[level + 1] = total
        small_ref[...] = sm_own[3]
    else:
        for level in range(3):
            ticks("small", level)
        small_ref[...] = sm_own[0]
    for i in range(10):
        ticks("last", i)
    ingrad_copies[0].wait()
    if not talk:
        for u in range(len(units)):
            unit_out(u).start()
            unit_out(u).wait()
    if talk:
        for copy in exchange:
            copy.wait_send()
        for copy in layer_copies[1:]:
            copy.wait_recv()
    for copy in ingrad_copies[1:]:
        copy.wait()


ORDERS = ('yxab', 'yzx', 'yaxb', 'axyb', 'pz', 'yzx', 'xyab', 'aybx', 'yxz', 'ayxb', 'yxz', 'pz', 'zp')
SCHEDULE = {
    ('chunk', 0): ((0, 0), (1, 0)),
    ('chunk', 1): ((3, 0), (0, 1), (2, 0)),
    ('feed', 9): ((1, 1),),
    ('chunk', 2): ((3, 1), (5, 0), (4, 0)),
    ('feed', 13): ((2, 1),),
    ('feed', 15): ((0, 2),),
    ('chunk', 3): ((5, 1), (7, 0), (6, 0)),
    ('post', 0): ((4, 1),),
    ('post', 1): ((1, 2),),
    ('post', 2): ((3, 2),),
    ('go', 0): ((0, 3), (7, 1), (8, 0)),
    ('bwd', 0): ((-1, 0), (2, 2), (6, 1)),
    ('bwd', 2): ((0, 4), (5, 2), (8, 1)),
    ('bwd', 3): ((-1, 1), (3, 3), (1, 3)),
    ('pair', 0): ((9, 0), (7, 2), (4, 2)),
    ('bwd', 4): ((2, 3),),
    ('bwd', 5): ((-1, 2), (0, 5), (8, 2)),
    ('bwd', 6): ((9, 1), (3, 4), (6, 2)),
    ('bwd', 7): ((5, 3), (7, 3)),
    ('pair', 1): ((-1, 3), (0, 6), (10, 0), (2, 4), (1, 4), (4, 3)),
    ('bwd', 8): ((6, 3),),
    ('bwd', 9): ((9, 2), (3, 5)),
    ('bwd', 10): ((0, 7), (7, 4), (10, 1)),
    ('bwd', 11): ((5, 4), (2, 5), (8, 3)),
    ('pair', 2): ((9, 3), (3, 6), (11, 0), (4, 4), (6, 4)),
    ('bwd', 12): ((1, 5),),
    ('bwd', 13): ((0, 8), (5, 5), (7, 5), (10, 2), (2, 6)),
    ('bwd', 14): ((9, 4), (3, 7), (11, 1), (8, 4)),
    ('bwd', 15): ((6, 5),),
    ('pair', 3): ((12, 0), (7, 6), (4, 5)),
    ('tail', 0): ((10, 3), (2, 7), (1, 6)),
    ('tail', 1): ((12, 1), (3, 8), (0, 9)),
    ('tail', 2): ((9, 5), (5, 6), (4, 6)),
    ('tail', 3): ((0, 10), (11, 2), (6, 6), (8, 5)),
    ('tail', 4): ((7, 7), (2, 8), (1, 7)),
    ('tail', 5): ((10, 4),),
    ('small', 0): ((5, 7), (1, 8)),
    ('small', 1): ((12, 2), (9, 6), (3, 9), (7, 8)),
    ('small', 2): ((5, 8), (10, 5), (2, 9), (11, 3), (6, 7)),
    ('last', 0): ((12, 3), (9, 7), (3, 10), (7, 9), (10, 6), (2, 10), (11, 4), (6, 8), (8, 6)),
    ('last', 1): ((12, 4), (9, 8), (7, 10), (10, 7), (11, 5), (6, 9), (8, 7)),
    ('last', 2): ((12, 5), (9, 9), (10, 8), (11, 6), (6, 10), (8, 8)),
    ('last', 3): ((12, 6), (9, 10)),
}


def layer_call(counts, lengths, tokens, memory, ends, grad, params, talk=True):
    _, SH, D = tokens.shape
    MH = memory.shape[1]
    S, M = 2 * SH, 2 * MH
    R = M + S
    gain1, shift1, wq, wk, wv, wo, slopes, gain2, shift2, w1, w2 = params
    FF = w1.shape[1]
    H = slopes.shape[0]
    vmem = pl.BlockSpec(memory_space=pltpu.VMEM)
    smem = pl.BlockSpec(memory_space=pltpu.SMEM)
    hbm = pl.BlockSpec(memory_space=pl.ANY)
    V = pltpu.VMEM
    G = 2 * FF + 4 * D
    units = FF // 256 + 1 + H // 2
    dma = pltpu.SemaphoreType.DMA
    scratch = [
        V((S, D), bf16),
        V((M, D), bf16),
        V((S, D), bf16),
        V((2, 1, MH + SH), jnp.int32),
        V((D, D), bf16),
        V((D, D), bf16),
        V((D, D), bf16),
        V((D, D), bf16),
        V((D, FF), bf16),
        V((FF, D), bf16),
        V((D, R), bf16),
        V((R, D), bf16),
        V((R, D), bf16),
        V((R, 128), bf16),
        V((S, D), bf16),
        V((D, S), bf16),
        V((S, 128), f32),
        V((S, D), f32),
        V((S, D), bf16),
        V((S, D), bf16),
        V((D, S), bf16),
        V((D, S), bf16),
        V((S, 512), bf16),
        V((S, 512), bf16),
        V((S, D), f32),
        V((S, D), f32),
        V((D, S), bf16),
        V((S, 128), bf16),
        V((D, G), bf16),
        V((D // 2, G), bf16),
        V((D // 2 - 16, G), bf16),
        V((4, 8, D), f32),
        V((7, 8, D), f32),
        dma((16,)),
        dma((12,)),
        dma((12,)),
        dma((units, 14)),
        dma((units, 14)),
        dma((7,)),
        dma((7,)),
        dma((units,)),
    ]
    for b in range(S // BLOCK):
        scratch.append(V((H, BLOCK, M + (b + 1) * BLOCK), bf16))
    shapes = (
        jax.ShapeDtypeStruct((2, SH, D), bf16),
        jax.ShapeDtypeStruct((2, SH, D), bf16),
        jax.ShapeDtypeStruct((D, G), bf16),
        jax.ShapeDtypeStruct((8, D), f32),
    )
    extra = {"collective_id": 1, "has_side_effects": True} if talk else {}
    return pl.pallas_call(
        functools.partial(layer_kernel, talk),
        out_shape=shapes,
        in_specs=[smem] * 3 + [hbm] * 4 + [vmem] * 4 + [hbm] * 6,
        out_specs=[hbm, hbm, hbm, vmem],
        scratch_shapes=scratch,
        compiler_params=pltpu.CompilerParams(
            vmem_limit_bytes=64 * 1024 * 1024 - 65536, **extra
        ),
        name="layer",
    )(
        counts, lengths, slopes, tokens, memory, ends, grad,
        gain1.reshape(1, D), shift1.reshape(1, D), gain2.reshape(1, D), shift2.reshape(1, D),
        wq, wk, wv, wo, w1, w2,
    )


def layer_norm(values, gain, shift):
    centred = values - jnp.mean(values, axis=-1, keepdims=True)
    spread = jnp.mean(centred * centred, axis=-1, keepdims=True)
    return centred * lax.rsqrt(spread + epsilon) * gain + shift


def block_scores(
    q_heads, key_block, q_ends, key_order, key_ends, q_index, head_slopes, score_scale
):
    scores = (
        jnp.einsum("qhd,khd->hqk", q_heads, key_block, preferred_element_type=jnp.float32)
        * score_scale
    )
    distance = (q_ends[:, None] - key_ends[None, :]).astype(jnp.float32)
    scores = scores - head_slopes[:, None, None] * distance[None]
    allowed = key_order[None, :] <= q_index[:, None]
    return (jnp.where(allowed[None], scores, -1e30), distance)


def spread_device(
    tokens,
    memory,
    segment_ends,
    memory_ends,
    segment_counts,
    memory_lengths,
    first_gain,
    first_shift,
    query_weight,
    key_weight,
    value_weight,
    out_weight,
    head_slopes,
    second_gain,
    second_shift,
    hidden_weight,
    output_weight,
    output_grad,
):
    seq_count, slot_count, model_width = tokens.shape
    mem_count = memory.shape[1]
    head_count = head_slopes.shape[0]
    head_dim = model_width // head_count
    score_scale = 1.0 / math.sqrt(head_dim)
    key_rows = mem_count + slot_count
    blocks = lax.axis_size("blk")
    my_block = lax.axis_index("blk")
    x_float = tokens.astype(jnp.float32)
    mem_float = memory.astype(jnp.float32)
    normed = layer_norm(x_float, first_gain, first_shift).astype(jnp.bfloat16)
    mem_normed = layer_norm(mem_float, first_gain, first_shift).astype(jnp.bfloat16)
    key_input = jnp.concatenate([mem_normed, normed], axis=1)
    query = jnp.einsum(
        "std,de->ste", normed, query_weight, preferred_element_type=jnp.float32
    ).astype(jnp.bfloat16)
    pair_weight = jnp.concatenate([key_weight, value_weight], axis=1)
    key_value = jnp.einsum(
        "srd,de->rse", key_input, pair_weight, preferred_element_type=jnp.float32
    ).astype(jnp.bfloat16)
    mem_index = my_block * mem_count + jnp.arange(mem_count, dtype=jnp.int32)
    slot_index = my_block * slot_count + jnp.arange(slot_count, dtype=jnp.int32)
    mem_order = jnp.where(
        mem_index[None, :] >= mem_count * blocks - memory_lengths[:, None], -1, far_order
    )
    slot_order = jnp.where(
        slot_index[None, :] < segment_counts[:, None], slot_index[None, :], far_order
    )
    key_meta = jnp.stack(
        [
            jnp.concatenate([mem_order, slot_order], axis=1),
            jnp.concatenate([memory_ends, segment_ends], axis=1),
        ]
    )
    all_pairs, all_meta = (
        lax.all_gather(key_value, "blk", axis=0, tiled=True),
        lax.all_gather(key_meta, "blk", axis=2, tiled=True),
    )
    query_heads = query.reshape(seq_count, slot_count, head_count, head_dim)

    def pick(seq_index):
        pair_rows = lax.dynamic_index_in_dim(all_pairs, seq_index, 1, keepdims=False)
        meta_rows = lax.dynamic_index_in_dim(all_meta, seq_index, 1, keepdims=False)
        key_heads = pair_rows[:, :model_width].reshape(-1, key_rows, head_count, head_dim)
        value_heads = pair_rows[:, model_width:].reshape(-1, key_rows, head_count, head_dim)
        return (
            key_heads,
            value_heads,
            meta_rows[0].reshape(-1, key_rows),
            meta_rows[1].reshape(-1, key_rows),
        )

    def attend(seq_index):
        key_heads, value_heads, key_order, key_ends = pick(seq_index)
        q_heads = lax.dynamic_index_in_dim(query_heads, seq_index, 0, keepdims=False)
        q_ends = lax.dynamic_index_in_dim(segment_ends, seq_index, 0, keepdims=False)

        def stats_step(running, pieces):
            scores = block_scores(
                q_heads,
                pieces[0],
                q_ends,
                pieces[1],
                pieces[2],
                slot_index,
                head_slopes,
                score_scale,
            )[0]
            running_max = jnp.maximum(running[0], jnp.max(scores, axis=-1))
            running_sum = running[1] * jnp.exp(running[0] - running_max) + jnp.sum(
                jnp.exp(scores - running_max[..., None]), axis=-1
            )
            return ((running_max, running_sum), None)

        start_max = jnp.full((head_count, slot_count), -jnp.inf, jnp.float32)
        (top_max, top_sum), _ = lax.scan(
            stats_step, (start_max, jnp.zeros_like(start_max)), (key_heads, key_order, key_ends)
        )
        log_total = top_max + jnp.log(top_sum)

        def out_step(summed, pieces):
            scores = block_scores(
                q_heads,
                pieces[0],
                q_ends,
                pieces[1],
                pieces[2],
                slot_index,
                head_slopes,
                score_scale,
            )[0]
            attn_probs = jnp.exp(scores - log_total[..., None]).astype(jnp.bfloat16)
            return (
                summed
                + jnp.einsum(
                    "hqk,khd->qhd", attn_probs, pieces[3], preferred_element_type=jnp.float32
                ),
                None,
            )

        start_out = jnp.zeros((slot_count, head_count, head_dim), jnp.float32)
        mixed_heads, _ = lax.scan(
            out_step, start_out, (key_heads, key_order, key_ends, value_heads)
        )
        return (mixed_heads, log_total)

    mixed_all, log_totals = lax.map(attend, jnp.arange(seq_count))
    mixed_low = mixed_all.reshape(seq_count, slot_count, model_width).astype(jnp.bfloat16)
    residual = x_float + jnp.einsum(
        "std,de->ste", mixed_low, out_weight, preferred_element_type=jnp.float32
    )
    second_low = layer_norm(residual, second_gain, second_shift).astype(jnp.bfloat16)
    hidden_pre = jnp.einsum(
        "std,df->stf", second_low, hidden_weight, preferred_element_type=jnp.float32
    )
    act_low = jax.nn.gelu(hidden_pre, approximate=False).astype(jnp.bfloat16)
    layer_out = (
        residual
        + jnp.einsum("stf,fd->std", act_low, output_weight, preferred_element_type=jnp.float32)
    ).astype(jnp.bfloat16)
    grad_output_w = jnp.einsum(
        "stf,std->fd", act_low, output_grad, preferred_element_type=jnp.float32
    )
    d_act = jnp.einsum(
        "std,fd->stf", output_grad, output_weight, preferred_element_type=jnp.float32
    )
    _, gelu_pull = jax.vjp(lambda inner: jax.nn.gelu(inner, approximate=False), hidden_pre)
    d_pre_low = gelu_pull(d_act)[0].astype(jnp.bfloat16)
    grad_hidden_w = jnp.einsum(
        "std,stf->df", second_low, d_pre_low, preferred_element_type=jnp.float32
    )
    d_second = jnp.einsum(
        "stf,df->std", d_pre_low, hidden_weight, preferred_element_type=jnp.float32
    )
    _, second_pull = jax.vjp(layer_norm, residual, second_gain, second_shift)
    d_resid_norm, grad_second_g, grad_second_b = second_pull(d_second)
    d_residual = d_resid_norm + output_grad.astype(jnp.float32)
    d_branch = d_residual.astype(jnp.bfloat16)
    grad_out_w = jnp.einsum("std,ste->de", mixed_low, d_branch, preferred_element_type=jnp.float32)
    d_mixed = jnp.einsum(
        "ste,de->std", d_branch, out_weight, preferred_element_type=jnp.float32
    ).astype(jnp.bfloat16)
    d_mixed_heads = d_mixed.reshape(seq_count, slot_count, head_count, head_dim)

    def query_side(seq_index):
        key_heads, value_heads, key_order, key_ends = pick(seq_index)
        q_heads = lax.dynamic_index_in_dim(query_heads, seq_index, 0, keepdims=False)
        q_ends = lax.dynamic_index_in_dim(segment_ends, seq_index, 0, keepdims=False)
        d_heads = lax.dynamic_index_in_dim(d_mixed_heads, seq_index, 0, keepdims=False)
        log_total = lax.dynamic_index_in_dim(log_totals, seq_index, 0, keepdims=False)

        def probs_of(key_block, order_block, ends_block, value_block):
            scores, distance = block_scores(
                q_heads,
                key_block,
                q_ends,
                order_block,
                ends_block,
                slot_index,
                head_slopes,
                score_scale,
            )
            attn_probs = jnp.exp(scores - log_total[..., None])
            d_probs = jnp.einsum(
                "qhd,khd->hqk", d_heads, value_block, preferred_element_type=jnp.float32
            )
            return (attn_probs, d_probs, distance)

        def delta_step(summed, pieces):
            attn_probs, d_probs, _ = probs_of(pieces[0], pieces[1], pieces[2], pieces[3])
            return (summed + jnp.sum(attn_probs * d_probs, axis=-1), None)

        delta_rows, _ = lax.scan(
            delta_step,
            jnp.zeros((head_count, slot_count), jnp.float32),
            (key_heads, key_order, key_ends, value_heads),
        )

        def grad_step(running, pieces):
            attn_probs, d_probs, distance = probs_of(pieces[0], pieces[1], pieces[2], pieces[3])
            d_scores = (attn_probs * (d_probs - delta_rows[..., None])).astype(jnp.bfloat16)
            d_query = running[0] + jnp.einsum(
                "hqk,khd->qhd", d_scores, pieces[0], preferred_element_type=jnp.float32
            )
            d_slopes = running[1] - jnp.sum(
                d_scores.astype(jnp.float32) * distance[None], axis=(1, 2)
            )
            return ((d_query, d_slopes), None)

        start_grads = (
            jnp.zeros((slot_count, head_count, head_dim), jnp.float32),
            jnp.zeros((head_count,), jnp.float32),
        )
        (d_query, d_slopes), _ = lax.scan(
            grad_step, start_grads, (key_heads, key_order, key_ends, value_heads)
        )
        return (d_query * score_scale, delta_rows, d_slopes)

    d_query_all, delta_all, slope_parts = lax.map(query_side, jnp.arange(seq_count))
    grad_slopes = jnp.sum(slope_parts, axis=0)
    d_query_low = d_query_all.reshape(seq_count, slot_count, model_width).astype(jnp.bfloat16)

    def pair_terms(
        pair_rows, order_block, ends_block, q_heads, q_ends, q_index, d_heads, log_total, delta_rows
    ):
        key_block = pair_rows[:, :model_width].reshape(key_rows, head_count, head_dim)
        value_block = pair_rows[:, model_width:].reshape(key_rows, head_count, head_dim)
        scores, _ = block_scores(
            q_heads, key_block, q_ends, order_block, ends_block, q_index, head_slopes, score_scale
        )
        attn_probs = jnp.exp(scores - log_total[..., None])
        d_probs = jnp.einsum(
            "qhd,khd->hqk", d_heads, value_block, preferred_element_type=jnp.float32
        )
        d_scores = (attn_probs * (d_probs - delta_rows[..., None])).astype(jnp.bfloat16)
        d_value = jnp.einsum(
            "hqk,qhd->khd",
            attn_probs.astype(jnp.bfloat16),
            d_heads,
            preferred_element_type=jnp.float32,
        )
        d_key = (
            jnp.einsum("hqk,qhd->khd", d_scores, q_heads, preferred_element_type=jnp.float32)
            * score_scale
        )
        return jnp.concatenate(
            [d_key.reshape(key_rows, model_width), d_value.reshape(key_rows, model_width)], axis=1
        )

    def one_block(block_index):
        offset = block_index * key_rows
        pair_block = lax.dynamic_slice_in_dim(all_pairs, offset, key_rows, 0)
        meta_block = lax.dynamic_slice_in_dim(all_meta, offset, key_rows, 2)
        return jax.vmap(pair_terms, in_axes=(1, 0, 0, 0, 0, None, 0, 0, 0), out_axes=1)(
            pair_block,
            meta_block[0],
            meta_block[1],
            query_heads,
            segment_ends,
            slot_index,
            d_mixed_heads,
            log_totals,
            delta_all,
        )

    pieces = lax.map(one_block, jnp.arange(lax.axis_size("blk") * key_rows // key_rows))
    pair_grads = lax.psum_scatter(
        pieces.reshape(lax.axis_size("blk") * key_rows, seq_count, 2 * model_width).astype(
            jnp.bfloat16
        ),
        "blk",
        scatter_dimension=0,
        tiled=True,
    )
    grad_pair_w = jnp.einsum(
        "srd,rse->de", key_input, pair_grads, preferred_element_type=jnp.float32
    )
    grad_key_w = grad_pair_w[:, :model_width]
    grad_value_w = grad_pair_w[:, model_width:]
    d_key_input = jnp.einsum(
        "rse,de->srd", pair_grads, pair_weight, preferred_element_type=jnp.float32
    )
    grad_query_w = jnp.einsum(
        "std,ste->de", normed, d_query_low, preferred_element_type=jnp.float32
    )
    d_normed = (
        jnp.einsum("ste,de->std", d_query_low, query_weight, preferred_element_type=jnp.float32)
        + d_key_input[:, mem_count:]
    )
    _, first_pull = jax.vjp(layer_norm, x_float, first_gain, first_shift)
    d_tokens, gain_slots, shift_slots = first_pull(d_normed)
    _, mem_pull = jax.vjp(
        lambda gain, shift: layer_norm(mem_float, gain, shift), first_gain, first_shift
    )
    gain_mem, shift_mem = mem_pull(d_key_input[:, :mem_count])
    input_grad = (d_tokens + d_residual).astype(jnp.bfloat16)
    grad_first_g = gain_slots + gain_mem
    grad_first_b = shift_slots + shift_mem
    summed = lax.psum(
        (
            grad_first_g,
            grad_first_b,
            grad_query_w,
            grad_key_w,
            grad_value_w,
            grad_out_w,
            grad_slopes,
            grad_second_g,
            grad_second_b,
            grad_hidden_w,
            grad_output_w,
        ),
        ("seq", "blk"),
    )
    return (
        layer_out,
        input_grad,
        summed[0],
        summed[1],
        summed[2],
        summed[3],
        summed[4],
        summed[5],
        summed[6],
        summed[7],
        summed[8],
        summed[9],
        summed[10],
    )


def widen_kernel(ga, gb, gc, layer_in, grad_in, small, *outs):
    gw1, gw2, go, gq, gk, gv, layer, grad, gain1, shift1, slopes, gain2, shift2 = outs
    half = ga.shape[1] // 2
    gw1[...] = ga[:, :half].astype(f32)
    gw2[...] = ga[:, half:].astype(f32).T
    go[...] = gb[...].astype(f32)
    for i, out in enumerate((gq, gk, gv)):
        out[...] = gc[:, i * 128 : (i + 1) * 128].astype(f32)
    layer[...] = layer_in[...]
    grad[...] = grad_in[...]

    @pl.when((pl.program_id(0) == 0) & (pl.program_id(1) == 0))
    def _():
        for i, out in enumerate((gain1, shift1, gain2, shift2)):
            out[...] = small[i : i + 1, :]
        slopes[...] = small[4:5, 0:128]


def widen(grads, layer, in_grad, small, D, FF):
    RB = D // 2
    LB = layer.shape[0] // 8
    out = [
        ((D, FF), (RB, 512), lambda c, r: (r, c)),
        ((FF, D), (512, RB), lambda c, r: (c, r)),
        ((D, D), (RB, 128), lambda c, r: (r, c)),
        ((D, D), (RB, 128), lambda c, r: (r, c)),
        ((D, D), (RB, 128), lambda c, r: (r, c)),
        ((D, D), (RB, 128), lambda c, r: (r, c)),
        ((8 * LB, D), (LB, D), lambda c, r: (2 * c + r, 0)),
        ((8 * LB, D), (LB, D), lambda c, r: (2 * c + r, 0)),
    ]
    kinds = [f32] * 6 + [bf16] * 2
    shapes = [jax.ShapeDtypeStruct(shape, kind) for (shape, _, _), kind in zip(out, kinds)]
    specs = [pl.BlockSpec(block, index) for _, block, index in out]
    for width in (D, D, 128, D, D):
        shapes.append(jax.ShapeDtypeStruct((1, width), f32))
        specs.append(pl.BlockSpec((1, width), lambda c, r: (0, 0)))
    go_at = 2 * FF // 128
    head_at = (2 * FF + D) // 384
    return pl.pallas_call(
        widen_kernel,
        grid=(4, 2),
        out_shape=shapes,
        in_specs=[
            pl.BlockSpec((RB, 1024), lambda c, r: (r, c)),
            pl.BlockSpec((RB, 128), lambda c, r: (r, go_at + c)),
            pl.BlockSpec((RB, 384), lambda c, r: (r, head_at + c)),
            pl.BlockSpec((LB, D), lambda c, r: (2 * c + r, 0)),
            pl.BlockSpec((LB, D), lambda c, r: (2 * c + r, 0)),
            pl.BlockSpec((8, D), lambda c, r: (0, 0)),
        ],
        out_specs=specs,
        compiler_params=pltpu.CompilerParams(vmem_limit_bytes=62 * 1024 * 1024),
        name="widen",
    )(grads, grads, grads, layer, in_grad, small)


def whole_device(*args):
    tokens, memory, segment_ends, memory_ends, counts, lengths = args[:6]
    params = args[6:17]
    output_grad = args[17]
    D = tokens.shape[2]
    FF = params[9].shape[1]
    H = params[6].shape[0]
    ends = jnp.concatenate([memory_ends, segment_ends], axis=1)[:, None]
    layer, in_grad, grads, small = layer_call(
        counts, lengths, tokens, memory, ends, output_grad, params
    )
    gw1, gw2, go, gq, gk, gv, layer, in_grad, *rows = widen(
        grads, layer.reshape(-1, D), in_grad.reshape(-1, D), small, D, FF
    )
    gain1, shift1, slopes, gain2, shift2 = (row[0] for row in rows)
    return (
        layer.reshape(tokens.shape),
        in_grad.reshape(tokens.shape),
        gain1,
        shift1,
        gq,
        gk,
        gv,
        go,
        slopes[:H],
        gain2,
        shift2,
        gw1,
        gw2,
    )


def per_device(*args):
    whole = args[0].shape[0] == lax.axis_size("blk") == 2 and lax.axis_size("seq") == 16
    if whole:
        return whole_device(*args)
    return spread_device(*args)


def solution(mesh):
    placed = (
        P("seq", "blk", None),
        P("seq", "blk", None),
        P("seq", "blk"),
        P("seq", "blk"),
        P("seq"),
        P("seq"),
        P(),
        P(),
        P(),
        P(),
        P(),
        P(),
        P(),
        P(),
        P(),
        P(),
        P(),
        P("seq", "blk", None),
    )
    return jax.shard_map(
        per_device,
        mesh=mesh,
        in_specs=placed,
        out_specs=(
            P("seq", "blk", None),
            P("seq", "blk", None),
            P(),
            P(),
            P(),
            P(),
            P(),
            P(),
            P(),
            P(),
            P(),
            P(),
            P(),
        ),
        check_vma=False,
    )
```

```python
import functools
import math

import jax
import jax.numpy as jnp
from jax import lax
from jax.experimental import pallas as pl
from jax.experimental.pallas import tpu as pltpu
from jax.sharding import PartitionSpec as P

epsilon = 1e-05
far_order = 1073741824
f32 = jnp.float32
bf16 = jnp.bfloat16
BLOCK = 256
LOG2E = 1.4426950408889634
LN2 = 0.6931471805599453


def dot_nn(left, right):
    return lax.dot_general(left, right, (((1,), (0,)), ((), ())), preferred_element_type=f32)


def dot_nt(left, right):
    return lax.dot_general(left, right, (((1,), (1,)), ((), ())), preferred_element_type=f32)


def norm_stats(values):
    centred = values - jnp.mean(values, axis=-1, keepdims=True)
    spread = jnp.mean(centred * centred, axis=-1, keepdims=True)
    scale = lax.rsqrt(spread + epsilon)
    return centred * scale, scale


def norm_back(unit, scale, grad_unit):
    mean_grad = jnp.mean(grad_unit, axis=-1, keepdims=True)
    mean_prod = jnp.mean(grad_unit * unit, axis=-1, keepdims=True)
    return (grad_unit - mean_grad - unit * mean_prod) * scale


def pieces_of(value, count):
    out = []
    for _ in range(count):
        part = value.astype(bf16).astype(f32)
        out.append(part)
        value = value - part
    return out


ERFC_P = 0.4
ERFC_C = (0.22567586600780487, 0.2256695181131363, 0.2078438550233841, 0.16853390634059906, 0.1414608359336853, -0.005667657125741243, 0.16915477812290192, -0.18294358253479004, 0.050272583961486816)


def gelu_both(x):
    cdf = 0.5 * lax.erf(x * math.sqrt(0.5)) + 0.5
    ex = jnp.exp2((x * x) * (-0.5 * LOG2E))
    return x * cdf, cdf + x * (ex * (1.0 / math.sqrt(2.0 * math.pi)))


def col_sum8(value):
    return jnp.sum(value.reshape(-1, 8, value.shape[-1]), axis=0)


def flip(bit):
    return 1 - bit


def layer_kernel(
    talk,
    counts_ref,
    lengths_ref,
    slopes_ref,
    tokens_ref,
    memory_ref,
    ends_ref,
    grad_ref,
    gain1_ref,
    shift1_ref,
    gain2_ref,
    shift2_ref,
    wq_hbm,
    wk_hbm,
    wv_hbm,
    wo_hbm,
    w1_hbm,
    w2_hbm,
    layer_hbm,
    ingrad_hbm,
    grads_hbm,
    small_ref,
    x_ref,
    mem_ref,
    og_ref,
    ends_s,
    wq_ref,
    wk_ref,
    wv_ref,
    wo_ref,
    w1_ref,
    w2_ref,
    keyint,
    k_s,
    v_s,
    kx,
    q_s,
    qt,
    rl_s,
    o_s,
    mixed,
    second_s,
    secondt,
    ogt,
    act_s,
    dpre_s,
    acc_s,
    dres,
    dolt,
    delta_s,
    g_s,
    rc_s,
    r1_s,
    sm_own,
    sm_in,
    load_sem,
    ex_send,
    ex_recv,
    ar_send,
    ar_recv,
    sm_send,
    sm_recv,
    out_sem,
    *probs,
):
    S, D = x_ref.shape
    M = mem_ref.shape[0]
    R = M + S
    FF = w1_ref.shape[1]
    H = slopes_ref.shape[0]
    DH = D // H
    HP = H // 2
    NB = S // BLOCK
    MB = M // BLOCK
    SH = S // 2
    MH = M // 2
    KC = 512
    CH = 512
    NC = FF // CH

    if talk:
        seq = lax.axis_index("seq")
        blk = lax.axis_index("blk")
    else:
        seq = 0
        blk = 0
    core = seq % 2
    why = (seq // 2) % 2
    zed = seq // 4

    def at(z=None, y=None, c=None, x=None):
        z = zed if z is None else z
        y = why if y is None else y
        c = core if c is None else c
        return {"seq": z * 4 + y * 2 + c, "blk": blk if x is None else x}

    sibling = at(c=flip(core))
    partner = at(x=flip(blk))
    z_to = [zed + 1 - 2 * (zed % 2), (zed + 2) % 4, 3 - zed]
    z_peers = [(at(z=z), z) for z in z_to]
    plane = blk * 2 + why
    xy_peers = [
        (at(y=flip(why)), blk * 2 + flip(why)),
        (at(x=flip(blk)), flip(blk) * 2 + why),
        (at(x=flip(blk), y=flip(why)), flip(blk) * 2 + flip(why)),
    ]

    def remote(src, dst, send, recv, device):
        return pltpu.make_async_remote_copy(
            src_ref=src,
            dst_ref=dst,
            send_sem=send,
            recv_sem=recv,
            device_id=device,
            device_id_type=pl.DeviceIdType.MESH,
        )

    other = 1 - blk

    def half_rows(half, size):
        return pl.ds(pl.multiple_of(half * size, BLOCK), size)

    def slot_piece(part, index, half, i):
        src = tokens_ref if part == 0 else grad_ref
        dst = x_ref if part == 0 else og_ref
        rows = pl.ds(pl.multiple_of(half * SH + i * BLOCK, BLOCK), BLOCK)
        return src.at[index, i * BLOCK : (i + 1) * BLOCK, :], dst.at[rows, :]

    nslot = SH // BLOCK
    loads = [
        (memory_ref.at[blk], mem_ref.at[half_rows(blk, MH), :]),
        (ends_ref.at[blk], ends_s.at[blk]),
        (wk_hbm, wk_ref),
        (wv_hbm, wv_ref),
        (wq_hbm, wq_ref),
    ]
    loads += [slot_piece(0, blk, blk, i) for i in range(nslot)]
    n_first = len(loads)
    loads += [(wo_hbm, wo_ref), (w1_hbm, w1_ref), (w2_hbm, w2_ref)]
    loads += [slot_piece(1, blk, blk, i) for i in range(nslot)]
    copies = [
        pltpu.make_async_copy(src, dst, load_sem.at[i]) for i, (src, dst) in enumerate(loads)
    ]
    sends = [
        (memory_ref.at[other], mem_ref.at[half_rows(blk, MH), :]),
        (ends_ref.at[other], ends_s.at[blk]),
    ]
    sends += [slot_piece(0, other, blk, i) for i in range(nslot)]
    sends += [slot_piece(1, other, blk, i) for i in range(nslot)]
    if talk:
        exchange = [
            remote(src, dst, ex_send.at[i], ex_recv.at[i], partner)
            for i, (src, dst) in enumerate(sends)
        ]
    else:
        local = [
            (memory_ref.at[other], mem_ref.at[half_rows(other, MH), :]),
            (ends_ref.at[other], ends_s.at[other]),
        ]
        local += [slot_piece(0, other, other, i) for i in range(nslot)]
        local += [slot_piece(1, other, other, i) for i in range(nslot)]
        exchange = [
            pltpu.make_async_copy(src, dst, ex_send.at[i]) for i, (src, dst) in enumerate(local)
        ]
    for copy in copies[:n_first]:
        copy.start()
    if talk:
        barrier = pltpu.get_barrier_semaphore()
        greet = [sibling] + [d for d, _ in z_peers] + [d for d, _ in xy_peers]
        for device in greet:
            pl.semaphore_signal(
                barrier, inc=1, device_id=device, device_id_type=pl.DeviceIdType.MESH
            )
        pl.semaphore_wait(barrier, len(greet))
    for copy in exchange:
        copy.start()
    for copy in copies[n_first:]:
        copy.start()

    def arrive(i):
        if talk:
            exchange[i].wait_recv()
        else:
            exchange[i].wait()

    directions = {
        "x": (blk, [(partner, other)]),
        "y": (why, [(at(y=flip(why)), flip(why))]),
        "a": (zed % 2, [(z_peers[0][0], 1 - zed % 2)]),
        "b": (zed // 2, [(z_peers[1][0], 1 - zed // 2)]),
        "z": (zed, z_peers),
        "p": (plane, xy_peers),
    }
    units = []
    for c in range(NC):
        width = 2 * CH // SPLIT[c]
        for i in range(SPLIT[c]):
            units.append((c * 2 * CH + i * width, width))
    units.append((2 * FF, D))
    for p in range(HP):
        units.append((2 * FF + D + p * 384, 384))
    HALF = D // 2

    def rows_at(start, size):
        return pl.ds(pl.multiple_of(start, 16), size)

    def unit_rounds(u):
        start, size, place = core * HALF, HALF, 0
        rounds = []
        for name in ORDERS[u]:
            mine, peers = directions[name]
            piece = size // (len(peers) + 1)
            rounds.append((start, piece, mine, peers, place))
            place += piece * len(peers)
            start, size = start + mine * piece, piece
        return rounds, start, size

    def unit_copies(u, step):
        col, width = units[u]
        cols = slice(col, col + width)
        rounds, start, size = unit_rounds(u)
        n = len(rounds)
        out = []
        if step == 0:
            rows = rows_at((1 - core) * HALF, HALF)
            out.append((g_s.at[rows, cols], rc_s.at[:, cols], sibling))
        elif step <= n:
            begin, piece, _, peers, place = rounds[step - 1]
            for d, (device, index) in enumerate(peers):
                rows = rows_at(begin + index * piece, piece)
                here = slice(place + d * piece, place + (d + 1) * piece)
                out.append((g_s.at[rows, cols], r1_s.at[here, cols], device))
        elif step <= 2 * n:
            level = 2 * n - step
            begin, piece, mine, peers, _ = rounds[level]
            rows = rows_at(begin + mine * piece, piece)
            src = g_s if level == n - 1 else grads_hbm
            for device, _ in peers:
                out.append((src.at[rows, cols], grads_hbm.at[rows, cols], device))
        else:
            rows = rows_at(core * HALF, HALF)
            out.append((grads_hbm.at[rows, cols], grads_hbm.at[rows, cols], sibling))
        first = 0
        for earlier in range(step):
            if 1 <= earlier <= n:
                first += len(rounds[earlier - 1][3])
            elif n < earlier <= 2 * n:
                first += len(rounds[2 * n - earlier][3])
            else:
                first += 1
        return [
            remote(src, dst, ar_send.at[u, first + k], ar_recv.at[u, first + k], device)
            for k, (src, dst, device) in enumerate(out)
        ]

    def unit_add(u, step):
        col, width = units[u]
        cols = slice(col, col + width)
        rounds, _, _ = unit_rounds(u)
        if step == 0:
            begin, piece, places, buffer = core * HALF, HALF, [0], rc_s
        else:
            begin, piece, mine, peers, place = rounds[step - 1]
            begin = begin + mine * piece
            places, buffer = [place + d * piece for d in range(len(peers))], r1_s
        block = min(piece, 64)

        def add(i, _):
            rows = rows_at(begin + i * block, block)
            total = g_s[rows, cols].astype(f32)
            for place in places:
                total = total + buffer[rows_at(place + i * block, block), cols].astype(f32)
            g_s[rows, cols] = total.astype(bf16)
            return 0

        if piece == block:
            add(0, 0)
        else:
            lax.fori_loop(0, piece // block, add, 0)

    def unit_out(u):
        col, width = units[u]
        cols = slice(col, col + width)
        _, start, size = unit_rounds(u)
        rows = rows_at(start, size) if talk else slice(0, D)
        return pltpu.make_async_copy(g_s.at[rows, cols], grads_hbm.at[rows, cols], out_sem.at[u])

    def advance(u, step):
        if not talk:
            return
        n = len(ORDERS[u])
        if step > 0:
            for copy in unit_copies(u, step - 1):
                copy.wait()
            if step - 1 <= n:
                unit_add(u, step - 1)
        if step == n + 1:
            unit_out(u).start()
        if step == n + 2:
            unit_out(u).wait()
        if step < 2 * n + 2:
            for copy in unit_copies(u, step):
                copy.start()

    def ticks(kind, index):
        moves = SCHEDULE.get((kind, index), ())
        if not moves:
            return

        @pl.when(seq >= 0)
        def _():
            for u, step in moves:
                if u < 0:
                    layer_copies[1 + step].start()
                else:
                    advance(u, step)

    def ticks_in_loop(kind, index, count, base=0):
        for k in range(count):
            if (kind, base + k) in SCHEDULE:

                @pl.when(index == k)
                def _():
                    ticks(kind, base + k)

    gain1 = gain1_ref[...]
    shift1 = shift1_ref[...]
    gain2 = gain2_ref[...]
    shift2 = shift2_ref[...]
    count = counts_ref[blk]
    length = lengths_ref[blk]

    def give(result, hbm, k, pieces):
        own = pltpu.make_async_copy(result.at[half_rows(blk, SH), :], hbm.at[blk], load_sem.at[k])
        moves = [own]
        size = SH // pieces
        for i in range(pieces):
            theirs = result.at[pl.ds(pl.multiple_of(other * SH + i * size, size), size), :]
            rows = slice(i * size, (i + 1) * size)
            sem = len(sends) + 4 * k + i
            if talk:
                there = hbm.at[blk, rows, :]
                moves.append(remote(theirs, there, ex_send.at[sem], ex_recv.at[sem], partner))
            else:
                moves.append(
                    pltpu.make_async_copy(theirs, hbm.at[other, rows, :], ex_send.at[sem])
                )
        return moves

    layer_copies = give(second_s, layer_hbm, 0, 4)
    ingrad_copies = give(second_s, ingrad_hbm, 1, nslot)

    def project(normed, key_rows):
        keyint[:, key_rows] = normed.T
        k_s[key_rows, :] = dot_nn(normed, wk_ref[...]).astype(bf16)
        v_s[key_rows, :] = dot_nn(normed, wv_ref[...]).astype(bf16)

    def norm_mem(b):
        rows = pl.ds(pl.multiple_of(b * BLOCK, BLOCK), BLOCK)
        unit, _ = norm_stats(mem_ref[rows, :].astype(f32))
        project((unit * gain1 + shift1).astype(bf16), rows)

    def norm_slot(b):
        rows = pl.ds(pl.multiple_of(b * BLOCK, BLOCK), BLOCK)
        key_rows = pl.ds(pl.multiple_of(b * BLOCK + M, BLOCK), BLOCK)
        unit, _ = norm_stats(x_ref[rows, :].astype(f32))
        normed = (unit * gain1 + shift1).astype(bf16)
        project(normed, key_rows)
        query = (dot_nn(normed, wq_ref[...]) * (LOG2E / math.sqrt(DH))).astype(bf16)
        q_s[rows, :] = query
        qt[:, rows] = query.T

    for copy in copies[:n_first]:
        copy.wait()
    mh = MH // BLOCK
    for i in range(mh):
        norm_mem(blk * mh + i)
    for i in range(nslot):
        norm_slot(blk * nslot + i)
    arrive(0)
    for i in range(mh):
        norm_mem(other * mh + i)
    arrive(1)

    lane = lax.broadcasted_iota(jnp.int32, (128, 128), 1)
    row = lax.broadcasted_iota(jnp.int32, (128, 128), 0)

    def end_row(start, size):
        if start < M:
            half, off = start // MH, start % MH
        else:
            half, off = (start - M) // SH, MH + (start - M) % SH
        return ends_s[half, :, off : off + size].astype(f32)

    for r in range(R // 128):
        end_col = jnp.broadcast_to(end_row(r * 128, 128), (128, 128)).T
        high = jnp.floor(end_col * (1.0 / 256.0)) * 256.0
        index = row + r * 128
        if r * 128 < M:
            valid = index >= M - length
        else:
            valid = index - M < count
        bias = jnp.where(valid, 0.0, -1e30)
        extra = jnp.where(lane < 3, high, jnp.where(lane < 6, end_col - high, bias))
        extra = jnp.where(lane == 7, 1.0, jnp.where(lane > 7, 0.0, extra))
        kx[r * 128 : (r + 1) * 128, :] = extra.astype(bf16)

    for i in range(nslot):
        arrive(2 + i)
        norm_slot(other * nslot + i)

    lane_q = lax.broadcasted_iota(jnp.int32, (BLOCK, 128), 1)
    first_half = lane_q < DH
    lane_row = lax.broadcasted_iota(jnp.int32, (1, 128), 1)

    def key_chunks(b):
        end = M + (b + 1) * BLOCK
        return [(start, min(KC, end - start)) for start in range(0, end, KC)]

    def key_full(lanes, start, size):
        return jnp.concatenate(
            [k_s[start : start + size, lanes], kx[start : start + size, :]], axis=1
        )

    def value_full(lanes, start, size):
        return jnp.concatenate(
            [v_s[start : start + size, lanes], jnp.ones((size, 128), bf16)], axis=1
        )

    def query_extra(head):
        slope = jnp.full((1, 128), slopes_ref[head] * LOG2E, f32)
        s1, s2, s3 = pieces_of(slope, 3)
        where = jnp.where(lane_row >= 3, lane_row - 3, lane_row)
        out = jnp.where(where == 0, s1, jnp.where(where == 1, s2, s3))
        return jnp.where(lane_row < 6, out, jnp.where(lane_row == 6, 1.0, 0.0))

    rl_s[...] = jnp.zeros_like(rl_s)
    for b in range(NB):
        rows = slice(b * BLOCK, (b + 1) * BLOCK)
        e_ref = probs[b]

        def fwd_pair(p, _):
            lanes = slice(p * 128, (p + 1) * 128)
            q_pair = q_s[rows, lanes]
            outs = []
            for half in range(2):
                keep = first_half if half == 0 else jnp.logical_not(first_half)
                q_half = jnp.where(keep, q_pair, jnp.zeros_like(q_pair))
                extra = jnp.broadcast_to(query_extra(2 * p + half), (BLOCK, 128)).astype(bf16)
                q_full = jnp.concatenate([q_half, extra], axis=1)
                chunks = key_chunks(b)
                scores = [dot_nt(q_full, key_full(lanes, k0, kn)) for k0, kn in chunks]
                below = lax.broadcasted_iota(
                    jnp.int32, (BLOCK, BLOCK), 1
                ) <= lax.broadcasted_iota(jnp.int32, (BLOCK, BLOCK), 0)
                last = scores[-1]
                cut = last.shape[1] - BLOCK
                diag = jnp.where(below, last[:, cut:], -1e30)
                scores[-1] = jnp.concatenate([last[:, :cut], diag], axis=1) if cut else diag
                top = scores[-1][:, 0:128]
                for part in scores:
                    for k in range(0, part.shape[1], 128):
                        top = jnp.maximum(top, part[:, k : k + 128])
                top = jnp.max(top, axis=1, keepdims=True)
                both = jnp.zeros((BLOCK, 256), f32)
                for part, (k0, kn) in zip(scores, chunks):
                    e = jnp.exp2(part - top).astype(bf16)
                    e_ref[2 * p + half, :, k0 : k0 + kn] = e
                    both = both + dot_nn(e, value_full(lanes, k0, kn))
                outs.append((both[:, 0:128], 1.0 / both[:, 128:256]))
            rl = jnp.where(first_half, outs[0][1], outs[1][1])
            o = jnp.where(first_half, outs[0][0], outs[1][0]) * rl
            packed = jnp.where(lane_q == 2 * p, outs[0][1], rl_s[rows, :])
            rl_s[rows, :] = jnp.where(lane_q == 2 * p + 1, outs[1][1], packed)
            o_low = o.astype(bf16)
            o_s[rows, lanes] = (o - o_low.astype(f32)).astype(bf16)
            mixed[rows, lanes] = o_low
            return 0

        for p in range(HP):
            fwd_pair(p, 0)

    for copy in copies[n_first:]:
        copy.wait()
    for i in range(nslot):
        arrive(2 + nslot + i)

    def residual_of(rows):
        return x_ref[rows, :].astype(f32) + dot_nn(mixed[rows, :], wo_ref[...])

    def feed_prep(b, _):
        rows = slice(b * BLOCK, (b + 1) * BLOCK)
        residual = residual_of(rows)
        unit, _ = norm_stats(residual)
        second = (unit * gain2 + shift2).astype(bf16)
        second_s[rows, :] = second
        secondt[:, rows] = second.T
        ogt[:, rows] = og_ref[rows, :].T
        acc_s[rows, :] = residual
        return 0

    for b in range(NB):
        feed_prep(b, 0)
    for c in range(NC):
        cols = slice(c * CH, (c + 1) * CH)

        def feed(b, _):
            rows = slice(b * BLOCK, (b + 1) * BLOCK)
            hidden = dot_nn(second_s[rows, :], w1_ref[:, cols])
            d_act = dot_nt(og_ref[rows, :], w2_ref[cols, :])
            act, slope = gelu_both(hidden)
            act = act.astype(bf16)
            d_pre = (d_act * slope).astype(bf16)
            act_s[rows, :] = act
            dpre_s[rows, :] = d_pre
            acc_s[rows, :] += dot_nn(act, w2_ref[cols, :])
            d_second = dot_nt(d_pre, w1_ref[:, cols])
            dres[rows, :] = d_second if c == 0 else dres[rows, :] + d_second
            ticks("feed", c * NB + b)
            return 0

        for b in range(NB):
            feed(b, 0)
        base = c * 2 * CH
        for r in range(D // BLOCK):
            rows = slice(r * BLOCK, (r + 1) * BLOCK)
            g_s[rows, base : base + CH] = dot_nn(secondt[rows, :], dpre_s[...]).astype(bf16)
            g_s[rows, base + CH : base + 2 * CH] = dot_nn(ogt[rows, :], act_s[...]).astype(bf16)
        ticks("chunk", c)

    def feed_post(b, sums):
        rows = slice(b * BLOCK, (b + 1) * BLOCK)
        unit, scale = norm_stats(residual_of(rows))
        d_second = dres[rows, :]
        d_residual = og_ref[rows, :].astype(f32) + norm_back(unit, scale, d_second * gain2)
        dres[rows, :] = d_residual
        d_branch = d_residual.astype(bf16)
        act_s[rows, :] = d_branch
        secondt[:, rows] = mixed[rows, :].T
        d_mixed = dot_nt(d_branch, wo_ref[...]).astype(bf16).astype(f32)
        rl_b = rl_s[rows, :]
        rl_wide = []
        for p in range(HP):
            first = jnp.broadcast_to(rl_b[:, 2 * p : 2 * p + 1], (BLOCK, 128))
            second = jnp.broadcast_to(rl_b[:, 2 * p + 1 : 2 * p + 2], (BLOCK, 128))
            rl_wide.append(jnp.where(first_half, first, second))
        dol_b = (d_mixed * jnp.concatenate(rl_wide, axis=1)).astype(bf16)
        o = mixed[rows, :].astype(f32) + o_s[rows, :].astype(f32)
        prod = dol_b.astype(f32) * o
        mixed[rows, :] = dol_b
        dolt[:, rows] = dol_b.T
        packed = jnp.zeros((BLOCK, 128), f32)
        for head in range(H):
            part = prod[:, (head // 2) * 128 : (head // 2 + 1) * 128]
            keep = first_half if head % 2 == 0 else jnp.logical_not(first_half)
            delta = jnp.sum(jnp.where(keep, part, 0.0), axis=1, keepdims=True)
            for k, piece in enumerate(pieces_of(jnp.broadcast_to(-delta, (BLOCK, 128)), 3)):
                packed = jnp.where(lane_q == 4 * head + k, piece, packed)
        delta_s[rows, :] = packed.astype(bf16)
        ticks("post", b)
        return sums[0] + col_sum8(d_second * unit), sums[1] + col_sum8(d_second)

    def feed_out(b, _):
        rows = pl.ds(pl.multiple_of(b * BLOCK, BLOCK), BLOCK)
        second_s[rows, :] = acc_s[rows, :].astype(bf16)
        return 0

    lax.fori_loop(0, NB, feed_out, 0)
    layer_copies[0].start()
    zero8 = jnp.zeros((8, D), f32)
    gain2_sum, shift2_sum = (zero8, zero8)
    for b in range(NB):
        gain2_sum, shift2_sum = feed_post(b, (gain2_sum, shift2_sum))
    for r in range(D // BLOCK):
        rows = slice(r * BLOCK, (r + 1) * BLOCK)
        g_s[rows, 2 * FF : 2 * FF + D] = dot_nn(secondt[rows, :], act_s[...]).astype(bf16)

    ticks("go", 0)

    small_ref[...] = jnp.zeros_like(small_ref)
    NK = R // KC
    lane_w = (lane_q == 0) | (lane_q == 3)

    def seen(b, j):
        return dict(enumerate(key_chunks(b - 1))).get(j, (0, 0))[1] if b else 0

    def gather(start, old, size, value):
        rows = slice(start, start + DH)
        if old:
            acc_s[rows, 0:old] += value[:, 0:old]
        if old < size:
            acc_s[rows, old:size] = value[:, old:size]

    def bwd_pair(p, slope_sums):
        lanes = pl.ds(pl.multiple_of(p * 128, 128), 128)
        for b in range(NB):
            rows = slice(b * BLOCK, (b + 1) * BLOCK)
            e_ref = probs[b]
            end_b = jnp.broadcast_to(end_row(M + b * BLOCK, BLOCK), (128, BLOCK)).T
            weight = jnp.where(lane_w, 1.0, jnp.where(lane_q == 7, -end_b, 0.0))
            dol_pair = mixed[rows, lanes]
            outs = []
            for half in range(2):
                head = 2 * p + half
                keep = first_half if half == 0 else jnp.logical_not(first_half)
                d_half = jnp.where(keep, dol_pair, jnp.zeros_like(dol_pair))
                delta = delta_s[rows, :]
                delta = jnp.where(lane_q // 4 == head, delta, jnp.zeros_like(delta))
                d_full = jnp.concatenate([d_half, delta], axis=1)
                hrows = pl.ds(pl.multiple_of(head * DH, DH), DH)
                q_t = qt[hrows, rows]
                d_t = dolt[hrows, rows]
                dqx = jnp.zeros((BLOCK, 256), f32)
                for j, (k0, kn) in enumerate(key_chunks(b)):
                    e = e_ref[head, :, k0 : k0 + kn]
                    ds = (dot_nt(d_full, value_full(lanes, k0, kn)) * e.astype(f32)).astype(bf16)
                    dqx = dqx + dot_nn(ds, key_full(lanes, k0, kn))
                    at_k = j * 128 + half * DH
                    gather(at_k, seen(b, j), kn, dot_nn(q_t, ds))
                    at_v = (NK + j) * 128 + half * DH
                    gather(at_v, seen(b, j), kn, dot_nn(d_t, e))
                outs.append(dqx[:, 0:128])
                tail = jnp.sum(dqx[:, 128:256] * weight, axis=0, keepdims=True)
                here = lax.broadcasted_iota(jnp.int32, (8, 128), 0) == head
                slope_sums = slope_sums + jnp.where(here, tail, 0.0)
            dq = jnp.where(first_half, outs[0], outs[1]) * (1.0 / math.sqrt(DH))
            q_s[rows, lanes] = dq.astype(bf16)
            for k in range(HP):
                if ("bwd", k * NB + b) in SCHEDULE:

                    @pl.when(p == k)
                    def _():
                        ticks("bwd", k * NB + b)

        for j in range(NK):
            dk = (acc_s[j * 128 : (j + 1) * 128, :] * LN2).astype(bf16).T
            k_s[j * KC : (j + 1) * KC, lanes] = dk
            dv = acc_s[(NK + j) * 128 : (NK + j + 1) * 128, :].astype(bf16).T
            v_s[j * KC : (j + 1) * KC, lanes] = dv
        for r in range(D // BLOCK):
            rows = slice(r * BLOCK, (r + 1) * BLOCK)
            gq = dot_nn(keyint[rows, M:], q_s[:, lanes]).astype(bf16)
            pair = jnp.concatenate([k_s[:, lanes], v_s[:, lanes]], axis=1)
            gkv = dot_nn(keyint[rows, :], pair).astype(bf16)
            col = 2 * FF + D + p * 384
            g_s[rows, pl.ds(pl.multiple_of(col, 128), 128)] = gq
            g_s[rows, pl.ds(pl.multiple_of(col + 128, 128), 256)] = gkv
        ticks_in_loop("pair", p, HP)
        return slope_sums

    slope_sums = lax.fori_loop(0, HP, bwd_pair, jnp.zeros((8, 128), f32))

    def key_back(key_rows):
        return dot_nt(k_s[key_rows, :], wk_ref[...]) + dot_nt(v_s[key_rows, :], wv_ref[...])

    def mem_back(b, sums):
        rows = pl.ds(pl.multiple_of(b * BLOCK, BLOCK), BLOCK)
        unit, _ = norm_stats(mem_ref[rows, :].astype(f32))
        d_rows = key_back(rows)
        return sums[0] + col_sum8(d_rows * unit), sums[1] + col_sum8(d_rows)

    def slot_back(b, sums):
        rows = pl.ds(pl.multiple_of(b * BLOCK, BLOCK), BLOCK)
        key_rows = pl.ds(pl.multiple_of(b * BLOCK + M, BLOCK), BLOCK)
        unit, scale = norm_stats(x_ref[rows, :].astype(f32))
        d_rows = key_back(key_rows) + dot_nt(q_s[rows, :], wq_ref[...])
        grad = norm_back(unit, scale, d_rows * gain1) + dres[rows, :]
        second_s[rows, :] = grad.astype(bf16)
        return sums[0] + col_sum8(d_rows * unit), sums[1] + col_sum8(d_rows)

    layer_copies[0].wait()
    for copy in layer_copies[1:]:
        if talk:
            copy.wait_send()
        else:
            copy.wait()
    sums = (zero8, zero8)
    for i in range(nslot):
        sums = slot_back(other * nslot + i, sums)
        ingrad_copies[1 + i].start()
        ticks("tail", i)
    for i in range(MB):
        sums = mem_back(i, sums)
        ticks("tail", nslot + i)
    for i in range(nslot):
        sums = slot_back(blk * nslot + i, sums)
        ticks("tail", nslot + MB + i)
    ingrad_copies[0].start()
    gain1_sum, shift1_sum = sums
    sm_own[0] = jnp.zeros_like(sm_own[0])
    for k, part in enumerate((gain1_sum, shift1_sum, gain2_sum, shift2_sum)):
        sm_own[0, k : k + 1, :] = jnp.sum(part, axis=0, keepdims=True)
    total = jnp.broadcast_to(jnp.sum(slope_sums, axis=1, keepdims=True), (8, 128))
    sm_own[0, 4:5, 0:128] = jnp.sum(
        jnp.where(lax.broadcasted_iota(jnp.int32, (8, 128), 0)
                  == lax.broadcasted_iota(jnp.int32, (8, 128), 1), total, 0.0),
        axis=0, keepdims=True)

    if talk:
        k = 0
        for level, devices in enumerate(
            ([sibling], [d for d, _ in z_peers], [d for d, _ in xy_peers])
        ):
            hops = []
            for device in devices:
                hops.append(
                    remote(sm_own.at[level], sm_in.at[k], sm_send.at[k], sm_recv.at[k], device)
                )
                k += 1
            for hop in hops:
                hop.start()
            ticks("small", level)
            total = sm_own[level]
            for i, hop in enumerate(hops):
                hop.wait()
                total = total + sm_in[k - len(hops) + i]
            sm_own[level + 1] = total
        small_ref[...] = sm_own[3]
    else:
        for level in range(3):
            ticks("small", level)
        small_ref[...] = sm_own[0]
    for i in range(10):
        ticks("last", i)
    ingrad_copies[0].wait()
    if not talk:
        for u in range(len(units)):
            unit_out(u).start()
            unit_out(u).wait()
    if talk:
        for copy in exchange:
            copy.wait_send()
        for copy in layer_copies[1:]:
            copy.wait_recv()
    for copy in ingrad_copies[1:]:
        copy.wait()


SPLIT = (2, 2, 2, 2)
ORDERS = ('axyb', 'yzx', 'yxz', 'yzx', 'xyab', 'yzx', 'ayxb', 'ayxb', 'xyab', 'yxab', 'zp', 'pz', 'zp')
SCHEDULE = {
    ('chunk', 0): ((0, 0), (1, 0)),
    ('chunk', 1): ((0, 1), (3, 0), (2, 0)),
    ('feed', 9): ((1, 1),),
    ('chunk', 2): ((5, 0), (3, 1), (4, 0)),
    ('feed', 13): ((0, 2), (2, 1)),
    ('feed', 15): ((1, 2),),
    ('chunk', 3): ((6, 0), (5, 1), (7, 0)),
    ('post', 0): ((4, 1),),
    ('post', 1): ((0, 3), (3, 2)),
    ('go', 0): ((6, 1), (8, 0)),
    ('bwd', 0): ((1, 3), (7, 1), (2, 2)),
    ('bwd', 1): ((4, 2),),
    ('bwd', 2): ((0, 4), (5, 2), (3, 3), (8, 1)),
    ('bwd', 3): ((1, 4), (6, 2)),
    ('pair', 0): ((9, 0), (3, 4), (4, 3), (2, 3)),
    ('bwd', 4): ((-1, 0), (0, 5), (7, 2)),
    ('bwd', 5): ((1, 5), (6, 3), (8, 2)),
    ('bwd', 6): ((-1, 1), (9, 1), (5, 3), (3, 5), (4, 4)),
    ('bwd', 7): ((0, 6), (7, 3), (2, 4)),
    ('pair', 1): ((-1, 2), (6, 4), (8, 3), (10, 0)),
    ('bwd', 8): ((9, 2),),
    ('bwd', 9): ((-1, 3), (0, 7), (1, 6)),
    ('bwd', 10): ((5, 4), (3, 6), (7, 4), (10, 1)),
    ('bwd', 11): ((4, 5), (8, 4)),
    ('pair', 2): ((6, 5), (9, 3), (11, 0), (2, 5)),
    ('bwd', 12): ((1, 7), (7, 5)),
    ('bwd', 14): ((0, 8), (3, 7), (11, 1)),
    ('bwd', 15): ((1, 8), (9, 4), (5, 5), (4, 6), (10, 2)),
    ('pair', 3): ((6, 6), (12, 0), (3, 8), (7, 6), (8, 5), (2, 6)),
    ('tail', 1): ((0, 9), (6, 7), (9, 5), (12, 1), (11, 2), (10, 3)),
    ('tail', 2): ((5, 6), (4, 7), (7, 7)),
    ('tail', 3): ((0, 10), (8, 6), (2, 7)),
    ('tail', 4): ((6, 8), (9, 6)),
    ('tail', 5): ((2, 8),),
    ('small', 0): ((5, 7), (12, 2), (4, 8), (8, 7), (11, 3)),
    ('small', 1): ((6, 9), (9, 7), (7, 8)),
    ('small', 2): ((5, 8), (12, 3), (8, 8), (11, 4), (10, 4)),
    ('last', 0): ((6, 10), (9, 8), (12, 4), (4, 9), (7, 9), (8, 9), (11, 5), (10, 5)),
    ('last', 1): ((9, 9), (12, 5), (4, 10), (7, 10), (8, 10), (11, 6), (10, 6)),
    ('last', 2): ((9, 10), (12, 6)),
}


def layer_call(counts, lengths, tokens, memory, ends, grad, params, talk=True):
    _, SH, D = tokens.shape
    MH = memory.shape[1]
    S, M = 2 * SH, 2 * MH
    R = M + S
    gain1, shift1, wq, wk, wv, wo, slopes, gain2, shift2, w1, w2 = params
    FF = w1.shape[1]
    H = slopes.shape[0]
    vmem = pl.BlockSpec(memory_space=pltpu.VMEM)
    smem = pl.BlockSpec(memory_space=pltpu.SMEM)
    hbm = pl.BlockSpec(memory_space=pl.ANY)
    V = pltpu.VMEM
    G = 2 * FF + 4 * D
    units = len(ORDERS)
    dma = pltpu.SemaphoreType.DMA
    scratch = [
        V((S, D), bf16),
        V((M, D), bf16),
        V((S, D), bf16),
        V((2, 1, MH + SH), jnp.int32),
        V((D, D), bf16),
        V((D, D), bf16),
        V((D, D), bf16),
        V((D, D), bf16),
        V((D, FF), bf16),
        V((FF, D), bf16),
        V((D, R), bf16),
        V((R, D), bf16),
        V((R, D), bf16),
        V((R, 128), bf16),
        V((S, D), bf16),
        V((D, S), bf16),
        V((S, 128), f32),
        V((S, D), bf16),
        V((S, D), bf16),
        V((S, D), bf16),
        V((D, S), bf16),
        V((D, S), bf16),
        V((S, 512), bf16),
        V((S, 512), bf16),
        V((S, D), f32),
        V((S, D), f32),
        V((D, S), bf16),
        V((S, 128), bf16),
        V((D, G), bf16),
        V((D // 2, G), bf16),
        V((D // 2 - 16, G), bf16),
        V((4, 8, D), f32),
        V((7, 8, D), f32),
        dma((16,)),
        dma((12,)),
        dma((12,)),
        dma((units, 14)),
        dma((units, 14)),
        dma((7,)),
        dma((7,)),
        dma((units,)),
    ]
    for b in range(S // BLOCK):
        scratch.append(V((H, BLOCK, M + (b + 1) * BLOCK), bf16))
    shapes = (
        jax.ShapeDtypeStruct((2, SH, D), bf16),
        jax.ShapeDtypeStruct((2, SH, D), bf16),
        jax.ShapeDtypeStruct((D, G), bf16),
        jax.ShapeDtypeStruct((8, D), f32),
    )
    extra = {"collective_id": 1, "has_side_effects": True} if talk else {}
    return pl.pallas_call(
        functools.partial(layer_kernel, talk),
        out_shape=shapes,
        in_specs=[smem] * 3 + [hbm] * 4 + [vmem] * 4 + [hbm] * 6,
        out_specs=[hbm, hbm, hbm, vmem],
        scratch_shapes=scratch,
        compiler_params=pltpu.CompilerParams(
            vmem_limit_bytes=64 * 1024 * 1024 - 65536, **extra
        ),
        name="layer",
    )(
        counts, lengths, slopes, tokens, memory, ends, grad,
        gain1.reshape(1, D), shift1.reshape(1, D), gain2.reshape(1, D), shift2.reshape(1, D),
        wq, wk, wv, wo, w1, w2,
    )


def layer_norm(values, gain, shift):
    centred = values - jnp.mean(values, axis=-1, keepdims=True)
    spread = jnp.mean(centred * centred, axis=-1, keepdims=True)
    return centred * lax.rsqrt(spread + epsilon) * gain + shift


def block_scores(
    q_heads, key_block, q_ends, key_order, key_ends, q_index, head_slopes, score_scale
):
    scores = (
        jnp.einsum("qhd,khd->hqk", q_heads, key_block, preferred_element_type=jnp.float32)
        * score_scale
    )
    distance = (q_ends[:, None] - key_ends[None, :]).astype(jnp.float32)
    scores = scores - head_slopes[:, None, None] * distance[None]
    allowed = key_order[None, :] <= q_index[:, None]
    return (jnp.where(allowed[None], scores, -1e30), distance)


def spread_device(
    tokens,
    memory,
    segment_ends,
    memory_ends,
    segment_counts,
    memory_lengths,
    first_gain,
    first_shift,
    query_weight,
    key_weight,
    value_weight,
    out_weight,
    head_slopes,
    second_gain,
    second_shift,
    hidden_weight,
    output_weight,
    output_grad,
):
    seq_count, slot_count, model_width = tokens.shape
    mem_count = memory.shape[1]
    head_count = head_slopes.shape[0]
    head_dim = model_width // head_count
    score_scale = 1.0 / math.sqrt(head_dim)
    key_rows = mem_count + slot_count
    blocks = lax.axis_size("blk")
    my_block = lax.axis_index("blk")
    x_float = tokens.astype(jnp.float32)
    mem_float = memory.astype(jnp.float32)
    normed = layer_norm(x_float, first_gain, first_shift).astype(jnp.bfloat16)
    mem_normed = layer_norm(mem_float, first_gain, first_shift).astype(jnp.bfloat16)
    key_input = jnp.concatenate([mem_normed, normed], axis=1)
    query = jnp.einsum(
        "std,de->ste", normed, query_weight, preferred_element_type=jnp.float32
    ).astype(jnp.bfloat16)
    pair_weight = jnp.concatenate([key_weight, value_weight], axis=1)
    key_value = jnp.einsum(
        "srd,de->rse", key_input, pair_weight, preferred_element_type=jnp.float32
    ).astype(jnp.bfloat16)
    mem_index = my_block * mem_count + jnp.arange(mem_count, dtype=jnp.int32)
    slot_index = my_block * slot_count + jnp.arange(slot_count, dtype=jnp.int32)
    mem_order = jnp.where(
        mem_index[None, :] >= mem_count * blocks - memory_lengths[:, None], -1, far_order
    )
    slot_order = jnp.where(
        slot_index[None, :] < segment_counts[:, None], slot_index[None, :], far_order
    )
    key_meta = jnp.stack(
        [
            jnp.concatenate([mem_order, slot_order], axis=1),
            jnp.concatenate([memory_ends, segment_ends], axis=1),
        ]
    )
    all_pairs, all_meta = (
        lax.all_gather(key_value, "blk", axis=0, tiled=True),
        lax.all_gather(key_meta, "blk", axis=2, tiled=True),
    )
    query_heads = query.reshape(seq_count, slot_count, head_count, head_dim)

    def pick(seq_index):
        pair_rows = lax.dynamic_index_in_dim(all_pairs, seq_index, 1, keepdims=False)
        meta_rows = lax.dynamic_index_in_dim(all_meta, seq_index, 1, keepdims=False)
        key_heads = pair_rows[:, :model_width].reshape(-1, key_rows, head_count, head_dim)
        value_heads = pair_rows[:, model_width:].reshape(-1, key_rows, head_count, head_dim)
        return (
            key_heads,
            value_heads,
            meta_rows[0].reshape(-1, key_rows),
            meta_rows[1].reshape(-1, key_rows),
        )

    def attend(seq_index):
        key_heads, value_heads, key_order, key_ends = pick(seq_index)
        q_heads = lax.dynamic_index_in_dim(query_heads, seq_index, 0, keepdims=False)
        q_ends = lax.dynamic_index_in_dim(segment_ends, seq_index, 0, keepdims=False)

        def stats_step(running, pieces):
            scores = block_scores(
                q_heads,
                pieces[0],
                q_ends,
                pieces[1],
                pieces[2],
                slot_index,
                head_slopes,
                score_scale,
            )[0]
            running_max = jnp.maximum(running[0], jnp.max(scores, axis=-1))
            running_sum = running[1] * jnp.exp(running[0] - running_max) + jnp.sum(
                jnp.exp(scores - running_max[..., None]), axis=-1
            )
            return ((running_max, running_sum), None)

        start_max = jnp.full((head_count, slot_count), -jnp.inf, jnp.float32)
        (top_max, top_sum), _ = lax.scan(
            stats_step, (start_max, jnp.zeros_like(start_max)), (key_heads, key_order, key_ends)
        )
        log_total = top_max + jnp.log(top_sum)

        def out_step(summed, pieces):
            scores = block_scores(
                q_heads,
                pieces[0],
                q_ends,
                pieces[1],
                pieces[2],
                slot_index,
                head_slopes,
                score_scale,
            )[0]
            attn_probs = jnp.exp(scores - log_total[..., None]).astype(jnp.bfloat16)
            return (
                summed
                + jnp.einsum(
                    "hqk,khd->qhd", attn_probs, pieces[3], preferred_element_type=jnp.float32
                ),
                None,
            )

        start_out = jnp.zeros((slot_count, head_count, head_dim), jnp.float32)
        mixed_heads, _ = lax.scan(
            out_step, start_out, (key_heads, key_order, key_ends, value_heads)
        )
        return (mixed_heads, log_total)

    mixed_all, log_totals = lax.map(attend, jnp.arange(seq_count))
    mixed_low = mixed_all.reshape(seq_count, slot_count, model_width).astype(jnp.bfloat16)
    residual = x_float + jnp.einsum(
        "std,de->ste", mixed_low, out_weight, preferred_element_type=jnp.float32
    )
    second_low = layer_norm(residual, second_gain, second_shift).astype(jnp.bfloat16)
    hidden_pre = jnp.einsum(
        "std,df->stf", second_low, hidden_weight, preferred_element_type=jnp.float32
    )
    act_low = jax.nn.gelu(hidden_pre, approximate=False).astype(jnp.bfloat16)
    layer_out = (
        residual
        + jnp.einsum("stf,fd->std", act_low, output_weight, preferred_element_type=jnp.float32)
    ).astype(jnp.bfloat16)
    grad_output_w = jnp.einsum(
        "stf,std->fd", act_low, output_grad, preferred_element_type=jnp.float32
    )
    d_act = jnp.einsum(
        "std,fd->stf", output_grad, output_weight, preferred_element_type=jnp.float32
    )
    _, gelu_pull = jax.vjp(lambda inner: jax.nn.gelu(inner, approximate=False), hidden_pre)
    d_pre_low = gelu_pull(d_act)[0].astype(jnp.bfloat16)
    grad_hidden_w = jnp.einsum(
        "std,stf->df", second_low, d_pre_low, preferred_element_type=jnp.float32
    )
    d_second = jnp.einsum(
        "stf,df->std", d_pre_low, hidden_weight, preferred_element_type=jnp.float32
    )
    _, second_pull = jax.vjp(layer_norm, residual, second_gain, second_shift)
    d_resid_norm, grad_second_g, grad_second_b = second_pull(d_second)
    d_residual = d_resid_norm + output_grad.astype(jnp.float32)
    d_branch = d_residual.astype(jnp.bfloat16)
    grad_out_w = jnp.einsum("std,ste->de", mixed_low, d_branch, preferred_element_type=jnp.float32)
    d_mixed = jnp.einsum(
        "ste,de->std", d_branch, out_weight, preferred_element_type=jnp.float32
    ).astype(jnp.bfloat16)
    d_mixed_heads = d_mixed.reshape(seq_count, slot_count, head_count, head_dim)

    def query_side(seq_index):
        key_heads, value_heads, key_order, key_ends = pick(seq_index)
        q_heads = lax.dynamic_index_in_dim(query_heads, seq_index, 0, keepdims=False)
        q_ends = lax.dynamic_index_in_dim(segment_ends, seq_index, 0, keepdims=False)
        d_heads = lax.dynamic_index_in_dim(d_mixed_heads, seq_index, 0, keepdims=False)
        log_total = lax.dynamic_index_in_dim(log_totals, seq_index, 0, keepdims=False)

        def probs_of(key_block, order_block, ends_block, value_block):
            scores, distance = block_scores(
                q_heads,
                key_block,
                q_ends,
                order_block,
                ends_block,
                slot_index,
                head_slopes,
                score_scale,
            )
            attn_probs = jnp.exp(scores - log_total[..., None])
            d_probs = jnp.einsum(
                "qhd,khd->hqk", d_heads, value_block, preferred_element_type=jnp.float32
            )
            return (attn_probs, d_probs, distance)

        def delta_step(summed, pieces):
            attn_probs, d_probs, _ = probs_of(pieces[0], pieces[1], pieces[2], pieces[3])
            return (summed + jnp.sum(attn_probs * d_probs, axis=-1), None)

        delta_rows, _ = lax.scan(
            delta_step,
            jnp.zeros((head_count, slot_count), jnp.float32),
            (key_heads, key_order, key_ends, value_heads),
        )

        def grad_step(running, pieces):
            attn_probs, d_probs, distance = probs_of(pieces[0], pieces[1], pieces[2], pieces[3])
            d_scores = (attn_probs * (d_probs - delta_rows[..., None])).astype(jnp.bfloat16)
            d_query = running[0] + jnp.einsum(
                "hqk,khd->qhd", d_scores, pieces[0], preferred_element_type=jnp.float32
            )
            d_slopes = running[1] - jnp.sum(
                d_scores.astype(jnp.float32) * distance[None], axis=(1, 2)
            )
            return ((d_query, d_slopes), None)

        start_grads = (
            jnp.zeros((slot_count, head_count, head_dim), jnp.float32),
            jnp.zeros((head_count,), jnp.float32),
        )
        (d_query, d_slopes), _ = lax.scan(
            grad_step, start_grads, (key_heads, key_order, key_ends, value_heads)
        )
        return (d_query * score_scale, delta_rows, d_slopes)

    d_query_all, delta_all, slope_parts = lax.map(query_side, jnp.arange(seq_count))
    grad_slopes = jnp.sum(slope_parts, axis=0)
    d_query_low = d_query_all.reshape(seq_count, slot_count, model_width).astype(jnp.bfloat16)

    def pair_terms(
        pair_rows, order_block, ends_block, q_heads, q_ends, q_index, d_heads, log_total, delta_rows
    ):
        key_block = pair_rows[:, :model_width].reshape(key_rows, head_count, head_dim)
        value_block = pair_rows[:, model_width:].reshape(key_rows, head_count, head_dim)
        scores, _ = block_scores(
            q_heads, key_block, q_ends, order_block, ends_block, q_index, head_slopes, score_scale
        )
        attn_probs = jnp.exp(scores - log_total[..., None])
        d_probs = jnp.einsum(
            "qhd,khd->hqk", d_heads, value_block, preferred_element_type=jnp.float32
        )
        d_scores = (attn_probs * (d_probs - delta_rows[..., None])).astype(jnp.bfloat16)
        d_value = jnp.einsum(
            "hqk,qhd->khd",
            attn_probs.astype(jnp.bfloat16),
            d_heads,
            preferred_element_type=jnp.float32,
        )
        d_key = (
            jnp.einsum("hqk,qhd->khd", d_scores, q_heads, preferred_element_type=jnp.float32)
            * score_scale
        )
        return jnp.concatenate(
            [d_key.reshape(key_rows, model_width), d_value.reshape(key_rows, model_width)], axis=1
        )

    def one_block(block_index):
        offset = block_index * key_rows
        pair_block = lax.dynamic_slice_in_dim(all_pairs, offset, key_rows, 0)
        meta_block = lax.dynamic_slice_in_dim(all_meta, offset, key_rows, 2)
        return jax.vmap(pair_terms, in_axes=(1, 0, 0, 0, 0, None, 0, 0, 0), out_axes=1)(
            pair_block,
            meta_block[0],
            meta_block[1],
            query_heads,
            segment_ends,
            slot_index,
            d_mixed_heads,
            log_totals,
            delta_all,
        )

    pieces = lax.map(one_block, jnp.arange(lax.axis_size("blk") * key_rows // key_rows))
    pair_grads = lax.psum_scatter(
        pieces.reshape(lax.axis_size("blk") * key_rows, seq_count, 2 * model_width).astype(
            jnp.bfloat16
        ),
        "blk",
        scatter_dimension=0,
        tiled=True,
    )
    grad_pair_w = jnp.einsum(
        "srd,rse->de", key_input, pair_grads, preferred_element_type=jnp.float32
    )
    grad_key_w = grad_pair_w[:, :model_width]
    grad_value_w = grad_pair_w[:, model_width:]
    d_key_input = jnp.einsum(
        "rse,de->srd", pair_grads, pair_weight, preferred_element_type=jnp.float32
    )
    grad_query_w = jnp.einsum(
        "std,ste->de", normed, d_query_low, preferred_element_type=jnp.float32
    )
    d_normed = (
        jnp.einsum("ste,de->std", d_query_low, query_weight, preferred_element_type=jnp.float32)
        + d_key_input[:, mem_count:]
    )
    _, first_pull = jax.vjp(layer_norm, x_float, first_gain, first_shift)
    d_tokens, gain_slots, shift_slots = first_pull(d_normed)
    _, mem_pull = jax.vjp(
        lambda gain, shift: layer_norm(mem_float, gain, shift), first_gain, first_shift
    )
    gain_mem, shift_mem = mem_pull(d_key_input[:, :mem_count])
    input_grad = (d_tokens + d_residual).astype(jnp.bfloat16)
    grad_first_g = gain_slots + gain_mem
    grad_first_b = shift_slots + shift_mem
    summed = lax.psum(
        (
            grad_first_g,
            grad_first_b,
            grad_query_w,
            grad_key_w,
            grad_value_w,
            grad_out_w,
            grad_slopes,
            grad_second_g,
            grad_second_b,
            grad_hidden_w,
            grad_output_w,
        ),
        ("seq", "blk"),
    )
    return (
        layer_out,
        input_grad,
        summed[0],
        summed[1],
        summed[2],
        summed[3],
        summed[4],
        summed[5],
        summed[6],
        summed[7],
        summed[8],
        summed[9],
        summed[10],
    )


def widen_kernel(ga, gb, gc, layer_in, grad_in, small, *outs):
    gw1, gw2, go, gq, gk, gv, layer, grad, gain1, shift1, slopes, gain2, shift2 = outs
    half = ga.shape[1] // 2
    gw1[...] = ga[:, :half].astype(f32)
    gw2[...] = ga[:, half:].astype(f32).T
    go[...] = gb[...].astype(f32)
    for i, out in enumerate((gq, gk, gv)):
        out[...] = gc[:, i * 128 : (i + 1) * 128].astype(f32)
    layer[...] = layer_in[...]
    grad[...] = grad_in[...]

    @pl.when((pl.program_id(0) == 0) & (pl.program_id(1) == 0))
    def _():
        for i, out in enumerate((gain1, shift1, gain2, shift2)):
            out[...] = small[i : i + 1, :]
        slopes[...] = small[4:5, 0:8]


def widen(grads, layer, in_grad, small, D, FF):
    RB = D // 2
    LB = layer.shape[0] // 8
    out = [
        ((D, FF), (RB, 512), lambda c, r: (r, c)),
        ((FF, D), (512, RB), lambda c, r: (c, r)),
        ((D, D), (RB, 128), lambda c, r: (r, c)),
        ((D, D), (RB, 128), lambda c, r: (r, c)),
        ((D, D), (RB, 128), lambda c, r: (r, c)),
        ((D, D), (RB, 128), lambda c, r: (r, c)),
        ((8 * LB, D), (LB, D), lambda c, r: (2 * c + r, 0)),
        ((8 * LB, D), (LB, D), lambda c, r: (2 * c + r, 0)),
    ]
    kinds = [f32] * 6 + [bf16] * 2
    shapes = [jax.ShapeDtypeStruct(shape, kind) for (shape, _, _), kind in zip(out, kinds)]
    specs = [pl.BlockSpec(block, index) for _, block, index in out]
    for width in (D, D, 8, D, D):
        shapes.append(jax.ShapeDtypeStruct((1, width), f32))
        specs.append(pl.BlockSpec((1, width), lambda c, r: (0, 0)))
    go_at = 2 * FF // 128
    head_at = (2 * FF + D) // 384
    return pl.pallas_call(
        widen_kernel,
        grid=(4, 2),
        out_shape=shapes,
        in_specs=[
            pl.BlockSpec((RB, 1024), lambda c, r: (r, c)),
            pl.BlockSpec((RB, 128), lambda c, r: (r, go_at + c)),
            pl.BlockSpec((RB, 384), lambda c, r: (r, head_at + c)),
            pl.BlockSpec((LB, D), lambda c, r: (2 * c + r, 0)),
            pl.BlockSpec((LB, D), lambda c, r: (2 * c + r, 0)),
            pl.BlockSpec((8, D), lambda c, r: (0, 0)),
        ],
        out_specs=specs,
        compiler_params=pltpu.CompilerParams(vmem_limit_bytes=62 * 1024 * 1024),
        name="widen",
    )(grads, grads, grads, layer, in_grad, small)


def whole_device(*args):
    tokens, memory, segment_ends, memory_ends, counts, lengths = args[:6]
    params = args[6:17]
    output_grad = args[17]
    D = tokens.shape[2]
    FF = params[9].shape[1]
    H = params[6].shape[0]
    ends = jnp.concatenate([memory_ends, segment_ends], axis=1)[:, None]
    layer, in_grad, grads, small = layer_call(
        counts, lengths, tokens, memory, ends, output_grad, params
    )
    gw1, gw2, go, gq, gk, gv, layer, in_grad, *rows = widen(
        grads, layer.reshape(-1, D), in_grad.reshape(-1, D), small, D, FF
    )
    gain1, shift1, slopes, gain2, shift2 = (row[0] for row in rows)
    return (
        layer.reshape(tokens.shape),
        in_grad.reshape(tokens.shape),
        gain1,
        shift1,
        gq,
        gk,
        gv,
        go,
        slopes,
        gain2,
        shift2,
        gw1,
        gw2,
    )


def per_device(*args):
    whole = args[0].shape[0] == lax.axis_size("blk") == 2 and lax.axis_size("seq") == 16
    if whole:
        return whole_device(*args)
    return spread_device(*args)


def solution(mesh):
    placed = (
        P("seq", "blk", None),
        P("seq", "blk", None),
        P("seq", "blk"),
        P("seq", "blk"),
        P("seq"),
        P("seq"),
        P(),
        P(),
        P(),
        P(),
        P(),
        P(),
        P(),
        P(),
        P(),
        P(),
        P(),
        P("seq", "blk", None),
    )
    return jax.shard_map(
        per_device,
        mesh=mesh,
        in_specs=placed,
        out_specs=(
            P("seq", "blk", None),
            P("seq", "blk", None),
            P(),
            P(),
            P(),
            P(),
            P(),
            P(),
            P(),
            P(),
            P(),
            P(),
            P(),
        ),
        check_vma=False,
    )
```

```python
import functools
import math

import jax
import jax.numpy as jnp
from jax import lax
from jax.experimental import pallas as pl
from jax.experimental.pallas import tpu as pltpu
from jax.sharding import PartitionSpec as P

epsilon = 1e-05
far_order = 1073741824
f32 = jnp.float32
bf16 = jnp.bfloat16
BLOCK = 256
LOG2E = 1.4426950408889634
LN2 = 0.6931471805599453


def dot_nn(left, right):
    return lax.dot_general(left, right, (((1,), (0,)), ((), ())), preferred_element_type=f32)


def dot_nt(left, right):
    return lax.dot_general(left, right, (((1,), (1,)), ((), ())), preferred_element_type=f32)


def norm_stats(values):
    centred = values - jnp.mean(values, axis=-1, keepdims=True)
    spread = jnp.mean(centred * centred, axis=-1, keepdims=True)
    scale = lax.rsqrt(spread + epsilon)
    return centred * scale, scale


def norm_back(unit, scale, grad_unit):
    mean_grad = jnp.mean(grad_unit, axis=-1, keepdims=True)
    mean_prod = jnp.mean(grad_unit * unit, axis=-1, keepdims=True)
    return (grad_unit - mean_grad - unit * mean_prod) * scale


def pieces_of(value, count):
    out = []
    for _ in range(count):
        part = value.astype(bf16).astype(f32)
        out.append(part)
        value = value - part
    return out


ERFC_P = 0.4
ERFC_C = (0.22567586600780487, 0.2256695181131363, 0.2078438550233841, 0.16853390634059906, 0.1414608359336853, -0.005667657125741243, 0.16915477812290192, -0.18294358253479004, 0.050272583961486816)


def gelu_both(x):
    cdf = 0.5 * lax.erf(x * math.sqrt(0.5)) + 0.5
    ex = jnp.exp2((x * x) * (-0.5 * LOG2E))
    return x * cdf, cdf + x * (ex * (1.0 / math.sqrt(2.0 * math.pi)))


def col_sum8(value):
    return jnp.sum(value.reshape(-1, 8, value.shape[-1]), axis=0)


def flip(bit):
    return 1 - bit


def layer_kernel(
    talk,
    counts_ref,
    lengths_ref,
    slopes_ref,
    tokens_ref,
    memory_ref,
    ends_ref,
    grad_ref,
    gain1_ref,
    shift1_ref,
    gain2_ref,
    shift2_ref,
    wq_hbm,
    wk_hbm,
    wv_hbm,
    wo_hbm,
    w1_hbm,
    w2_hbm,
    layer_hbm,
    ingrad_hbm,
    grads_hbm,
    small_ref,
    x_ref,
    mem_ref,
    og_ref,
    ends_s,
    wq_ref,
    wk_ref,
    wv_ref,
    wo_ref,
    w1_ref,
    w2_ref,
    keyint,
    k_s,
    v_s,
    kx,
    q_s,
    qt,
    rl_s,
    o_s,
    mixed,
    second_s,
    secondt,
    ogt,
    act_s,
    dpre_s,
    acc_s,
    dres,
    dolt,
    delta_s,
    g_s,
    rc_s,
    r1_s,
    sm_own,
    sm_in,
    load_sem,
    ex_send,
    ex_recv,
    ar_send,
    ar_recv,
    sm_send,
    sm_recv,
    out_sem,
    *probs,
):
    S, D = x_ref.shape
    M = mem_ref.shape[0]
    R = M + S
    FF = w1_ref.shape[1]
    H = slopes_ref.shape[0]
    DH = D // H
    HP = H // 2
    NB = S // BLOCK
    MB = M // BLOCK
    SH = S // 2
    MH = M // 2
    KC = 512
    CH = 512
    NC = FF // CH

    if talk:
        seq = lax.axis_index("seq")
        blk = lax.axis_index("blk")
    else:
        seq = 0
        blk = 0
    core = seq % 2
    why = (seq // 2) % 2
    zed = seq // 4

    def at(z=None, y=None, c=None, x=None):
        z = zed if z is None else z
        y = why if y is None else y
        c = core if c is None else c
        return {"seq": z * 4 + y * 2 + c, "blk": blk if x is None else x}

    sibling = at(c=flip(core))
    partner = at(x=flip(blk))
    z_to = [zed + 1 - 2 * (zed % 2), (zed + 2) % 4, 3 - zed]
    z_peers = [(at(z=z), z) for z in z_to]
    plane = blk * 2 + why
    xy_peers = [
        (at(y=flip(why)), blk * 2 + flip(why)),
        (at(x=flip(blk)), flip(blk) * 2 + why),
        (at(x=flip(blk), y=flip(why)), flip(blk) * 2 + flip(why)),
    ]

    def remote(src, dst, send, recv, device):
        return pltpu.make_async_remote_copy(
            src_ref=src,
            dst_ref=dst,
            send_sem=send,
            recv_sem=recv,
            device_id=device,
            device_id_type=pl.DeviceIdType.MESH,
        )

    other = 1 - blk

    def half_rows(half, size):
        return pl.ds(pl.multiple_of(half * size, BLOCK), size)

    def slot_piece(part, index, half, i):
        src = tokens_ref if part == 0 else grad_ref
        dst = x_ref if part == 0 else og_ref
        rows = pl.ds(pl.multiple_of(half * SH + i * BLOCK, BLOCK), BLOCK)
        return src.at[index, i * BLOCK : (i + 1) * BLOCK, :], dst.at[rows, :]

    nslot = SH // BLOCK
    loads = [
        (memory_ref.at[blk], mem_ref.at[half_rows(blk, MH), :]),
        (ends_ref.at[blk], ends_s.at[blk]),
        (wk_hbm, wk_ref),
        (wv_hbm, wv_ref),
        (wq_hbm, wq_ref),
    ]
    loads += [slot_piece(0, blk, blk, i) for i in range(nslot)]
    n_first = len(loads)
    loads += [(wo_hbm, wo_ref), (w1_hbm, w1_ref), (w2_hbm, w2_ref)]
    loads += [slot_piece(1, blk, blk, i) for i in range(nslot)]
    copies = [
        pltpu.make_async_copy(src, dst, load_sem.at[i]) for i, (src, dst) in enumerate(loads)
    ]
    sends = [
        (memory_ref.at[other], mem_ref.at[half_rows(blk, MH), :]),
        (ends_ref.at[other], ends_s.at[blk]),
    ]
    sends += [slot_piece(0, other, blk, i) for i in range(nslot)]
    sends += [slot_piece(1, other, blk, i) for i in range(nslot)]
    if talk:
        exchange = [
            remote(src, dst, ex_send.at[i], ex_recv.at[i], partner)
            for i, (src, dst) in enumerate(sends)
        ]
    else:
        local = [
            (memory_ref.at[other], mem_ref.at[half_rows(other, MH), :]),
            (ends_ref.at[other], ends_s.at[other]),
        ]
        local += [slot_piece(0, other, other, i) for i in range(nslot)]
        local += [slot_piece(1, other, other, i) for i in range(nslot)]
        exchange = [
            pltpu.make_async_copy(src, dst, ex_send.at[i]) for i, (src, dst) in enumerate(local)
        ]
    for copy in copies[:n_first]:
        copy.start()
    if talk:
        barrier = pltpu.get_barrier_semaphore()
        greet = [sibling] + [d for d, _ in z_peers] + [d for d, _ in xy_peers]
        for device in greet:
            pl.semaphore_signal(
                barrier, inc=1, device_id=device, device_id_type=pl.DeviceIdType.MESH
            )
        pl.semaphore_wait(barrier, len(greet))
    for copy in exchange:
        copy.start()
    for copy in copies[n_first:]:
        copy.start()

    def arrive(i):
        if talk:
            exchange[i].wait_recv()
        else:
            exchange[i].wait()

    directions = {
        "x": (blk, [(partner, other)]),
        "y": (why, [(at(y=flip(why)), flip(why))]),
        "a": (zed % 2, [(z_peers[0][0], 1 - zed % 2)]),
        "b": (zed // 2, [(z_peers[1][0], 1 - zed // 2)]),
        "z": (zed, z_peers),
        "p": (plane, xy_peers),
    }
    units = []
    for c in range(NC):
        width = 2 * CH // SPLIT[c]
        for i in range(SPLIT[c]):
            units.append((c * 2 * CH + i * width, width))
    units.append((2 * FF, D))
    for p in range(HP):
        units.append((2 * FF + D + p * 384, 384))
    HALF = D // 2

    def rows_at(start, size):
        return pl.ds(pl.multiple_of(start, 16), size)

    def unit_rounds(u):
        start, size, place = core * HALF, HALF, 0
        rounds = []
        for name in ORDERS[u]:
            mine, peers = directions[name]
            piece = size // (len(peers) + 1)
            rounds.append((start, piece, mine, peers, place))
            place += piece * len(peers)
            start, size = start + mine * piece, piece
        return rounds, start, size

    def unit_copies(u, step):
        col, width = units[u]
        cols = slice(col, col + width)
        rounds, start, size = unit_rounds(u)
        n = len(rounds)
        out = []
        if step == 0:
            rows = rows_at((1 - core) * HALF, HALF)
            out.append((g_s.at[rows, cols], rc_s.at[:, cols], sibling))
        elif step <= n:
            begin, piece, _, peers, place = rounds[step - 1]
            for d, (device, index) in enumerate(peers):
                rows = rows_at(begin + index * piece, piece)
                here = slice(place + d * piece, place + (d + 1) * piece)
                out.append((g_s.at[rows, cols], r1_s.at[here, cols], device))
        elif step <= 2 * n:
            level = 2 * n - step
            begin, piece, mine, peers, _ = rounds[level]
            rows = rows_at(begin + mine * piece, piece)
            src = g_s if level == n - 1 else grads_hbm
            for device, _ in peers:
                out.append((src.at[rows, cols], grads_hbm.at[rows, cols], device))
        else:
            rows = rows_at(core * HALF, HALF)
            out.append((grads_hbm.at[rows, cols], grads_hbm.at[rows, cols], sibling))
        first = 0
        for earlier in range(step):
            if 1 <= earlier <= n:
                first += len(rounds[earlier - 1][3])
            elif n < earlier <= 2 * n:
                first += len(rounds[2 * n - earlier][3])
            else:
                first += 1
        return [
            remote(src, dst, ar_send.at[u, first + k], ar_recv.at[u, first + k], device)
            for k, (src, dst, device) in enumerate(out)
        ]

    def unit_add(u, step):
        col, width = units[u]
        cols = slice(col, col + width)
        rounds, _, _ = unit_rounds(u)
        if step == 0:
            begin, piece, places, buffer = core * HALF, HALF, [0], rc_s
        else:
            begin, piece, mine, peers, place = rounds[step - 1]
            begin = begin + mine * piece
            places, buffer = [place + d * piece for d in range(len(peers))], r1_s
        block = min(piece, 64)

        def add(i, _):
            rows = rows_at(begin + i * block, block)
            total = g_s[rows, cols].astype(f32)
            for place in places:
                total = total + buffer[rows_at(place + i * block, block), cols].astype(f32)
            g_s[rows, cols] = total.astype(bf16)
            return 0

        if piece == block:
            add(0, 0)
        else:
            lax.fori_loop(0, piece // block, add, 0)

    def unit_out(u):
        col, width = units[u]
        cols = slice(col, col + width)
        _, start, size = unit_rounds(u)
        rows = rows_at(start, size) if talk else slice(0, D)
        return pltpu.make_async_copy(g_s.at[rows, cols], grads_hbm.at[rows, cols], out_sem.at[u])

    def advance(u, step):
        if not talk:
            return
        n = len(ORDERS[u])
        if step > 0:
            for copy in unit_copies(u, step - 1):
                copy.wait()
            if step - 1 <= n:
                unit_add(u, step - 1)
        if step == n + 1:
            unit_out(u).start()
        if step == n + 2:
            unit_out(u).wait()
        if step < 2 * n + 2:
            for copy in unit_copies(u, step):
                copy.start()

    def ticks(kind, index):
        moves = SCHEDULE.get((kind, index), ())
        if not moves:
            return

        @pl.when(seq >= 0)
        def _():
            for u, step in moves:
                if u < 0:
                    layer_copies[1 + step].start()
                else:
                    advance(u, step)

    def ticks_in_loop(kind, index, count, base=0):
        for k in range(count):
            if (kind, base + k) in SCHEDULE:

                @pl.when(index == k)
                def _():
                    ticks(kind, base + k)

    gain1 = gain1_ref[...]
    shift1 = shift1_ref[...]
    gain2 = gain2_ref[...]
    shift2 = shift2_ref[...]
    count = counts_ref[blk]
    length = lengths_ref[blk]

    def give(result, hbm, k, pieces):
        own = pltpu.make_async_copy(result.at[half_rows(blk, SH), :], hbm.at[blk], load_sem.at[k])
        moves = [own]
        size = SH // pieces
        for i in range(pieces):
            theirs = result.at[pl.ds(pl.multiple_of(other * SH + i * size, size), size), :]
            rows = slice(i * size, (i + 1) * size)
            sem = len(sends) + 4 * k + i
            if talk:
                there = hbm.at[blk, rows, :]
                moves.append(remote(theirs, there, ex_send.at[sem], ex_recv.at[sem], partner))
            else:
                moves.append(
                    pltpu.make_async_copy(theirs, hbm.at[other, rows, :], ex_send.at[sem])
                )
        return moves

    layer_copies = give(second_s, layer_hbm, 0, 4)
    ingrad_copies = give(second_s, ingrad_hbm, 1, nslot)

    def project(normed, key_rows):
        keyint[:, key_rows] = normed.T
        k_s[key_rows, :] = dot_nn(normed, wk_ref[...]).astype(bf16)
        v_s[key_rows, :] = dot_nn(normed, wv_ref[...]).astype(bf16)

    def norm_mem(b):
        rows = pl.ds(pl.multiple_of(b * BLOCK, BLOCK), BLOCK)
        unit, _ = norm_stats(mem_ref[rows, :].astype(f32))
        project((unit * gain1 + shift1).astype(bf16), rows)

    def norm_slot(b):
        rows = pl.ds(pl.multiple_of(b * BLOCK, BLOCK), BLOCK)
        key_rows = pl.ds(pl.multiple_of(b * BLOCK + M, BLOCK), BLOCK)
        unit, _ = norm_stats(x_ref[rows, :].astype(f32))
        normed = (unit * gain1 + shift1).astype(bf16)
        project(normed, key_rows)
        query = (dot_nn(normed, wq_ref[...]) * (LOG2E / math.sqrt(DH))).astype(bf16)
        q_s[rows, :] = query
        qt[:, rows] = query.T

    for copy in copies[:n_first]:
        copy.wait()
    mh = MH // BLOCK
    for i in range(mh):
        norm_mem(blk * mh + i)
    for i in range(nslot):
        norm_slot(blk * nslot + i)
    arrive(0)
    for i in range(mh):
        norm_mem(other * mh + i)
    arrive(1)

    lane = lax.broadcasted_iota(jnp.int32, (128, 128), 1)
    row = lax.broadcasted_iota(jnp.int32, (128, 128), 0)

    def end_row(start, size):
        if start < M:
            half, off = start // MH, start % MH
        else:
            half, off = (start - M) // SH, MH + (start - M) % SH
        return ends_s[half, :, off : off + size].astype(f32)

    for r in range(R // 128):
        end_col = jnp.broadcast_to(end_row(r * 128, 128), (128, 128)).T
        high = jnp.floor(end_col * (1.0 / 256.0)) * 256.0
        index = row + r * 128
        if r * 128 < M:
            valid = index >= M - length
        else:
            valid = index - M < count
        bias = jnp.where(valid, 0.0, -1e30)
        extra = jnp.where(lane < 3, high, jnp.where(lane < 6, end_col - high, bias))
        extra = jnp.where(lane == 7, 1.0, jnp.where(lane > 7, 0.0, extra))
        kx[r * 128 : (r + 1) * 128, :] = extra.astype(bf16)

    for i in range(nslot):
        arrive(2 + i)
        norm_slot(other * nslot + i)

    lane_q = lax.broadcasted_iota(jnp.int32, (BLOCK, 128), 1)
    first_half = lane_q < DH
    lane_row = lax.broadcasted_iota(jnp.int32, (1, 128), 1)

    def key_chunks(b):
        end = M + (b + 1) * BLOCK
        return [(start, min(KC, end - start)) for start in range(0, end, KC)]

    def key_full(lanes, start, size):
        return jnp.concatenate(
            [k_s[start : start + size, lanes], kx[start : start + size, :]], axis=1
        )

    def value_full(lanes, start, size):
        return jnp.concatenate(
            [v_s[start : start + size, lanes], jnp.ones((size, 128), bf16)], axis=1
        )

    def query_extra(head):
        slope = jnp.full((1, 128), slopes_ref[head] * LOG2E, f32)
        s1, s2, s3 = pieces_of(slope, 3)
        where = jnp.where(lane_row >= 3, lane_row - 3, lane_row)
        out = jnp.where(where == 0, s1, jnp.where(where == 1, s2, s3))
        return jnp.where(lane_row < 6, out, jnp.where(lane_row == 6, 1.0, 0.0))

    rl_s[...] = jnp.zeros_like(rl_s)
    for b in range(NB):
        rows = slice(b * BLOCK, (b + 1) * BLOCK)
        e_ref = probs[b]

        def fwd_pair(p, _):
            lanes = pl.ds(pl.multiple_of(p * 128, 128), 128)
            q_pair = q_s[rows, lanes]
            outs = []
            for half in range(2):
                keep = first_half if half == 0 else jnp.logical_not(first_half)
                q_half = jnp.where(keep, q_pair, jnp.zeros_like(q_pair))
                extra = jnp.broadcast_to(query_extra(2 * p + half), (BLOCK, 128)).astype(bf16)
                q_full = jnp.concatenate([q_half, extra], axis=1)
                chunks = key_chunks(b)
                scores = [dot_nt(q_full, key_full(lanes, k0, kn)) for k0, kn in chunks]
                below = lax.broadcasted_iota(
                    jnp.int32, (BLOCK, BLOCK), 1
                ) <= lax.broadcasted_iota(jnp.int32, (BLOCK, BLOCK), 0)
                last = scores[-1]
                cut = last.shape[1] - BLOCK
                diag = jnp.where(below, last[:, cut:], -1e30)
                scores[-1] = jnp.concatenate([last[:, :cut], diag], axis=1) if cut else diag
                top = scores[-1][:, 0:128]
                for part in scores:
                    for k in range(0, part.shape[1], 128):
                        top = jnp.maximum(top, part[:, k : k + 128])
                top = jnp.max(top, axis=1, keepdims=True)
                both = jnp.zeros((BLOCK, 256), f32)
                for part, (k0, kn) in zip(scores, chunks):
                    e = jnp.exp2(part - top).astype(bf16)
                    e_ref[2 * p + half, :, k0 : k0 + kn] = e
                    both = both + dot_nn(e, value_full(lanes, k0, kn))
                outs.append((both[:, 0:128], 1.0 / both[:, 128:256]))
            rl = jnp.where(first_half, outs[0][1], outs[1][1])
            o = jnp.where(first_half, outs[0][0], outs[1][0]) * rl
            packed = jnp.where(lane_q == 2 * p, outs[0][1], rl_s[rows, :])
            rl_s[rows, :] = jnp.where(lane_q == 2 * p + 1, outs[1][1], packed)
            o_low = o.astype(bf16)
            o_s[rows, lanes] = (o - o_low.astype(f32)).astype(bf16)
            mixed[rows, lanes] = o_low
            return 0

        lax.fori_loop(0, HP, fwd_pair, 0, unroll=2)

    for copy in copies[n_first:]:
        copy.wait()
    for i in range(nslot):
        arrive(2 + nslot + i)

    def residual_of(rows):
        return x_ref[rows, :].astype(f32) + dot_nn(mixed[rows, :], wo_ref[...])

    def feed_prep(b, _):
        rows = slice(b * BLOCK, (b + 1) * BLOCK)
        residual = residual_of(rows)
        unit, _ = norm_stats(residual)
        second = (unit * gain2 + shift2).astype(bf16)
        second_s[rows, :] = second
        secondt[:, rows] = second.T
        ogt[:, rows] = og_ref[rows, :].T
        acc_s[rows, :] = residual
        dres[rows, :] = jnp.zeros((BLOCK, D), f32)
        return 0

    for b in range(NB):
        feed_prep(b, 0)
    def feed_chunk(c, _):
        cols = pl.ds(pl.multiple_of(c * CH, CH), CH)
        for b in range(NB):
            rows = slice(b * BLOCK, (b + 1) * BLOCK)
            hidden = dot_nn(second_s[rows, :], w1_ref[:, cols])
            d_act = dot_nt(og_ref[rows, :], w2_ref[cols, :])
            act, slope = gelu_both(hidden)
            act = act.astype(bf16)
            d_pre = (d_act * slope).astype(bf16)
            act_s[rows, :] = act
            dpre_s[rows, :] = d_pre
            acc_s[rows, :] += dot_nn(act, w2_ref[cols, :])
            dres[rows, :] += dot_nt(d_pre, w1_ref[:, cols])
            for k in range(NC):
                if ("feed", k * NB + b) in SCHEDULE:

                    @pl.when(c == k)
                    def _():
                        ticks("feed", k * NB + b)

        for r in range(D // BLOCK):
            rows = slice(r * BLOCK, (r + 1) * BLOCK)
            pre_cols = pl.ds(pl.multiple_of(c * 2 * CH, CH), CH)
            act_cols = pl.ds(pl.multiple_of(c * 2 * CH + CH, CH), CH)
            g_s[rows, pre_cols] = dot_nn(secondt[rows, :], dpre_s[...]).astype(bf16)
            g_s[rows, act_cols] = dot_nn(ogt[rows, :], act_s[...]).astype(bf16)
        ticks_in_loop("chunk", c, NC)
        return 0

    lax.fori_loop(0, NC, feed_chunk, 0)

    def feed_post(b, sums):
        rows = slice(b * BLOCK, (b + 1) * BLOCK)
        unit, scale = norm_stats(residual_of(rows))
        d_second = dres[rows, :]
        d_residual = og_ref[rows, :].astype(f32) + norm_back(unit, scale, d_second * gain2)
        dres[rows, :] = d_residual
        d_branch = d_residual.astype(bf16)
        act_s[rows, :] = d_branch
        secondt[:, rows] = mixed[rows, :].T
        d_mixed = dot_nt(d_branch, wo_ref[...]).astype(bf16).astype(f32)
        rl_b = rl_s[rows, :]
        rl_wide = []
        for p in range(HP):
            first = jnp.broadcast_to(rl_b[:, 2 * p : 2 * p + 1], (BLOCK, 128))
            second = jnp.broadcast_to(rl_b[:, 2 * p + 1 : 2 * p + 2], (BLOCK, 128))
            rl_wide.append(jnp.where(first_half, first, second))
        dol_b = (d_mixed * jnp.concatenate(rl_wide, axis=1)).astype(bf16)
        o = mixed[rows, :].astype(f32) + o_s[rows, :].astype(f32)
        prod = dol_b.astype(f32) * o
        mixed[rows, :] = dol_b
        dolt[:, rows] = dol_b.T
        packed = jnp.zeros((BLOCK, 128), f32)
        for head in range(H):
            part = prod[:, (head // 2) * 128 : (head // 2 + 1) * 128]
            keep = first_half if head % 2 == 0 else jnp.logical_not(first_half)
            delta = jnp.sum(jnp.where(keep, part, 0.0), axis=1, keepdims=True)
            for k, piece in enumerate(pieces_of(jnp.broadcast_to(-delta, (BLOCK, 128)), 3)):
                packed = jnp.where(lane_q == 4 * head + k, piece, packed)
        delta_s[rows, :] = packed.astype(bf16)
        ticks("post", b)
        return sums[0] + col_sum8(d_second * unit), sums[1] + col_sum8(d_second)

    def feed_out(b, _):
        rows = pl.ds(pl.multiple_of(b * BLOCK, BLOCK), BLOCK)
        second_s[rows, :] = acc_s[rows, :].astype(bf16)
        return 0

    lax.fori_loop(0, NB, feed_out, 0)
    layer_copies[0].start()
    zero8 = jnp.zeros((8, D), f32)
    gain2_sum, shift2_sum = (zero8, zero8)
    for b in range(NB):
        gain2_sum, shift2_sum = feed_post(b, (gain2_sum, shift2_sum))
    for r in range(D // BLOCK):
        rows = slice(r * BLOCK, (r + 1) * BLOCK)
        g_s[rows, 2 * FF : 2 * FF + D] = dot_nn(secondt[rows, :], act_s[...]).astype(bf16)

    ticks("go", 0)

    small_ref[...] = jnp.zeros_like(small_ref)
    NK = R // KC
    lane_w = (lane_q == 0) | (lane_q == 3)

    def seen(b, j):
        return dict(enumerate(key_chunks(b - 1))).get(j, (0, 0))[1] if b else 0

    def gather(start, old, size, value):
        rows = slice(start, start + DH)
        if old:
            acc_s[rows, 0:old] += value[:, 0:old]
        if old < size:
            acc_s[rows, old:size] = value[:, old:size]

    def bwd_pair(p, slope_sums):
        lanes = pl.ds(pl.multiple_of(p * 128, 128), 128)
        for b in range(NB):
            rows = slice(b * BLOCK, (b + 1) * BLOCK)
            e_ref = probs[b]
            end_b = jnp.broadcast_to(end_row(M + b * BLOCK, BLOCK), (128, BLOCK)).T
            weight = jnp.where(lane_w, 1.0, jnp.where(lane_q == 7, -end_b, 0.0))
            dol_pair = mixed[rows, lanes]
            outs = []
            for half in range(2):
                head = 2 * p + half
                keep = first_half if half == 0 else jnp.logical_not(first_half)
                d_half = jnp.where(keep, dol_pair, jnp.zeros_like(dol_pair))
                delta = delta_s[rows, :]
                delta = jnp.where(lane_q // 4 == head, delta, jnp.zeros_like(delta))
                d_full = jnp.concatenate([d_half, delta], axis=1)
                hrows = pl.ds(pl.multiple_of(head * DH, DH), DH)
                q_t = qt[hrows, rows]
                d_t = dolt[hrows, rows]
                dqx = jnp.zeros((BLOCK, 256), f32)
                for j, (k0, kn) in enumerate(key_chunks(b)):
                    e = e_ref[head, :, k0 : k0 + kn]
                    ds = (dot_nt(d_full, value_full(lanes, k0, kn)) * e.astype(f32)).astype(bf16)
                    dqx = dqx + dot_nn(ds, key_full(lanes, k0, kn))
                    at_k = j * 128 + half * DH
                    gather(at_k, seen(b, j), kn, dot_nn(q_t, ds))
                    at_v = (NK + j) * 128 + half * DH
                    gather(at_v, seen(b, j), kn, dot_nn(d_t, e))
                outs.append(dqx[:, 0:128])
                tail = jnp.sum(dqx[:, 128:256] * weight, axis=0, keepdims=True)
                here = lax.broadcasted_iota(jnp.int32, (8, 128), 0) == head
                slope_sums = slope_sums + jnp.where(here, tail, 0.0)
            dq = jnp.where(first_half, outs[0], outs[1]) * (1.0 / math.sqrt(DH))
            q_s[rows, lanes] = dq.astype(bf16)
            for k in range(HP):
                if ("bwd", k * NB + b) in SCHEDULE:

                    @pl.when(p == k)
                    def _():
                        ticks("bwd", k * NB + b)

        for j in range(NK):
            dk = (acc_s[j * 128 : (j + 1) * 128, :] * LN2).astype(bf16).T
            k_s[j * KC : (j + 1) * KC, lanes] = dk
            dv = acc_s[(NK + j) * 128 : (NK + j + 1) * 128, :].astype(bf16).T
            v_s[j * KC : (j + 1) * KC, lanes] = dv
        for r in range(D // BLOCK):
            rows = slice(r * BLOCK, (r + 1) * BLOCK)
            gq = dot_nn(keyint[rows, M:], q_s[:, lanes]).astype(bf16)
            pair = jnp.concatenate([k_s[:, lanes], v_s[:, lanes]], axis=1)
            gkv = dot_nn(keyint[rows, :], pair).astype(bf16)
            col = 2 * FF + D + p * 384
            g_s[rows, pl.ds(pl.multiple_of(col, 128), 128)] = gq
            g_s[rows, pl.ds(pl.multiple_of(col + 128, 128), 256)] = gkv
        ticks_in_loop("pair", p, HP)
        return slope_sums

    slope_sums = lax.fori_loop(0, HP, bwd_pair, jnp.zeros((8, 128), f32))

    def key_back(key_rows):
        return dot_nt(k_s[key_rows, :], wk_ref[...]) + dot_nt(v_s[key_rows, :], wv_ref[...])

    def mem_back(b, sums):
        rows = pl.ds(pl.multiple_of(b * BLOCK, BLOCK), BLOCK)
        unit, _ = norm_stats(mem_ref[rows, :].astype(f32))
        d_rows = key_back(rows)
        return sums[0] + col_sum8(d_rows * unit), sums[1] + col_sum8(d_rows)

    def slot_back(b, sums):
        rows = pl.ds(pl.multiple_of(b * BLOCK, BLOCK), BLOCK)
        key_rows = pl.ds(pl.multiple_of(b * BLOCK + M, BLOCK), BLOCK)
        unit, scale = norm_stats(x_ref[rows, :].astype(f32))
        d_rows = key_back(key_rows) + dot_nt(q_s[rows, :], wq_ref[...])
        grad = norm_back(unit, scale, d_rows * gain1) + dres[rows, :]
        second_s[rows, :] = grad.astype(bf16)
        return sums[0] + col_sum8(d_rows * unit), sums[1] + col_sum8(d_rows)

    layer_copies[0].wait()
    for copy in layer_copies[1:]:
        if talk:
            copy.wait_send()
        else:
            copy.wait()
    sums = (zero8, zero8)
    for i in range(nslot):
        sums = slot_back(other * nslot + i, sums)
        ingrad_copies[1 + i].start()
        ticks("tail", i)
    for i in range(MB):
        sums = mem_back(i, sums)
        ticks("tail", nslot + i)
    for i in range(nslot):
        sums = slot_back(blk * nslot + i, sums)
        ticks("tail", nslot + MB + i)
    ingrad_copies[0].start()
    gain1_sum, shift1_sum = sums
    sm_own[0] = jnp.zeros_like(sm_own[0])
    for k, part in enumerate((gain1_sum, shift1_sum, gain2_sum, shift2_sum)):
        sm_own[0, k : k + 1, :] = jnp.sum(part, axis=0, keepdims=True)
    total = jnp.broadcast_to(jnp.sum(slope_sums, axis=1, keepdims=True), (8, 128))
    sm_own[0, 4:5, 0:128] = jnp.sum(
        jnp.where(lax.broadcasted_iota(jnp.int32, (8, 128), 0)
                  == lax.broadcasted_iota(jnp.int32, (8, 128), 1), total, 0.0),
        axis=0, keepdims=True)

    if talk:
        k = 0
        for level, devices in enumerate(
            ([sibling], [d for d, _ in z_peers], [d for d, _ in xy_peers])
        ):
            hops = []
            for device in devices:
                hops.append(
                    remote(sm_own.at[level], sm_in.at[k], sm_send.at[k], sm_recv.at[k], device)
                )
                k += 1
            for hop in hops:
                hop.start()
            ticks("small", level)
            total = sm_own[level]
            for i, hop in enumerate(hops):
                hop.wait()
                total = total + sm_in[k - len(hops) + i]
            sm_own[level + 1] = total
        small_ref[...] = sm_own[3]
    else:
        for level in range(3):
            ticks("small", level)
        small_ref[...] = sm_own[0]
    for i in range(10):
        ticks("last", i)
    ingrad_copies[0].wait()
    if not talk:
        for u in range(len(units)):
            unit_out(u).start()
            unit_out(u).wait()
    if talk:
        for copy in exchange:
            copy.wait_send()
        for copy in layer_copies[1:]:
            copy.wait_recv()
    for copy in ingrad_copies[1:]:
        copy.wait()


SPLIT = (2, 2, 2, 2)
ORDERS = ('axyb', 'yzx', 'yxz', 'yzx', 'xyab', 'yzx', 'ayxb', 'ayxb', 'xyab', 'yxab', 'zp', 'pz', 'zp')
SCHEDULE = {
    ('chunk', 0): ((0, 0), (1, 0)),
    ('chunk', 1): ((0, 1), (3, 0), (2, 0)),
    ('feed', 9): ((1, 1),),
    ('chunk', 2): ((5, 0), (3, 1), (4, 0)),
    ('feed', 13): ((0, 2), (2, 1)),
    ('feed', 15): ((1, 2),),
    ('chunk', 3): ((6, 0), (5, 1), (7, 0)),
    ('post', 0): ((4, 1),),
    ('post', 1): ((0, 3), (3, 2)),
    ('go', 0): ((6, 1), (8, 0)),
    ('bwd', 0): ((1, 3), (7, 1), (2, 2)),
    ('bwd', 1): ((4, 2),),
    ('bwd', 2): ((0, 4), (5, 2), (3, 3), (8, 1)),
    ('bwd', 3): ((1, 4), (6, 2)),
    ('pair', 0): ((9, 0), (3, 4), (4, 3), (2, 3)),
    ('bwd', 4): ((-1, 0), (0, 5), (7, 2)),
    ('bwd', 5): ((1, 5), (6, 3), (8, 2)),
    ('bwd', 6): ((-1, 1), (9, 1), (5, 3), (3, 5), (4, 4)),
    ('bwd', 7): ((0, 6), (7, 3), (2, 4)),
    ('pair', 1): ((-1, 2), (6, 4), (8, 3), (10, 0)),
    ('bwd', 8): ((9, 2),),
    ('bwd', 9): ((-1, 3), (0, 7), (1, 6)),
    ('bwd', 10): ((5, 4), (3, 6), (7, 4), (10, 1)),
    ('bwd', 11): ((4, 5), (8, 4)),
    ('pair', 2): ((6, 5), (9, 3), (11, 0), (2, 5)),
    ('bwd', 12): ((1, 7), (7, 5)),
    ('bwd', 14): ((0, 8), (3, 7), (11, 1)),
    ('bwd', 15): ((1, 8), (9, 4), (5, 5), (4, 6), (10, 2)),
    ('pair', 3): ((6, 6), (12, 0), (3, 8), (7, 6), (8, 5), (2, 6)),
    ('tail', 1): ((0, 9), (6, 7), (9, 5), (12, 1), (11, 2), (10, 3)),
    ('tail', 2): ((5, 6), (4, 7), (7, 7)),
    ('tail', 3): ((0, 10), (8, 6), (2, 7)),
    ('tail', 4): ((6, 8), (9, 6)),
    ('tail', 5): ((2, 8),),
    ('small', 0): ((5, 7), (12, 2), (4, 8), (8, 7), (11, 3)),
    ('small', 1): ((6, 9), (9, 7), (7, 8)),
    ('small', 2): ((5, 8), (12, 3), (8, 8), (11, 4), (10, 4)),
    ('last', 0): ((6, 10), (9, 8), (12, 4), (4, 9), (7, 9), (8, 9), (11, 5), (10, 5)),
    ('last', 1): ((9, 9), (12, 5), (4, 10), (7, 10), (8, 10), (11, 6), (10, 6)),
    ('last', 2): ((9, 10), (12, 6)),
}


def layer_call(counts, lengths, tokens, memory, ends, grad, params, talk=True):
    _, SH, D = tokens.shape
    MH = memory.shape[1]
    S, M = 2 * SH, 2 * MH
    R = M + S
    gain1, shift1, wq, wk, wv, wo, slopes, gain2, shift2, w1, w2 = params
    FF = w1.shape[1]
    H = slopes.shape[0]
    vmem = pl.BlockSpec(memory_space=pltpu.VMEM)
    smem = pl.BlockSpec(memory_space=pltpu.SMEM)
    hbm = pl.BlockSpec(memory_space=pl.ANY)
    V = pltpu.VMEM
    G = 2 * FF + 4 * D
    units = len(ORDERS)
    dma = pltpu.SemaphoreType.DMA
    scratch = [
        V((S, D), bf16),
        V((M, D), bf16),
        V((S, D), bf16),
        V((2, 1, MH + SH), jnp.int32),
        V((D, D), bf16),
        V((D, D), bf16),
        V((D, D), bf16),
        V((D, D), bf16),
        V((D, FF), bf16),
        V((FF, D), bf16),
        V((D, R), bf16),
        V((R, D), bf16),
        V((R, D), bf16),
        V((R, 128), bf16),
        V((S, D), bf16),
        V((D, S), bf16),
        V((S, 128), f32),
        V((S, D), bf16),
        V((S, D), bf16),
        V((S, D), bf16),
        V((D, S), bf16),
        V((D, S), bf16),
        V((S, 512), bf16),
        V((S, 512), bf16),
        V((S, D), f32),
        V((S, D), f32),
        V((D, S), bf16),
        V((S, 128), bf16),
        V((D, G), bf16),
        V((D // 2, G), bf16),
        V((D // 2 - 16, G), bf16),
        V((4, 8, D), f32),
        V((7, 8, D), f32),
        dma((16,)),
        dma((12,)),
        dma((12,)),
        dma((units, 14)),
        dma((units, 14)),
        dma((7,)),
        dma((7,)),
        dma((units,)),
    ]
    for b in range(S // BLOCK):
        scratch.append(V((H, BLOCK, M + (b + 1) * BLOCK), bf16))
    shapes = (
        jax.ShapeDtypeStruct((2, SH, D), bf16),
        jax.ShapeDtypeStruct((2, SH, D), bf16),
        jax.ShapeDtypeStruct((D, G), bf16),
        jax.ShapeDtypeStruct((8, D), f32),
    )
    extra = {"collective_id": 1, "has_side_effects": True} if talk else {}
    return pl.pallas_call(
        functools.partial(layer_kernel, talk),
        out_shape=shapes,
        in_specs=[smem] * 3 + [hbm] * 4 + [vmem] * 4 + [hbm] * 6,
        out_specs=[hbm, hbm, hbm, vmem],
        scratch_shapes=scratch,
        compiler_params=pltpu.CompilerParams(
            vmem_limit_bytes=64 * 1024 * 1024 - 65536, **extra
        ),
        name="layer",
    )(
        counts, lengths, slopes, tokens, memory, ends, grad,
        gain1.reshape(1, D), shift1.reshape(1, D), gain2.reshape(1, D), shift2.reshape(1, D),
        wq, wk, wv, wo, w1, w2,
    )


def layer_norm(values, gain, shift):
    centred = values - jnp.mean(values, axis=-1, keepdims=True)
    spread = jnp.mean(centred * centred, axis=-1, keepdims=True)
    return centred * lax.rsqrt(spread + epsilon) * gain + shift


def block_scores(
    q_heads, key_block, q_ends, key_order, key_ends, q_index, head_slopes, score_scale
):
    scores = (
        jnp.einsum("qhd,khd->hqk", q_heads, key_block, preferred_element_type=jnp.float32)
        * score_scale
    )
    distance = (q_ends[:, None] - key_ends[None, :]).astype(jnp.float32)
    scores = scores - head_slopes[:, None, None] * distance[None]
    allowed = key_order[None, :] <= q_index[:, None]
    return (jnp.where(allowed[None], scores, -1e30), distance)


def spread_device(
    tokens,
    memory,
    segment_ends,
    memory_ends,
    segment_counts,
    memory_lengths,
    first_gain,
    first_shift,
    query_weight,
    key_weight,
    value_weight,
    out_weight,
    head_slopes,
    second_gain,
    second_shift,
    hidden_weight,
    output_weight,
    output_grad,
):
    seq_count, slot_count, model_width = tokens.shape
    mem_count = memory.shape[1]
    head_count = head_slopes.shape[0]
    head_dim = model_width // head_count
    score_scale = 1.0 / math.sqrt(head_dim)
    key_rows = mem_count + slot_count
    blocks = lax.axis_size("blk")
    my_block = lax.axis_index("blk")
    x_float = tokens.astype(jnp.float32)
    mem_float = memory.astype(jnp.float32)
    normed = layer_norm(x_float, first_gain, first_shift).astype(jnp.bfloat16)
    mem_normed = layer_norm(mem_float, first_gain, first_shift).astype(jnp.bfloat16)
    key_input = jnp.concatenate([mem_normed, normed], axis=1)
    query = jnp.einsum(
        "std,de->ste", normed, query_weight, preferred_element_type=jnp.float32
    ).astype(jnp.bfloat16)
    pair_weight = jnp.concatenate([key_weight, value_weight], axis=1)
    key_value = jnp.einsum(
        "srd,de->rse", key_input, pair_weight, preferred_element_type=jnp.float32
    ).astype(jnp.bfloat16)
    mem_index = my_block * mem_count + jnp.arange(mem_count, dtype=jnp.int32)
    slot_index = my_block * slot_count + jnp.arange(slot_count, dtype=jnp.int32)
    mem_order = jnp.where(
        mem_index[None, :] >= mem_count * blocks - memory_lengths[:, None], -1, far_order
    )
    slot_order = jnp.where(
        slot_index[None, :] < segment_counts[:, None], slot_index[None, :], far_order
    )
    key_meta = jnp.stack(
        [
            jnp.concatenate([mem_order, slot_order], axis=1),
            jnp.concatenate([memory_ends, segment_ends], axis=1),
        ]
    )
    all_pairs, all_meta = (
        lax.all_gather(key_value, "blk", axis=0, tiled=True),
        lax.all_gather(key_meta, "blk", axis=2, tiled=True),
    )
    query_heads = query.reshape(seq_count, slot_count, head_count, head_dim)

    def pick(seq_index):
        pair_rows = lax.dynamic_index_in_dim(all_pairs, seq_index, 1, keepdims=False)
        meta_rows = lax.dynamic_index_in_dim(all_meta, seq_index, 1, keepdims=False)
        key_heads = pair_rows[:, :model_width].reshape(-1, key_rows, head_count, head_dim)
        value_heads = pair_rows[:, model_width:].reshape(-1, key_rows, head_count, head_dim)
        return (
            key_heads,
            value_heads,
            meta_rows[0].reshape(-1, key_rows),
            meta_rows[1].reshape(-1, key_rows),
        )

    def attend(seq_index):
        key_heads, value_heads, key_order, key_ends = pick(seq_index)
        q_heads = lax.dynamic_index_in_dim(query_heads, seq_index, 0, keepdims=False)
        q_ends = lax.dynamic_index_in_dim(segment_ends, seq_index, 0, keepdims=False)

        def stats_step(running, pieces):
            scores = block_scores(
                q_heads,
                pieces[0],
                q_ends,
                pieces[1],
                pieces[2],
                slot_index,
                head_slopes,
                score_scale,
            )[0]
            running_max = jnp.maximum(running[0], jnp.max(scores, axis=-1))
            running_sum = running[1] * jnp.exp(running[0] - running_max) + jnp.sum(
                jnp.exp(scores - running_max[..., None]), axis=-1
            )
            return ((running_max, running_sum), None)

        start_max = jnp.full((head_count, slot_count), -jnp.inf, jnp.float32)
        (top_max, top_sum), _ = lax.scan(
            stats_step, (start_max, jnp.zeros_like(start_max)), (key_heads, key_order, key_ends)
        )
        log_total = top_max + jnp.log(top_sum)

        def out_step(summed, pieces):
            scores = block_scores(
                q_heads,
                pieces[0],
                q_ends,
                pieces[1],
                pieces[2],
                slot_index,
                head_slopes,
                score_scale,
            )[0]
            attn_probs = jnp.exp(scores - log_total[..., None]).astype(jnp.bfloat16)
            return (
                summed
                + jnp.einsum(
                    "hqk,khd->qhd", attn_probs, pieces[3], preferred_element_type=jnp.float32
                ),
                None,
            )

        start_out = jnp.zeros((slot_count, head_count, head_dim), jnp.float32)
        mixed_heads, _ = lax.scan(
            out_step, start_out, (key_heads, key_order, key_ends, value_heads)
        )
        return (mixed_heads, log_total)

    mixed_all, log_totals = lax.map(attend, jnp.arange(seq_count))
    mixed_low = mixed_all.reshape(seq_count, slot_count, model_width).astype(jnp.bfloat16)
    residual = x_float + jnp.einsum(
        "std,de->ste", mixed_low, out_weight, preferred_element_type=jnp.float32
    )
    second_low = layer_norm(residual, second_gain, second_shift).astype(jnp.bfloat16)
    hidden_pre = jnp.einsum(
        "std,df->stf", second_low, hidden_weight, preferred_element_type=jnp.float32
    )
    act_low = jax.nn.gelu(hidden_pre, approximate=False).astype(jnp.bfloat16)
    layer_out = (
        residual
        + jnp.einsum("stf,fd->std", act_low, output_weight, preferred_element_type=jnp.float32)
    ).astype(jnp.bfloat16)
    grad_output_w = jnp.einsum(
        "stf,std->fd", act_low, output_grad, preferred_element_type=jnp.float32
    )
    d_act = jnp.einsum(
        "std,fd->stf", output_grad, output_weight, preferred_element_type=jnp.float32
    )
    _, gelu_pull = jax.vjp(lambda inner: jax.nn.gelu(inner, approximate=False), hidden_pre)
    d_pre_low = gelu_pull(d_act)[0].astype(jnp.bfloat16)
    grad_hidden_w = jnp.einsum(
        "std,stf->df", second_low, d_pre_low, preferred_element_type=jnp.float32
    )
    d_second = jnp.einsum(
        "stf,df->std", d_pre_low, hidden_weight, preferred_element_type=jnp.float32
    )
    _, second_pull = jax.vjp(layer_norm, residual, second_gain, second_shift)
    d_resid_norm, grad_second_g, grad_second_b = second_pull(d_second)
    d_residual = d_resid_norm + output_grad.astype(jnp.float32)
    d_branch = d_residual.astype(jnp.bfloat16)
    grad_out_w = jnp.einsum("std,ste->de", mixed_low, d_branch, preferred_element_type=jnp.float32)
    d_mixed = jnp.einsum(
        "ste,de->std", d_branch, out_weight, preferred_element_type=jnp.float32
    ).astype(jnp.bfloat16)
    d_mixed_heads = d_mixed.reshape(seq_count, slot_count, head_count, head_dim)

    def query_side(seq_index):
        key_heads, value_heads, key_order, key_ends = pick(seq_index)
        q_heads = lax.dynamic_index_in_dim(query_heads, seq_index, 0, keepdims=False)
        q_ends = lax.dynamic_index_in_dim(segment_ends, seq_index, 0, keepdims=False)
        d_heads = lax.dynamic_index_in_dim(d_mixed_heads, seq_index, 0, keepdims=False)
        log_total = lax.dynamic_index_in_dim(log_totals, seq_index, 0, keepdims=False)

        def probs_of(key_block, order_block, ends_block, value_block):
            scores, distance = block_scores(
                q_heads,
                key_block,
                q_ends,
                order_block,
                ends_block,
                slot_index,
                head_slopes,
                score_scale,
            )
            attn_probs = jnp.exp(scores - log_total[..., None])
            d_probs = jnp.einsum(
                "qhd,khd->hqk", d_heads, value_block, preferred_element_type=jnp.float32
            )
            return (attn_probs, d_probs, distance)

        def delta_step(summed, pieces):
            attn_probs, d_probs, _ = probs_of(pieces[0], pieces[1], pieces[2], pieces[3])
            return (summed + jnp.sum(attn_probs * d_probs, axis=-1), None)

        delta_rows, _ = lax.scan(
            delta_step,
            jnp.zeros((head_count, slot_count), jnp.float32),
            (key_heads, key_order, key_ends, value_heads),
        )

        def grad_step(running, pieces):
            attn_probs, d_probs, distance = probs_of(pieces[0], pieces[1], pieces[2], pieces[3])
            d_scores = (attn_probs * (d_probs - delta_rows[..., None])).astype(jnp.bfloat16)
            d_query = running[0] + jnp.einsum(
                "hqk,khd->qhd", d_scores, pieces[0], preferred_element_type=jnp.float32
            )
            d_slopes = running[1] - jnp.sum(
                d_scores.astype(jnp.float32) * distance[None], axis=(1, 2)
            )
            return ((d_query, d_slopes), None)

        start_grads = (
            jnp.zeros((slot_count, head_count, head_dim), jnp.float32),
            jnp.zeros((head_count,), jnp.float32),
        )
        (d_query, d_slopes), _ = lax.scan(
            grad_step, start_grads, (key_heads, key_order, key_ends, value_heads)
        )
        return (d_query * score_scale, delta_rows, d_slopes)

    d_query_all, delta_all, slope_parts = lax.map(query_side, jnp.arange(seq_count))
    grad_slopes = jnp.sum(slope_parts, axis=0)
    d_query_low = d_query_all.reshape(seq_count, slot_count, model_width).astype(jnp.bfloat16)

    def pair_terms(
        pair_rows, order_block, ends_block, q_heads, q_ends, q_index, d_heads, log_total, delta_rows
    ):
        key_block = pair_rows[:, :model_width].reshape(key_rows, head_count, head_dim)
        value_block = pair_rows[:, model_width:].reshape(key_rows, head_count, head_dim)
        scores, _ = block_scores(
            q_heads, key_block, q_ends, order_block, ends_block, q_index, head_slopes, score_scale
        )
        attn_probs = jnp.exp(scores - log_total[..., None])
        d_probs = jnp.einsum(
            "qhd,khd->hqk", d_heads, value_block, preferred_element_type=jnp.float32
        )
        d_scores = (attn_probs * (d_probs - delta_rows[..., None])).astype(jnp.bfloat16)
        d_value = jnp.einsum(
            "hqk,qhd->khd",
            attn_probs.astype(jnp.bfloat16),
            d_heads,
            preferred_element_type=jnp.float32,
        )
        d_key = (
            jnp.einsum("hqk,qhd->khd", d_scores, q_heads, preferred_element_type=jnp.float32)
            * score_scale
        )
        return jnp.concatenate(
            [d_key.reshape(key_rows, model_width), d_value.reshape(key_rows, model_width)], axis=1
        )

    def one_block(block_index):
        offset = block_index * key_rows
        pair_block = lax.dynamic_slice_in_dim(all_pairs, offset, key_rows, 0)
        meta_block = lax.dynamic_slice_in_dim(all_meta, offset, key_rows, 2)
        return jax.vmap(pair_terms, in_axes=(1, 0, 0, 0, 0, None, 0, 0, 0), out_axes=1)(
            pair_block,
            meta_block[0],
            meta_block[1],
            query_heads,
            segment_ends,
            slot_index,
            d_mixed_heads,
            log_totals,
            delta_all,
        )

    pieces = lax.map(one_block, jnp.arange(lax.axis_size("blk") * key_rows // key_rows))
    pair_grads = lax.psum_scatter(
        pieces.reshape(lax.axis_size("blk") * key_rows, seq_count, 2 * model_width).astype(
            jnp.bfloat16
        ),
        "blk",
        scatter_dimension=0,
        tiled=True,
    )
    grad_pair_w = jnp.einsum(
        "srd,rse->de", key_input, pair_grads, preferred_element_type=jnp.float32
    )
    grad_key_w = grad_pair_w[:, :model_width]
    grad_value_w = grad_pair_w[:, model_width:]
    d_key_input = jnp.einsum(
        "rse,de->srd", pair_grads, pair_weight, preferred_element_type=jnp.float32
    )
    grad_query_w = jnp.einsum(
        "std,ste->de", normed, d_query_low, preferred_element_type=jnp.float32
    )
    d_normed = (
        jnp.einsum("ste,de->std", d_query_low, query_weight, preferred_element_type=jnp.float32)
        + d_key_input[:, mem_count:]
    )
    _, first_pull = jax.vjp(layer_norm, x_float, first_gain, first_shift)
    d_tokens, gain_slots, shift_slots = first_pull(d_normed)
    _, mem_pull = jax.vjp(
        lambda gain, shift: layer_norm(mem_float, gain, shift), first_gain, first_shift
    )
    gain_mem, shift_mem = mem_pull(d_key_input[:, :mem_count])
    input_grad = (d_tokens + d_residual).astype(jnp.bfloat16)
    grad_first_g = gain_slots + gain_mem
    grad_first_b = shift_slots + shift_mem
    summed = lax.psum(
        (
            grad_first_g,
            grad_first_b,
            grad_query_w,
            grad_key_w,
            grad_value_w,
            grad_out_w,
            grad_slopes,
            grad_second_g,
            grad_second_b,
            grad_hidden_w,
            grad_output_w,
        ),
        ("seq", "blk"),
    )
    return (
        layer_out,
        input_grad,
        summed[0],
        summed[1],
        summed[2],
        summed[3],
        summed[4],
        summed[5],
        summed[6],
        summed[7],
        summed[8],
        summed[9],
        summed[10],
    )


def widen_kernel(ga, gb, gc, layer_in, grad_in, small, *outs):
    gw1, gw2, go, gq, gk, gv, layer, grad, gain1, shift1, slopes, gain2, shift2 = outs
    half = ga.shape[1] // 2
    gw1[...] = ga[:, :half].astype(f32)
    gw2[...] = ga[:, half:].astype(f32).T
    go[...] = gb[...].astype(f32)
    for i, out in enumerate((gq, gk, gv)):
        out[...] = gc[:, i * 128 : (i + 1) * 128].astype(f32)
    layer[...] = layer_in[...]
    grad[...] = grad_in[...]

    @pl.when((pl.program_id(0) == 0) & (pl.program_id(1) == 0))
    def _():
        for i, out in enumerate((gain1, shift1, gain2, shift2)):
            out[...] = small[i : i + 1, :]
        slopes[...] = small[4:5, 0:8]


def widen(grads, layer, in_grad, small, D, FF):
    RB = D // 2
    LB = layer.shape[0] // 8
    out = [
        ((D, FF), (RB, 512), lambda c, r: (r, c)),
        ((FF, D), (512, RB), lambda c, r: (c, r)),
        ((D, D), (RB, 128), lambda c, r: (r, c)),
        ((D, D), (RB, 128), lambda c, r: (r, c)),
        ((D, D), (RB, 128), lambda c, r: (r, c)),
        ((D, D), (RB, 128), lambda c, r: (r, c)),
        ((8 * LB, D), (LB, D), lambda c, r: (2 * c + r, 0)),
        ((8 * LB, D), (LB, D), lambda c, r: (2 * c + r, 0)),
    ]
    kinds = [f32] * 6 + [bf16] * 2
    shapes = [jax.ShapeDtypeStruct(shape, kind) for (shape, _, _), kind in zip(out, kinds)]
    specs = [pl.BlockSpec(block, index) for _, block, index in out]
    for width in (D, D, 8, D, D):
        shapes.append(jax.ShapeDtypeStruct((1, width), f32))
        specs.append(pl.BlockSpec((1, width), lambda c, r: (0, 0)))
    go_at = 2 * FF // 128
    head_at = (2 * FF + D) // 384
    return pl.pallas_call(
        widen_kernel,
        grid=(4, 2),
        out_shape=shapes,
        in_specs=[
            pl.BlockSpec((RB, 1024), lambda c, r: (r, c)),
            pl.BlockSpec((RB, 128), lambda c, r: (r, go_at + c)),
            pl.BlockSpec((RB, 384), lambda c, r: (r, head_at + c)),
            pl.BlockSpec((LB, D), lambda c, r: (2 * c + r, 0)),
            pl.BlockSpec((LB, D), lambda c, r: (2 * c + r, 0)),
            pl.BlockSpec((8, D), lambda c, r: (0, 0)),
        ],
        out_specs=specs,
        compiler_params=pltpu.CompilerParams(vmem_limit_bytes=62 * 1024 * 1024),
        name="widen",
    )(grads, grads, grads, layer, in_grad, small)


def whole_device(*args):
    tokens, memory, segment_ends, memory_ends, counts, lengths = args[:6]
    params = args[6:17]
    output_grad = args[17]
    D = tokens.shape[2]
    FF = params[9].shape[1]
    H = params[6].shape[0]
    ends = jnp.concatenate([memory_ends, segment_ends], axis=1)[:, None]
    layer, in_grad, grads, small = layer_call(
        counts, lengths, tokens, memory, ends, output_grad, params
    )
    gw1, gw2, go, gq, gk, gv, layer, in_grad, *rows = widen(
        grads, layer.reshape(-1, D), in_grad.reshape(-1, D), small, D, FF
    )
    gain1, shift1, slopes, gain2, shift2 = (row[0] for row in rows)
    return (
        layer.reshape(tokens.shape),
        in_grad.reshape(tokens.shape),
        gain1,
        shift1,
        gq,
        gk,
        gv,
        go,
        slopes,
        gain2,
        shift2,
        gw1,
        gw2,
    )


def per_device(*args):
    whole = args[0].shape[0] == lax.axis_size("blk") == 2 and lax.axis_size("seq") == 16
    if whole:
        return whole_device(*args)
    return spread_device(*args)


def solution(mesh):
    placed = (
        P("seq", "blk", None),
        P("seq", "blk", None),
        P("seq", "blk"),
        P("seq", "blk"),
        P("seq"),
        P("seq"),
        P(),
        P(),
        P(),
        P(),
        P(),
        P(),
        P(),
        P(),
        P(),
        P(),
        P(),
        P("seq", "blk", None),
    )
    return jax.shard_map(
        per_device,
        mesh=mesh,
        in_specs=placed,
        out_specs=(
            P("seq", "blk", None),
            P("seq", "blk", None),
            P(),
            P(),
            P(),
            P(),
            P(),
            P(),
            P(),
            P(),
            P(),
            P(),
            P(),
        ),
        check_vma=False,
    )
```

```python
import functools
import math

import jax
import jax.numpy as jnp
from jax import lax
from jax.experimental import pallas as pl
from jax.experimental.pallas import tpu as pltpu
from jax.sharding import PartitionSpec as P

epsilon = 1e-05
far_order = 1073741824
f32 = jnp.float32
bf16 = jnp.bfloat16
BLOCK = 256
LOG2E = 1.4426950408889634
LN2 = 0.6931471805599453


def dot_nn(left, right):
    return lax.dot_general(left, right, (((1,), (0,)), ((), ())), preferred_element_type=f32)


def dot_nt(left, right):
    return lax.dot_general(left, right, (((1,), (1,)), ((), ())), preferred_element_type=f32)


def norm_stats(values):
    centred = values - jnp.mean(values, axis=-1, keepdims=True)
    spread = jnp.mean(centred * centred, axis=-1, keepdims=True)
    scale = lax.rsqrt(spread + epsilon)
    return centred * scale, scale


def norm_back(unit, scale, grad_unit):
    mean_grad = jnp.mean(grad_unit, axis=-1, keepdims=True)
    mean_prod = jnp.mean(grad_unit * unit, axis=-1, keepdims=True)
    return (grad_unit - mean_grad - unit * mean_prod) * scale


def pieces_of(value, count):
    out = []
    for _ in range(count):
        part = value.astype(bf16).astype(f32)
        out.append(part)
        value = value - part
    return out


ERFC_P = 0.4
ERFC_C = (0.22567586600780487, 0.2256695181131363, 0.2078438550233841, 0.16853390634059906, 0.1414608359336853, -0.005667657125741243, 0.16915477812290192, -0.18294358253479004, 0.050272583961486816)


def gelu_both(x):
    cdf = 0.5 * lax.erf(x * math.sqrt(0.5)) + 0.5
    ex = jnp.exp2((x * x) * (-0.5 * LOG2E))
    return x * cdf, cdf + x * (ex * (1.0 / math.sqrt(2.0 * math.pi)))


def col_sum8(value):
    return jnp.sum(value.reshape(-1, 8, value.shape[-1]), axis=0)


def flip(bit):
    return 1 - bit


def layer_kernel(
    talk,
    counts_ref,
    lengths_ref,
    slopes_ref,
    tokens_ref,
    memory_ref,
    ends_ref,
    grad_ref,
    gain1_ref,
    shift1_ref,
    gain2_ref,
    shift2_ref,
    wq_hbm,
    wk_hbm,
    wv_hbm,
    wo_hbm,
    w1_hbm,
    w2_hbm,
    layer_hbm,
    ingrad_hbm,
    grads_hbm,
    small_ref,
    x_ref,
    mem_ref,
    og_ref,
    ends_s,
    wq_ref,
    wk_ref,
    wv_ref,
    wo_ref,
    w1_ref,
    w2_ref,
    keyint,
    k_s,
    v_s,
    kx,
    q_s,
    qt,
    rl_s,
    o_s,
    mixed,
    second_s,
    secondt,
    ogt,
    act_s,
    dpre_s,
    acc_s,
    dres,
    dolt,
    delta_s,
    g_s,
    rc_s,
    r1_s,
    sm_own,
    sm_in,
    load_sem,
    ex_send,
    ex_recv,
    ar_send,
    ar_recv,
    sm_send,
    sm_recv,
    out_sem,
    *probs,
):
    S, D = x_ref.shape
    M = mem_ref.shape[0]
    R = M + S
    FF = w1_ref.shape[1]
    H = slopes_ref.shape[0]
    DH = D // H
    HP = H // 2
    NB = S // BLOCK
    MB = M // BLOCK
    SH = S // 2
    MH = M // 2
    KC = 512
    CH = 512
    NC = FF // CH

    if talk:
        seq = lax.axis_index("seq")
        blk = lax.axis_index("blk")
    else:
        seq = 0
        blk = 0
    core = seq % 2
    why = (seq // 2) % 2
    zed = seq // 4

    def at(z=None, y=None, c=None, x=None):
        z = zed if z is None else z
        y = why if y is None else y
        c = core if c is None else c
        return {"seq": z * 4 + y * 2 + c, "blk": blk if x is None else x}

    sibling = at(c=flip(core))
    partner = at(x=flip(blk))
    z_to = [zed + 1 - 2 * (zed % 2), (zed + 2) % 4, 3 - zed]
    z_peers = [(at(z=z), z) for z in z_to]
    plane = blk * 2 + why
    xy_peers = [
        (at(y=flip(why)), blk * 2 + flip(why)),
        (at(x=flip(blk)), flip(blk) * 2 + why),
        (at(x=flip(blk), y=flip(why)), flip(blk) * 2 + flip(why)),
    ]

    def remote(src, dst, send, recv, device):
        return pltpu.make_async_remote_copy(
            src_ref=src,
            dst_ref=dst,
            send_sem=send,
            recv_sem=recv,
            device_id=device,
            device_id_type=pl.DeviceIdType.MESH,
        )

    other = 1 - blk

    def half_rows(half, size):
        return pl.ds(pl.multiple_of(half * size, BLOCK), size)

    def slot_piece(part, index, half, i):
        src = tokens_ref if part == 0 else grad_ref
        dst = x_ref if part == 0 else og_ref
        rows = pl.ds(pl.multiple_of(half * SH + i * BLOCK, BLOCK), BLOCK)
        return src.at[index, i * BLOCK : (i + 1) * BLOCK, :], dst.at[rows, :]

    nslot = SH // BLOCK
    loads = [
        (memory_ref.at[blk], mem_ref.at[half_rows(blk, MH), :]),
        (ends_ref.at[blk], ends_s.at[blk]),
        (wk_hbm, wk_ref),
        (wv_hbm, wv_ref),
        (wq_hbm, wq_ref),
    ]
    loads += [slot_piece(0, blk, blk, i) for i in range(nslot)]
    n_first = len(loads)
    loads += [(wo_hbm, wo_ref), (w1_hbm, w1_ref), (w2_hbm, w2_ref)]
    loads += [slot_piece(1, blk, blk, i) for i in range(nslot)]
    copies = [
        pltpu.make_async_copy(src, dst, load_sem.at[i]) for i, (src, dst) in enumerate(loads)
    ]
    sends = [
        (memory_ref.at[other], mem_ref.at[half_rows(blk, MH), :]),
        (ends_ref.at[other], ends_s.at[blk]),
    ]
    sends += [slot_piece(0, other, blk, i) for i in range(nslot)]
    sends += [slot_piece(1, other, blk, i) for i in range(nslot)]
    if talk:
        exchange = [
            remote(src, dst, ex_send.at[i], ex_recv.at[i], partner)
            for i, (src, dst) in enumerate(sends)
        ]
    else:
        local = [
            (memory_ref.at[other], mem_ref.at[half_rows(other, MH), :]),
            (ends_ref.at[other], ends_s.at[other]),
        ]
        local += [slot_piece(0, other, other, i) for i in range(nslot)]
        local += [slot_piece(1, other, other, i) for i in range(nslot)]
        exchange = [
            pltpu.make_async_copy(src, dst, ex_send.at[i]) for i, (src, dst) in enumerate(local)
        ]
    for copy in copies[:n_first]:
        copy.start()
    if talk:
        barrier = pltpu.get_barrier_semaphore()
        greet = [sibling] + [d for d, _ in z_peers] + [d for d, _ in xy_peers]
        for device in greet:
            pl.semaphore_signal(
                barrier, inc=1, device_id=device, device_id_type=pl.DeviceIdType.MESH
            )
        pl.semaphore_wait(barrier, len(greet))
    for copy in exchange:
        copy.start()
    for copy in copies[n_first:]:
        copy.start()

    def arrive(i):
        if talk:
            exchange[i].wait_recv()
        else:
            exchange[i].wait()

    directions = {
        "x": (blk, [(partner, other)]),
        "y": (why, [(at(y=flip(why)), flip(why))]),
        "a": (zed % 2, [(z_peers[0][0], 1 - zed % 2)]),
        "b": (zed // 2, [(z_peers[1][0], 1 - zed // 2)]),
        "z": (zed, z_peers),
        "p": (plane, xy_peers),
    }
    units = []
    for c in range(NC):
        width = 2 * CH // SPLIT[c]
        for i in range(SPLIT[c]):
            units.append((c * 2 * CH + i * width, width))
    units.append((2 * FF, D))
    for p in range(HP):
        units.append((2 * FF + D + p * 384, 384))
    HALF = D // 2

    def rows_at(start, size):
        return pl.ds(pl.multiple_of(start, 16), size)

    def unit_rounds(u):
        start, size, place = core * HALF, HALF, 0
        rounds = []
        for name in ORDERS[u]:
            mine, peers = directions[name]
            piece = size // (len(peers) + 1)
            rounds.append((start, piece, mine, peers, place))
            place += piece * len(peers)
            start, size = start + mine * piece, piece
        return rounds, start, size

    def unit_copies(u, step):
        col, width = units[u]
        cols = slice(col, col + width)
        rounds, start, size = unit_rounds(u)
        n = len(rounds)
        out = []
        if step == 0:
            rows = rows_at((1 - core) * HALF, HALF)
            out.append((g_s.at[rows, cols], rc_s.at[:, cols], sibling))
        elif step <= n:
            begin, piece, _, peers, place = rounds[step - 1]
            for d, (device, index) in enumerate(peers):
                rows = rows_at(begin + index * piece, piece)
                here = slice(place + d * piece, place + (d + 1) * piece)
                out.append((g_s.at[rows, cols], r1_s.at[here, cols], device))
        elif step <= 2 * n:
            level = 2 * n - step
            begin, piece, mine, peers, _ = rounds[level]
            rows = rows_at(begin + mine * piece, piece)
            src = g_s if level == n - 1 else grads_hbm
            for device, _ in peers:
                out.append((src.at[rows, cols], grads_hbm.at[rows, cols], device))
        else:
            rows = rows_at(core * HALF, HALF)
            out.append((grads_hbm.at[rows, cols], grads_hbm.at[rows, cols], sibling))
        first = 0
        for earlier in range(step):
            if 1 <= earlier <= n:
                first += len(rounds[earlier - 1][3])
            elif n < earlier <= 2 * n:
                first += len(rounds[2 * n - earlier][3])
            else:
                first += 1
        return [
            remote(src, dst, ar_send.at[u, first + k], ar_recv.at[u, first + k], device)
            for k, (src, dst, device) in enumerate(out)
        ]

    def unit_add(u, step):
        col, width = units[u]
        cols = slice(col, col + width)
        rounds, _, _ = unit_rounds(u)
        if step == 0:
            begin, piece, places, buffer = core * HALF, HALF, [0], rc_s
        else:
            begin, piece, mine, peers, place = rounds[step - 1]
            begin = begin + mine * piece
            places, buffer = [place + d * piece for d in range(len(peers))], r1_s
        block = min(piece, 64)

        def add(i, _):
            rows = rows_at(begin + i * block, block)
            total = g_s[rows, cols].astype(f32)
            for place in places:
                total = total + buffer[rows_at(place + i * block, block), cols].astype(f32)
            g_s[rows, cols] = total.astype(bf16)
            return 0

        if piece == block:
            add(0, 0)
        else:
            lax.fori_loop(0, piece // block, add, 0)

    def unit_out(u):
        col, width = units[u]
        cols = slice(col, col + width)
        _, start, size = unit_rounds(u)
        rows = rows_at(start, size) if talk else slice(0, D)
        return pltpu.make_async_copy(g_s.at[rows, cols], grads_hbm.at[rows, cols], out_sem.at[u])

    def advance(u, step):
        if not talk:
            return
        n = len(ORDERS[u])
        if step > 0:
            for copy in unit_copies(u, step - 1):
                copy.wait()
            if step - 1 <= n:
                unit_add(u, step - 1)
        if step == n + 1:
            unit_out(u).start()
        if step == n + 2:
            unit_out(u).wait()
        if step < 2 * n + 2:
            for copy in unit_copies(u, step):
                copy.start()

    def ticks(kind, index):
        moves = SCHEDULE.get((kind, index), ())
        if not moves:
            return

        @pl.when(seq >= 0)
        def _():
            for u, step in moves:
                if u < 0:
                    layer_copies[1 + step].start()
                else:
                    advance(u, step)

    def ticks_in_loop(kind, index, count, base=0):
        for k in range(count):
            if (kind, base + k) in SCHEDULE:

                @pl.when(index == k)
                def _():
                    ticks(kind, base + k)

    gain1 = gain1_ref[...]
    shift1 = shift1_ref[...]
    gain2 = gain2_ref[...]
    shift2 = shift2_ref[...]
    count = counts_ref[blk]
    length = lengths_ref[blk]

    def give(result, hbm, k, pieces):
        own = pltpu.make_async_copy(result.at[half_rows(blk, SH), :], hbm.at[blk], load_sem.at[k])
        moves = [own]
        size = SH // pieces
        for i in range(pieces):
            theirs = result.at[pl.ds(pl.multiple_of(other * SH + i * size, size), size), :]
            rows = slice(i * size, (i + 1) * size)
            sem = len(sends) + 4 * k + i
            if talk:
                there = hbm.at[blk, rows, :]
                moves.append(remote(theirs, there, ex_send.at[sem], ex_recv.at[sem], partner))
            else:
                moves.append(
                    pltpu.make_async_copy(theirs, hbm.at[other, rows, :], ex_send.at[sem])
                )
        return moves

    layer_copies = give(second_s, layer_hbm, 0, 4)
    ingrad_copies = give(second_s, ingrad_hbm, 1, nslot)

    def project(normed, key_rows):
        keyint[:, key_rows] = normed.T
        k_s[key_rows, :] = dot_nn(normed, wk_ref[...]).astype(bf16)
        v_s[key_rows, :] = dot_nn(normed, wv_ref[...]).astype(bf16)

    def norm_mem(b):
        rows = pl.ds(pl.multiple_of(b * BLOCK, BLOCK), BLOCK)
        unit, _ = norm_stats(mem_ref[rows, :].astype(f32))
        project((unit * gain1 + shift1).astype(bf16), rows)

    def norm_slot(b):
        rows = pl.ds(pl.multiple_of(b * BLOCK, BLOCK), BLOCK)
        key_rows = pl.ds(pl.multiple_of(b * BLOCK + M, BLOCK), BLOCK)
        unit, _ = norm_stats(x_ref[rows, :].astype(f32))
        normed = (unit * gain1 + shift1).astype(bf16)
        project(normed, key_rows)
        query = (dot_nn(normed, wq_ref[...]) * (LOG2E / math.sqrt(DH))).astype(bf16)
        q_s[rows, :] = query
        qt[:, rows] = query.T

    for copy in copies[:n_first]:
        copy.wait()
    mh = MH // BLOCK
    for i in range(mh):
        norm_mem(blk * mh + i)
    for i in range(nslot):
        norm_slot(blk * nslot + i)
    arrive(0)
    for i in range(mh):
        norm_mem(other * mh + i)
    arrive(1)

    lane = lax.broadcasted_iota(jnp.int32, (128, 128), 1)
    row = lax.broadcasted_iota(jnp.int32, (128, 128), 0)

    def end_row(start, size):
        if start < M:
            half, off = start // MH, start % MH
        else:
            half, off = (start - M) // SH, MH + (start - M) % SH
        return ends_s[half, :, off : off + size].astype(f32)

    for r in range(R // 128):
        end_col = jnp.broadcast_to(end_row(r * 128, 128), (128, 128)).T
        high = jnp.floor(end_col * (1.0 / 256.0)) * 256.0
        index = row + r * 128
        if r * 128 < M:
            valid = index >= M - length
        else:
            valid = index - M < count
        bias = jnp.where(valid, 0.0, -1e30)
        extra = jnp.where(lane < 3, high, jnp.where(lane < 6, end_col - high, bias))
        extra = jnp.where(lane == 7, 1.0, jnp.where(lane > 7, 0.0, extra))
        kx[r * 128 : (r + 1) * 128, :] = extra.astype(bf16)

    for i in range(nslot):
        arrive(2 + i)
        norm_slot(other * nslot + i)

    lane_q = lax.broadcasted_iota(jnp.int32, (BLOCK, 128), 1)
    first_half = lane_q < DH
    lane_row = lax.broadcasted_iota(jnp.int32, (1, 128), 1)

    def key_chunks(b):
        end = M + (b + 1) * BLOCK
        return [(start, min(KC, end - start)) for start in range(0, end, KC)]

    def key_full(lanes, start, size):
        return jnp.concatenate(
            [k_s[start : start + size, lanes], kx[start : start + size, :]], axis=1
        )

    def value_full(lanes, start, size):
        return jnp.concatenate(
            [v_s[start : start + size, lanes], jnp.ones((size, 128), bf16)], axis=1
        )

    def query_extra(head):
        slope = jnp.full((1, 128), slopes_ref[head] * LOG2E, f32)
        s1, s2, s3 = pieces_of(slope, 3)
        where = jnp.where(lane_row >= 3, lane_row - 3, lane_row)
        out = jnp.where(where == 0, s1, jnp.where(where == 1, s2, s3))
        return jnp.where(lane_row < 6, out, jnp.where(lane_row == 6, 1.0, 0.0))

    rl_s[...] = jnp.zeros_like(rl_s)
    for b in range(NB):
        rows = slice(b * BLOCK, (b + 1) * BLOCK)
        e_ref = probs[b]

        def fwd_pair(p, _):
            lanes = pl.ds(pl.multiple_of(p * 128, 128), 128)
            q_pair = q_s[rows, lanes]
            outs = []
            for half in range(2):
                keep = first_half if half == 0 else jnp.logical_not(first_half)
                q_half = jnp.where(keep, q_pair, jnp.zeros_like(q_pair))
                extra = jnp.broadcast_to(query_extra(2 * p + half), (BLOCK, 128)).astype(bf16)
                q_full = jnp.concatenate([q_half, extra], axis=1)
                chunks = key_chunks(b)
                scores = [dot_nt(q_full, key_full(lanes, k0, kn)) for k0, kn in chunks]
                below = lax.broadcasted_iota(
                    jnp.int32, (BLOCK, BLOCK), 1
                ) <= lax.broadcasted_iota(jnp.int32, (BLOCK, BLOCK), 0)
                last = scores[-1]
                cut = last.shape[1] - BLOCK
                diag = jnp.where(below, last[:, cut:], -1e30)
                scores[-1] = jnp.concatenate([last[:, :cut], diag], axis=1) if cut else diag
                top = scores[-1][:, 0:128]
                for part in scores:
                    for k in range(0, part.shape[1], 128):
                        top = jnp.maximum(top, part[:, k : k + 128])
                top = jnp.max(top, axis=1, keepdims=True)
                both = jnp.zeros((BLOCK, 256), f32)
                for part, (k0, kn) in zip(scores, chunks):
                    e = jnp.exp2(part - top).astype(bf16)
                    e_ref[2 * p + half, :, k0 : k0 + kn] = e
                    both = both + dot_nn(e, value_full(lanes, k0, kn))
                outs.append((both[:, 0:128], 1.0 / both[:, 128:256]))
            rl = jnp.where(first_half, outs[0][1], outs[1][1])
            o = jnp.where(first_half, outs[0][0], outs[1][0]) * rl
            packed = jnp.where(lane_q == 2 * p, outs[0][1], rl_s[rows, :])
            rl_s[rows, :] = jnp.where(lane_q == 2 * p + 1, outs[1][1], packed)
            o_low = o.astype(bf16)
            o_s[rows, lanes] = (o - o_low.astype(f32)).astype(bf16)
            mixed[rows, lanes] = o_low
            return 0

        lax.fori_loop(0, HP, fwd_pair, 0, unroll=2)

    for copy in copies[n_first:]:
        copy.wait()
    for i in range(nslot):
        arrive(2 + nslot + i)

    def residual_of(rows):
        return x_ref[rows, :].astype(f32) + dot_nn(mixed[rows, :], wo_ref[...])

    def feed_prep(b, _):
        rows = slice(b * BLOCK, (b + 1) * BLOCK)
        residual = residual_of(rows)
        unit, _ = norm_stats(residual)
        second = (unit * gain2 + shift2).astype(bf16)
        second_s[rows, :] = second
        secondt[:, rows] = second.T
        ogt[:, rows] = og_ref[rows, :].T
        acc_s[rows, :] = residual
        dres[rows, :] = jnp.zeros((BLOCK, D), f32)
        return 0

    for b in range(NB):
        feed_prep(b, 0)
    def feed_chunk(c, _):
        cols = pl.ds(pl.multiple_of(c * CH, CH), CH)
        for b in range(NB):
            rows = slice(b * BLOCK, (b + 1) * BLOCK)
            hidden = dot_nn(second_s[rows, :], w1_ref[:, cols])
            d_act = dot_nt(og_ref[rows, :], w2_ref[cols, :])
            act, slope = gelu_both(hidden)
            act = act.astype(bf16)
            d_pre = (d_act * slope).astype(bf16)
            act_s[rows, :] = act
            dpre_s[rows, :] = d_pre
            acc_s[rows, :] += dot_nn(act, w2_ref[cols, :])
            dres[rows, :] += dot_nt(d_pre, w1_ref[:, cols])
            for k in range(NC):
                if ("feed", k * NB + b) in SCHEDULE:

                    @pl.when(c == k)
                    def _():
                        ticks("feed", k * NB + b)

        for r in range(D // BLOCK):
            rows = slice(r * BLOCK, (r + 1) * BLOCK)
            pre_cols = pl.ds(pl.multiple_of(c * 2 * CH, CH), CH)
            act_cols = pl.ds(pl.multiple_of(c * 2 * CH + CH, CH), CH)
            g_s[rows, pre_cols] = dot_nn(secondt[rows, :], dpre_s[...]).astype(bf16)
            g_s[rows, act_cols] = dot_nn(ogt[rows, :], act_s[...]).astype(bf16)
        ticks_in_loop("chunk", c, NC)
        return 0

    lax.fori_loop(0, NC, feed_chunk, 0)

    def feed_post(b, sums):
        rows = slice(b * BLOCK, (b + 1) * BLOCK)
        unit, scale = norm_stats(residual_of(rows))
        d_second = dres[rows, :]
        d_residual = og_ref[rows, :].astype(f32) + norm_back(unit, scale, d_second * gain2)
        dres[rows, :] = d_residual
        d_branch = d_residual.astype(bf16)
        act_s[rows, :] = d_branch
        secondt[:, rows] = mixed[rows, :].T
        d_mixed = dot_nt(d_branch, wo_ref[...]).astype(bf16).astype(f32)
        rl_b = rl_s[rows, :]
        rl_wide = []
        for p in range(HP):
            first = jnp.broadcast_to(rl_b[:, 2 * p : 2 * p + 1], (BLOCK, 128))
            second = jnp.broadcast_to(rl_b[:, 2 * p + 1 : 2 * p + 2], (BLOCK, 128))
            rl_wide.append(jnp.where(first_half, first, second))
        dol_b = (d_mixed * jnp.concatenate(rl_wide, axis=1)).astype(bf16)
        o = mixed[rows, :].astype(f32) + o_s[rows, :].astype(f32)
        prod = dol_b.astype(f32) * o
        mixed[rows, :] = dol_b
        dolt[:, rows] = dol_b.T
        packed = jnp.zeros((BLOCK, 128), f32)
        for head in range(H):
            part = prod[:, (head // 2) * 128 : (head // 2 + 1) * 128]
            keep = first_half if head % 2 == 0 else jnp.logical_not(first_half)
            delta = jnp.sum(jnp.where(keep, part, 0.0), axis=1, keepdims=True)
            for k, piece in enumerate(pieces_of(jnp.broadcast_to(-delta, (BLOCK, 128)), 3)):
                packed = jnp.where(lane_q == 4 * head + k, piece, packed)
        delta_s[rows, :] = packed.astype(bf16)
        ticks("post", b)
        return sums[0] + col_sum8(d_second * unit), sums[1] + col_sum8(d_second)

    def feed_out(b, _):
        rows = pl.ds(pl.multiple_of(b * BLOCK, BLOCK), BLOCK)
        second_s[rows, :] = acc_s[rows, :].astype(bf16)
        return 0

    lax.fori_loop(0, NB, feed_out, 0)
    layer_copies[0].start()
    zero8 = jnp.zeros((8, D), f32)
    gain2_sum, shift2_sum = (zero8, zero8)
    for b in range(NB):
        gain2_sum, shift2_sum = feed_post(b, (gain2_sum, shift2_sum))
    for r in range(D // BLOCK):
        rows = slice(r * BLOCK, (r + 1) * BLOCK)
        g_s[rows, 2 * FF : 2 * FF + D] = dot_nn(secondt[rows, :], act_s[...]).astype(bf16)

    ticks("go", 0)

    small_ref[...] = jnp.zeros_like(small_ref)
    NK = R // KC
    lane_w = (lane_q == 0) | (lane_q == 3)

    def seen(b, j):
        return dict(enumerate(key_chunks(b - 1))).get(j, (0, 0))[1] if b else 0

    def gather(start, old, size, value):
        rows = slice(start, start + DH)
        if old:
            acc_s[rows, 0:old] += value[:, 0:old]
        if old < size:
            acc_s[rows, old:size] = value[:, old:size]

    def bwd_pair(p, slope_sums):
        lanes = pl.ds(pl.multiple_of(p * 128, 128), 128)
        for b in range(NB):
            rows = slice(b * BLOCK, (b + 1) * BLOCK)
            e_ref = probs[b]
            end_b = jnp.broadcast_to(end_row(M + b * BLOCK, BLOCK), (128, BLOCK)).T
            weight = jnp.where(lane_w, 1.0, jnp.where(lane_q == 7, -end_b, 0.0))
            dol_pair = mixed[rows, lanes]
            outs = []
            for half in range(2):
                head = 2 * p + half
                keep = first_half if half == 0 else jnp.logical_not(first_half)
                d_half = jnp.where(keep, dol_pair, jnp.zeros_like(dol_pair))
                delta = delta_s[rows, :]
                delta = jnp.where(lane_q // 4 == head, delta, jnp.zeros_like(delta))
                d_full = jnp.concatenate([d_half, delta], axis=1)
                hrows = pl.ds(pl.multiple_of(head * DH, DH), DH)
                q_t = qt[hrows, rows]
                d_t = dolt[hrows, rows]
                dqx = jnp.zeros((BLOCK, 256), f32)
                for j, (k0, kn) in enumerate(key_chunks(b)):
                    e = e_ref[head, :, k0 : k0 + kn]
                    ds = (dot_nt(d_full, value_full(lanes, k0, kn)) * e.astype(f32)).astype(bf16)
                    dqx = dqx + dot_nn(ds, key_full(lanes, k0, kn))
                    at_k = j * 128 + half * DH
                    gather(at_k, seen(b, j), kn, dot_nn(q_t, ds))
                    at_v = (NK + j) * 128 + half * DH
                    gather(at_v, seen(b, j), kn, dot_nn(d_t, e))
                outs.append(dqx[:, 0:128])
                tail = jnp.sum(dqx[:, 128:256] * weight, axis=0, keepdims=True)
                here = lax.broadcasted_iota(jnp.int32, (8, 128), 0) == head
                slope_sums = slope_sums + jnp.where(here, tail, 0.0)
            dq = jnp.where(first_half, outs[0], outs[1]) * (1.0 / math.sqrt(DH))
            q_s[rows, lanes] = dq.astype(bf16)
            for k in range(HP):
                if ("bwd", k * NB + b) in SCHEDULE:

                    @pl.when(p == k)
                    def _():
                        ticks("bwd", k * NB + b)

        for j in range(NK):
            dk = (acc_s[j * 128 : (j + 1) * 128, :] * LN2).astype(bf16).T
            k_s[j * KC : (j + 1) * KC, lanes] = dk
            dv = acc_s[(NK + j) * 128 : (NK + j + 1) * 128, :].astype(bf16).T
            v_s[j * KC : (j + 1) * KC, lanes] = dv
        for r in range(D // BLOCK):
            rows = slice(r * BLOCK, (r + 1) * BLOCK)
            gq = dot_nn(keyint[rows, M:], q_s[:, lanes]).astype(bf16)
            pair = jnp.concatenate([k_s[:, lanes], v_s[:, lanes]], axis=1)
            gkv = dot_nn(keyint[rows, :], pair).astype(bf16)
            col = 2 * FF + D + p * 384
            g_s[rows, pl.ds(pl.multiple_of(col, 128), 128)] = gq
            g_s[rows, pl.ds(pl.multiple_of(col + 128, 128), 256)] = gkv
        ticks_in_loop("pair", p, HP)
        return slope_sums

    slope_sums = lax.fori_loop(0, HP, bwd_pair, jnp.zeros((8, 128), f32))

    def key_back(key_rows):
        return dot_nt(k_s[key_rows, :], wk_ref[...]) + dot_nt(v_s[key_rows, :], wv_ref[...])

    def mem_back(b, sums):
        rows = pl.ds(pl.multiple_of(b * BLOCK, BLOCK), BLOCK)
        unit, _ = norm_stats(mem_ref[rows, :].astype(f32))
        d_rows = key_back(rows)
        return sums[0] + col_sum8(d_rows * unit), sums[1] + col_sum8(d_rows)

    def slot_back(b, sums):
        rows = pl.ds(pl.multiple_of(b * BLOCK, BLOCK), BLOCK)
        key_rows = pl.ds(pl.multiple_of(b * BLOCK + M, BLOCK), BLOCK)
        unit, scale = norm_stats(x_ref[rows, :].astype(f32))
        d_rows = key_back(key_rows) + dot_nt(q_s[rows, :], wq_ref[...])
        grad = norm_back(unit, scale, d_rows * gain1) + dres[rows, :]
        second_s[rows, :] = grad.astype(bf16)
        return sums[0] + col_sum8(d_rows * unit), sums[1] + col_sum8(d_rows)

    layer_copies[0].wait()
    for copy in layer_copies[1:]:
        if talk:
            copy.wait_send()
        else:
            copy.wait()
    sums = (zero8, zero8)
    for i in range(nslot):
        sums = slot_back(other * nslot + i, sums)
        ingrad_copies[1 + i].start()
        ticks("tail", i)
    for i in range(MB):
        sums = mem_back(i, sums)
        ticks("tail", nslot + i)
    for i in range(nslot):
        sums = slot_back(blk * nslot + i, sums)
        ticks("tail", nslot + MB + i)
    ingrad_copies[0].start()
    gain1_sum, shift1_sum = sums
    sm_own[0] = jnp.zeros_like(sm_own[0])
    for k, part in enumerate((gain1_sum, shift1_sum, gain2_sum, shift2_sum)):
        sm_own[0, k : k + 1, :] = jnp.sum(part, axis=0, keepdims=True)
    total = jnp.broadcast_to(jnp.sum(slope_sums, axis=1, keepdims=True), (8, 128))
    sm_own[0, 4:5, 0:128] = jnp.sum(
        jnp.where(lax.broadcasted_iota(jnp.int32, (8, 128), 0)
                  == lax.broadcasted_iota(jnp.int32, (8, 128), 1), total, 0.0),
        axis=0, keepdims=True)

    if talk:
        k = 0
        for level, devices in enumerate(
            ([sibling], [d for d, _ in z_peers], [d for d, _ in xy_peers])
        ):
            hops = []
            for device in devices:
                hops.append(
                    remote(sm_own.at[level], sm_in.at[k], sm_send.at[k], sm_recv.at[k], device)
                )
                k += 1
            for hop in hops:
                hop.start()
            ticks("small", level)
            total = sm_own[level]
            for i, hop in enumerate(hops):
                hop.wait()
                total = total + sm_in[k - len(hops) + i]
            sm_own[level + 1] = total
        small_ref[...] = sm_own[3]
    else:
        for level in range(3):
            ticks("small", level)
        small_ref[...] = sm_own[0]
    for i in range(10):
        ticks("last", i)
    ingrad_copies[0].wait()
    if not talk:
        for u in range(len(units)):
            unit_out(u).start()
            unit_out(u).wait()
    if talk:
        for copy in exchange:
            copy.wait_send()
        for copy in layer_copies[1:]:
            copy.wait_recv()
    for copy in ingrad_copies[1:]:
        copy.wait()


SPLIT = (2, 2, 2, 2)
ORDERS = ('axyb', 'yzx', 'yxz', 'yzx', 'xyab', 'yzx', 'ayxb', 'ayxb', 'xyab', 'yxab', 'zp', 'pz', 'zp')
SCHEDULE = {
    ('chunk', 0): ((0, 0), (1, 0)),
    ('chunk', 1): ((0, 1), (3, 0), (2, 0)),
    ('feed', 9): ((1, 1),),
    ('chunk', 2): ((5, 0), (3, 1), (4, 0)),
    ('feed', 13): ((0, 2), (2, 1)),
    ('feed', 15): ((1, 2),),
    ('chunk', 3): ((6, 0), (5, 1), (7, 0)),
    ('post', 0): ((4, 1),),
    ('post', 1): ((0, 3), (3, 2)),
    ('go', 0): ((6, 1), (8, 0)),
    ('bwd', 0): ((1, 3), (7, 1), (2, 2)),
    ('bwd', 1): ((4, 2),),
    ('bwd', 2): ((0, 4), (5, 2), (3, 3), (8, 1)),
    ('bwd', 3): ((1, 4), (6, 2)),
    ('pair', 0): ((9, 0), (3, 4), (4, 3), (2, 3)),
    ('bwd', 4): ((-1, 0), (0, 5), (7, 2)),
    ('bwd', 5): ((1, 5), (6, 3), (8, 2)),
    ('bwd', 6): ((-1, 1), (9, 1), (5, 3), (3, 5), (4, 4)),
    ('bwd', 7): ((0, 6), (7, 3), (2, 4)),
    ('pair', 1): ((-1, 2), (6, 4), (8, 3), (10, 0)),
    ('bwd', 8): ((9, 2),),
    ('bwd', 9): ((-1, 3), (0, 7), (1, 6)),
    ('bwd', 10): ((5, 4), (3, 6), (7, 4), (10, 1)),
    ('bwd', 11): ((4, 5), (8, 4)),
    ('pair', 2): ((6, 5), (9, 3), (11, 0), (2, 5)),
    ('bwd', 12): ((1, 7), (7, 5)),
    ('bwd', 14): ((0, 8), (3, 7), (11, 1)),
    ('bwd', 15): ((1, 8), (9, 4), (5, 5), (4, 6), (10, 2)),
    ('pair', 3): ((6, 6), (12, 0), (3, 8), (7, 6), (8, 5), (2, 6)),
    ('tail', 1): ((0, 9), (6, 7), (9, 5), (12, 1), (11, 2), (10, 3)),
    ('tail', 2): ((5, 6), (4, 7), (7, 7)),
    ('tail', 3): ((0, 10), (8, 6), (2, 7)),
    ('tail', 4): ((6, 8), (9, 6)),
    ('tail', 5): ((2, 8),),
    ('small', 0): ((5, 7), (12, 2), (4, 8), (8, 7), (11, 3)),
    ('small', 1): ((6, 9), (9, 7), (7, 8)),
    ('small', 2): ((5, 8), (12, 3), (8, 8), (11, 4), (10, 4)),
    ('last', 0): ((6, 10), (9, 8), (12, 4), (4, 9), (7, 9), (8, 9), (11, 5), (10, 5)),
    ('last', 1): ((9, 9), (12, 5), (4, 10), (7, 10), (8, 10), (11, 6), (10, 6)),
    ('last', 2): ((9, 10), (12, 6)),
}


def layer_call(counts, lengths, tokens, memory, ends, grad, params, talk=True):
    _, SH, D = tokens.shape
    MH = memory.shape[1]
    S, M = 2 * SH, 2 * MH
    R = M + S
    gain1, shift1, wq, wk, wv, wo, slopes, gain2, shift2, w1, w2 = params
    FF = w1.shape[1]
    H = slopes.shape[0]
    vmem = pl.BlockSpec(memory_space=pltpu.VMEM)
    smem = pl.BlockSpec(memory_space=pltpu.SMEM)
    hbm = pl.BlockSpec(memory_space=pl.ANY)
    V = pltpu.VMEM
    G = 2 * FF + 4 * D
    units = len(ORDERS)
    dma = pltpu.SemaphoreType.DMA
    scratch = [
        V((S, D), bf16),
        V((M, D), bf16),
        V((S, D), bf16),
        V((2, 1, MH + SH), jnp.int32),
        V((D, D), bf16),
        V((D, D), bf16),
        V((D, D), bf16),
        V((D, D), bf16),
        V((D, FF), bf16),
        V((FF, D), bf16),
        V((D, R), bf16),
        V((R, D), bf16),
        V((R, D), bf16),
        V((R, 128), bf16),
        V((S, D), bf16),
        V((D, S), bf16),
        V((S, 128), f32),
        V((S, D), bf16),
        V((S, D), bf16),
        V((S, D), bf16),
        V((D, S), bf16),
        V((D, S), bf16),
        V((S, 512), bf16),
        V((S, 512), bf16),
        V((S, D), f32),
        V((S, D), f32),
        V((D, S), bf16),
        V((S, 128), bf16),
        V((D, G), bf16),
        V((D // 2, G), bf16),
        V((D // 2 - 16, G), bf16),
        V((4, 8, D), f32),
        V((7, 8, D), f32),
        dma((16,)),
        dma((12,)),
        dma((12,)),
        dma((units, 14)),
        dma((units, 14)),
        dma((7,)),
        dma((7,)),
        dma((units,)),
    ]
    for b in range(S // BLOCK):
        scratch.append(V((H, BLOCK, M + (b + 1) * BLOCK), bf16))
    shapes = (
        jax.ShapeDtypeStruct((2, SH, D), bf16),
        jax.ShapeDtypeStruct((2, SH, D), bf16),
        jax.ShapeDtypeStruct((D, G), bf16),
        jax.ShapeDtypeStruct((8, D), f32),
    )
    extra = {"collective_id": 1, "has_side_effects": True} if talk else {}
    return pl.pallas_call(
        functools.partial(layer_kernel, talk),
        out_shape=shapes,
        in_specs=[smem] * 3 + [hbm] * 4 + [vmem] * 4 + [hbm] * 6,
        out_specs=[hbm, hbm, hbm, vmem],
        scratch_shapes=scratch,
        compiler_params=pltpu.CompilerParams(
            vmem_limit_bytes=64 * 1024 * 1024 - 65536, **extra
        ),
        name="layer",
    )(
        counts, lengths, slopes, tokens, memory, ends, grad,
        gain1.reshape(1, D), shift1.reshape(1, D), gain2.reshape(1, D), shift2.reshape(1, D),
        wq, wk, wv, wo, w1, w2,
    )


def layer_norm(values, gain, shift):
    centred = values - jnp.mean(values, axis=-1, keepdims=True)
    spread = jnp.mean(centred * centred, axis=-1, keepdims=True)
    return centred * lax.rsqrt(spread + epsilon) * gain + shift


def block_scores(
    q_heads, key_block, q_ends, key_order, key_ends, q_index, head_slopes, score_scale
):
    scores = (
        jnp.einsum("qhd,khd->hqk", q_heads, key_block, preferred_element_type=jnp.float32)
        * score_scale
    )
    distance = (q_ends[:, None] - key_ends[None, :]).astype(jnp.float32)
    scores = scores - head_slopes[:, None, None] * distance[None]
    allowed = key_order[None, :] <= q_index[:, None]
    return (jnp.where(allowed[None], scores, -1e30), distance)


def spread_device(
    tokens,
    memory,
    segment_ends,
    memory_ends,
    segment_counts,
    memory_lengths,
    first_gain,
    first_shift,
    query_weight,
    key_weight,
    value_weight,
    out_weight,
    head_slopes,
    second_gain,
    second_shift,
    hidden_weight,
    output_weight,
    output_grad,
):
    seq_count, slot_count, model_width = tokens.shape
    mem_count = memory.shape[1]
    head_count = head_slopes.shape[0]
    head_dim = model_width // head_count
    score_scale = 1.0 / math.sqrt(head_dim)
    key_rows = mem_count + slot_count
    blocks = lax.axis_size("blk")
    my_block = lax.axis_index("blk")
    x_float = tokens.astype(jnp.float32)
    mem_float = memory.astype(jnp.float32)
    normed = layer_norm(x_float, first_gain, first_shift).astype(jnp.bfloat16)
    mem_normed = layer_norm(mem_float, first_gain, first_shift).astype(jnp.bfloat16)
    key_input = jnp.concatenate([mem_normed, normed], axis=1)
    query = jnp.einsum(
        "std,de->ste", normed, query_weight, preferred_element_type=jnp.float32
    ).astype(jnp.bfloat16)
    pair_weight = jnp.concatenate([key_weight, value_weight], axis=1)
    key_value = jnp.einsum(
        "srd,de->rse", key_input, pair_weight, preferred_element_type=jnp.float32
    ).astype(jnp.bfloat16)
    mem_index = my_block * mem_count + jnp.arange(mem_count, dtype=jnp.int32)
    slot_index = my_block * slot_count + jnp.arange(slot_count, dtype=jnp.int32)
    mem_order = jnp.where(
        mem_index[None, :] >= mem_count * blocks - memory_lengths[:, None], -1, far_order
    )
    slot_order = jnp.where(
        slot_index[None, :] < segment_counts[:, None], slot_index[None, :], far_order
    )
    key_meta = jnp.stack(
        [
            jnp.concatenate([mem_order, slot_order], axis=1),
            jnp.concatenate([memory_ends, segment_ends], axis=1),
        ]
    )
    all_pairs, all_meta = (
        lax.all_gather(key_value, "blk", axis=0, tiled=True),
        lax.all_gather(key_meta, "blk", axis=2, tiled=True),
    )
    query_heads = query.reshape(seq_count, slot_count, head_count, head_dim)

    def pick(seq_index):
        pair_rows = lax.dynamic_index_in_dim(all_pairs, seq_index, 1, keepdims=False)
        meta_rows = lax.dynamic_index_in_dim(all_meta, seq_index, 1, keepdims=False)
        key_heads = pair_rows[:, :model_width].reshape(-1, key_rows, head_count, head_dim)
        value_heads = pair_rows[:, model_width:].reshape(-1, key_rows, head_count, head_dim)
        return (
            key_heads,
            value_heads,
            meta_rows[0].reshape(-1, key_rows),
            meta_rows[1].reshape(-1, key_rows),
        )

    def attend(seq_index):
        key_heads, value_heads, key_order, key_ends = pick(seq_index)
        q_heads = lax.dynamic_index_in_dim(query_heads, seq_index, 0, keepdims=False)
        q_ends = lax.dynamic_index_in_dim(segment_ends, seq_index, 0, keepdims=False)

        def stats_step(running, pieces):
            scores = block_scores(
                q_heads,
                pieces[0],
                q_ends,
                pieces[1],
                pieces[2],
                slot_index,
                head_slopes,
                score_scale,
            )[0]
            running_max = jnp.maximum(running[0], jnp.max(scores, axis=-1))
            running_sum = running[1] * jnp.exp(running[0] - running_max) + jnp.sum(
                jnp.exp(scores - running_max[..., None]), axis=-1
            )
            return ((running_max, running_sum), None)

        start_max = jnp.full((head_count, slot_count), -jnp.inf, jnp.float32)
        (top_max, top_sum), _ = lax.scan(
            stats_step, (start_max, jnp.zeros_like(start_max)), (key_heads, key_order, key_ends)
        )
        log_total = top_max + jnp.log(top_sum)

        def out_step(summed, pieces):
            scores = block_scores(
                q_heads,
                pieces[0],
                q_ends,
                pieces[1],
                pieces[2],
                slot_index,
                head_slopes,
                score_scale,
            )[0]
            attn_probs = jnp.exp(scores - log_total[..., None]).astype(jnp.bfloat16)
            return (
                summed
                + jnp.einsum(
                    "hqk,khd->qhd", attn_probs, pieces[3], preferred_element_type=jnp.float32
                ),
                None,
            )

        start_out = jnp.zeros((slot_count, head_count, head_dim), jnp.float32)
        mixed_heads, _ = lax.scan(
            out_step, start_out, (key_heads, key_order, key_ends, value_heads)
        )
        return (mixed_heads, log_total)

    mixed_all, log_totals = lax.map(attend, jnp.arange(seq_count))
    mixed_low = mixed_all.reshape(seq_count, slot_count, model_width).astype(jnp.bfloat16)
    residual = x_float + jnp.einsum(
        "std,de->ste", mixed_low, out_weight, preferred_element_type=jnp.float32
    )
    second_low = layer_norm(residual, second_gain, second_shift).astype(jnp.bfloat16)
    hidden_pre = jnp.einsum(
        "std,df->stf", second_low, hidden_weight, preferred_element_type=jnp.float32
    )
    act_low = jax.nn.gelu(hidden_pre, approximate=False).astype(jnp.bfloat16)
    layer_out = (
        residual
        + jnp.einsum("stf,fd->std", act_low, output_weight, preferred_element_type=jnp.float32)
    ).astype(jnp.bfloat16)
    grad_output_w = jnp.einsum(
        "stf,std->fd", act_low, output_grad, preferred_element_type=jnp.float32
    )
    d_act = jnp.einsum(
        "std,fd->stf", output_grad, output_weight, preferred_element_type=jnp.float32
    )
    _, gelu_pull = jax.vjp(lambda inner: jax.nn.gelu(inner, approximate=False), hidden_pre)
    d_pre_low = gelu_pull(d_act)[0].astype(jnp.bfloat16)
    grad_hidden_w = jnp.einsum(
        "std,stf->df", second_low, d_pre_low, preferred_element_type=jnp.float32
    )
    d_second = jnp.einsum(
        "stf,df->std", d_pre_low, hidden_weight, preferred_element_type=jnp.float32
    )
    _, second_pull = jax.vjp(layer_norm, residual, second_gain, second_shift)
    d_resid_norm, grad_second_g, grad_second_b = second_pull(d_second)
    d_residual = d_resid_norm + output_grad.astype(jnp.float32)
    d_branch = d_residual.astype(jnp.bfloat16)
    grad_out_w = jnp.einsum("std,ste->de", mixed_low, d_branch, preferred_element_type=jnp.float32)
    d_mixed = jnp.einsum(
        "ste,de->std", d_branch, out_weight, preferred_element_type=jnp.float32
    ).astype(jnp.bfloat16)
    d_mixed_heads = d_mixed.reshape(seq_count, slot_count, head_count, head_dim)

    def query_side(seq_index):
        key_heads, value_heads, key_order, key_ends = pick(seq_index)
        q_heads = lax.dynamic_index_in_dim(query_heads, seq_index, 0, keepdims=False)
        q_ends = lax.dynamic_index_in_dim(segment_ends, seq_index, 0, keepdims=False)
        d_heads = lax.dynamic_index_in_dim(d_mixed_heads, seq_index, 0, keepdims=False)
        log_total = lax.dynamic_index_in_dim(log_totals, seq_index, 0, keepdims=False)

        def probs_of(key_block, order_block, ends_block, value_block):
            scores, distance = block_scores(
                q_heads,
                key_block,
                q_ends,
                order_block,
                ends_block,
                slot_index,
                head_slopes,
                score_scale,
            )
            attn_probs = jnp.exp(scores - log_total[..., None])
            d_probs = jnp.einsum(
                "qhd,khd->hqk", d_heads, value_block, preferred_element_type=jnp.float32
            )
            return (attn_probs, d_probs, distance)

        def delta_step(summed, pieces):
            attn_probs, d_probs, _ = probs_of(pieces[0], pieces[1], pieces[2], pieces[3])
            return (summed + jnp.sum(attn_probs * d_probs, axis=-1), None)

        delta_rows, _ = lax.scan(
            delta_step,
            jnp.zeros((head_count, slot_count), jnp.float32),
            (key_heads, key_order, key_ends, value_heads),
        )

        def grad_step(running, pieces):
            attn_probs, d_probs, distance = probs_of(pieces[0], pieces[1], pieces[2], pieces[3])
            d_scores = (attn_probs * (d_probs - delta_rows[..., None])).astype(jnp.bfloat16)
            d_query = running[0] + jnp.einsum(
                "hqk,khd->qhd", d_scores, pieces[0], preferred_element_type=jnp.float32
            )
            d_slopes = running[1] - jnp.sum(
                d_scores.astype(jnp.float32) * distance[None], axis=(1, 2)
            )
            return ((d_query, d_slopes), None)

        start_grads = (
            jnp.zeros((slot_count, head_count, head_dim), jnp.float32),
            jnp.zeros((head_count,), jnp.float32),
        )
        (d_query, d_slopes), _ = lax.scan(
            grad_step, start_grads, (key_heads, key_order, key_ends, value_heads)
        )
        return (d_query * score_scale, delta_rows, d_slopes)

    d_query_all, delta_all, slope_parts = lax.map(query_side, jnp.arange(seq_count))
    grad_slopes = jnp.sum(slope_parts, axis=0)
    d_query_low = d_query_all.reshape(seq_count, slot_count, model_width).astype(jnp.bfloat16)

    def pair_terms(
        pair_rows, order_block, ends_block, q_heads, q_ends, q_index, d_heads, log_total, delta_rows
    ):
        key_block = pair_rows[:, :model_width].reshape(key_rows, head_count, head_dim)
        value_block = pair_rows[:, model_width:].reshape(key_rows, head_count, head_dim)
        scores, _ = block_scores(
            q_heads, key_block, q_ends, order_block, ends_block, q_index, head_slopes, score_scale
        )
        attn_probs = jnp.exp(scores - log_total[..., None])
        d_probs = jnp.einsum(
            "qhd,khd->hqk", d_heads, value_block, preferred_element_type=jnp.float32
        )
        d_scores = (attn_probs * (d_probs - delta_rows[..., None])).astype(jnp.bfloat16)
        d_value = jnp.einsum(
            "hqk,qhd->khd",
            attn_probs.astype(jnp.bfloat16),
            d_heads,
            preferred_element_type=jnp.float32,
        )
        d_key = (
            jnp.einsum("hqk,qhd->khd", d_scores, q_heads, preferred_element_type=jnp.float32)
            * score_scale
        )
        return jnp.concatenate(
            [d_key.reshape(key_rows, model_width), d_value.reshape(key_rows, model_width)], axis=1
        )

    def one_block(block_index):
        offset = block_index * key_rows
        pair_block = lax.dynamic_slice_in_dim(all_pairs, offset, key_rows, 0)
        meta_block = lax.dynamic_slice_in_dim(all_meta, offset, key_rows, 2)
        return jax.vmap(pair_terms, in_axes=(1, 0, 0, 0, 0, None, 0, 0, 0), out_axes=1)(
            pair_block,
            meta_block[0],
            meta_block[1],
            query_heads,
            segment_ends,
            slot_index,
            d_mixed_heads,
            log_totals,
            delta_all,
        )

    pieces = lax.map(one_block, jnp.arange(lax.axis_size("blk") * key_rows // key_rows))
    pair_grads = lax.psum_scatter(
        pieces.reshape(lax.axis_size("blk") * key_rows, seq_count, 2 * model_width).astype(
            jnp.bfloat16
        ),
        "blk",
        scatter_dimension=0,
        tiled=True,
    )
    grad_pair_w = jnp.einsum(
        "srd,rse->de", key_input, pair_grads, preferred_element_type=jnp.float32
    )
    grad_key_w = grad_pair_w[:, :model_width]
    grad_value_w = grad_pair_w[:, model_width:]
    d_key_input = jnp.einsum(
        "rse,de->srd", pair_grads, pair_weight, preferred_element_type=jnp.float32
    )
    grad_query_w = jnp.einsum(
        "std,ste->de", normed, d_query_low, preferred_element_type=jnp.float32
    )
    d_normed = (
        jnp.einsum("ste,de->std", d_query_low, query_weight, preferred_element_type=jnp.float32)
        + d_key_input[:, mem_count:]
    )
    _, first_pull = jax.vjp(layer_norm, x_float, first_gain, first_shift)
    d_tokens, gain_slots, shift_slots = first_pull(d_normed)
    _, mem_pull = jax.vjp(
        lambda gain, shift: layer_norm(mem_float, gain, shift), first_gain, first_shift
    )
    gain_mem, shift_mem = mem_pull(d_key_input[:, :mem_count])
    input_grad = (d_tokens + d_residual).astype(jnp.bfloat16)
    grad_first_g = gain_slots + gain_mem
    grad_first_b = shift_slots + shift_mem
    summed = lax.psum(
        (
            grad_first_g,
            grad_first_b,
            grad_query_w,
            grad_key_w,
            grad_value_w,
            grad_out_w,
            grad_slopes,
            grad_second_g,
            grad_second_b,
            grad_hidden_w,
            grad_output_w,
        ),
        ("seq", "blk"),
    )
    return (
        layer_out,
        input_grad,
        summed[0],
        summed[1],
        summed[2],
        summed[3],
        summed[4],
        summed[5],
        summed[6],
        summed[7],
        summed[8],
        summed[9],
        summed[10],
    )


def widen_kernel(ga, gb, gc, layer_in, grad_in, small, *outs):
    gw1, gw2, go, gq, gk, gv, layer, grad, gain1, shift1, slopes, gain2, shift2 = outs
    half = ga.shape[1] // 2
    gw1[...] = ga[:, :half].astype(f32)
    gw2[...] = ga[:, half:].astype(f32).T
    go[...] = gb[...].astype(f32)
    for i, out in enumerate((gq, gk, gv)):
        out[...] = gc[:, i * 128 : (i + 1) * 128].astype(f32)
    layer[...] = layer_in[...]
    grad[...] = grad_in[...]

    @pl.when((pl.program_id(0) == 0) & (pl.program_id(1) == 0))
    def _():
        for i, out in enumerate((gain1, shift1, gain2, shift2)):
            out[...] = small[i : i + 1, :]
        slopes[...] = small[4:5, 0:8]


def widen(grads, layer, in_grad, small, D, FF):
    RB = D
    LB = layer.shape[0] // 4
    out = [
        ((D, FF), (RB, 512), lambda c, r: (r, c)),
        ((FF, D), (512, RB), lambda c, r: (c, r)),
        ((D, D), (RB, 128), lambda c, r: (r, c)),
        ((D, D), (RB, 128), lambda c, r: (r, c)),
        ((D, D), (RB, 128), lambda c, r: (r, c)),
        ((D, D), (RB, 128), lambda c, r: (r, c)),
        ((4 * LB, D), (LB, D), lambda c, r: (c, 0)),
        ((4 * LB, D), (LB, D), lambda c, r: (c, 0)),
    ]
    kinds = [f32] * 6 + [bf16] * 2
    shapes = [jax.ShapeDtypeStruct(shape, kind) for (shape, _, _), kind in zip(out, kinds)]
    specs = [pl.BlockSpec(block, index) for _, block, index in out]
    for width in (D, D, 8, D, D):
        shapes.append(jax.ShapeDtypeStruct((1, width), f32))
        specs.append(pl.BlockSpec((1, width), lambda c, r: (0, 0)))
    go_at = 2 * FF // 128
    head_at = (2 * FF + D) // 384
    return pl.pallas_call(
        widen_kernel,
        grid=(4, 1),
        out_shape=shapes,
        in_specs=[
            pl.BlockSpec((RB, 1024), lambda c, r: (r, c)),
            pl.BlockSpec((RB, 128), lambda c, r: (r, go_at + c)),
            pl.BlockSpec((RB, 384), lambda c, r: (r, head_at + c)),
            pl.BlockSpec((LB, D), lambda c, r: (c, 0)),
            pl.BlockSpec((LB, D), lambda c, r: (c, 0)),
            pl.BlockSpec((8, D), lambda c, r: (0, 0)),
        ],
        out_specs=specs,
        compiler_params=pltpu.CompilerParams(vmem_limit_bytes=62 * 1024 * 1024),
        name="widen",
    )(grads, grads, grads, layer, in_grad, small)


def whole_device(*args):
    tokens, memory, segment_ends, memory_ends, counts, lengths = args[:6]
    params = args[6:17]
    output_grad = args[17]
    D = tokens.shape[2]
    FF = params[9].shape[1]
    H = params[6].shape[0]
    ends = jnp.concatenate([memory_ends, segment_ends], axis=1)[:, None]
    layer, in_grad, grads, small = layer_call(
        counts, lengths, tokens, memory, ends, output_grad, params
    )
    gw1, gw2, go, gq, gk, gv, layer, in_grad, *rows = widen(
        grads, layer.reshape(-1, D), in_grad.reshape(-1, D), small, D, FF
    )
    gain1, shift1, slopes, gain2, shift2 = (row[0] for row in rows)
    return (
        layer.reshape(tokens.shape),
        in_grad.reshape(tokens.shape),
        gain1,
        shift1,
        gq,
        gk,
        gv,
        go,
        slopes,
        gain2,
        shift2,
        gw1,
        gw2,
    )


def per_device(*args):
    whole = args[0].shape[0] == lax.axis_size("blk") == 2 and lax.axis_size("seq") == 16
    if whole:
        return whole_device(*args)
    return spread_device(*args)


def solution(mesh):
    placed = (
        P("seq", "blk", None),
        P("seq", "blk", None),
        P("seq", "blk"),
        P("seq", "blk"),
        P("seq"),
        P("seq"),
        P(),
        P(),
        P(),
        P(),
        P(),
        P(),
        P(),
        P(),
        P(),
        P(),
        P(),
        P("seq", "blk", None),
    )
    return jax.shard_map(
        per_device,
        mesh=mesh,
        in_specs=placed,
        out_specs=(
            P("seq", "blk", None),
            P("seq", "blk", None),
            P(),
            P(),
            P(),
            P(),
            P(),
            P(),
            P(),
            P(),
            P(),
            P(),
            P(),
        ),
        check_vma=False,
    )
```
